32 devices in a mesh: seq: 4 (over y, x), batch: 8 (over z, core).
Axes of the slice: x: 2, y: 2, z: 4, core: 2. Of those that a mesh axis runs over, the one named last changes fastest.
Arguments:
- layer_input: bfloat16 [8, 2048, 768], P('batch', 'seq'), may hold values from -6 to 6
- w_query: bfloat16 [768, 768], replicated, may hold values from -0.3125 to 0.3125
- b_query: bfloat16 [768], replicated, may hold values from -3 to 3
- w_key: bfloat16 [768, 768], replicated, may hold values from -0.3125 to 0.3125
- b_key: bfloat16 [768], replicated, may hold values from -3 to 3
- w_value: bfloat16 [768, 768], replicated, may hold values from -0.21875 to 0.21875
- b_value: bfloat16 [768], replicated, may hold values from -3 to 3
- w_out: bfloat16 [768, 768], replicated, may hold values from -1.75 to 1.75
- b_out: bfloat16 [768], replicated, may hold values from -3 to 3
- gain_attn: bfloat16 [768], replicated, may hold values from 0.5 to 1.5
- shift_attn: bfloat16 [768], replicated, may hold values from -1.75 to 1.75
- w_in: bfloat16 [768, 3072], replicated, may hold values from -0.21875 to 0.21875
- b_in: bfloat16 [3072], replicated, may hold values from -3 to 3
- w_down: bfloat16 [3072, 768], replicated, may hold values from -0.109375 to 0.109375
- b_down: bfloat16 [768], replicated, may hold values from -1.75 to 1.75
- gain_ffn: bfloat16 [768], replicated, may hold values from 0.5 to 1.5
- shift_ffn: bfloat16 [768], replicated, may hold values from -1.75 to 1.75
- rel_table: bfloat16 [512, 768], replicated, may hold values from -6 to 6
- segment_ids: int32 [8, 2048], P('batch'), may hold values from 0 to 3, never falling along the last dimension, each value on 1 to 1024 neighbouring positions
- cotangent: bfloat16 [8, 2048, 768], P('batch', 'seq'), may hold values from -8 to 8
Outputs:
- layer_out: bfloat16 [8, 2048, 768], P('batch', 'seq')
- input_grad: float32 [8, 2048, 768], P('batch', 'seq')
- w_query_grad: float32 [768, 768], P('batch')
- b_query_grad: float32 [768], P('batch')
- w_key_grad: float32 [768, 768], P('batch')
- b_key_grad: float32 [768], P('batch')
- w_value_grad: float32 [768, 768], P('batch')
- b_value_grad: float32 [768], P('batch')
- w_out_grad: float32 [768, 768], P('batch')
- b_out_grad: float32 [768], P('batch')
- gain_attn_grad: float32 [768], P('batch')
- shift_attn_grad: float32 [768], P('batch')
- w_in_grad: float32 [768, 3072], P('batch')
- b_in_grad: float32 [3072], P('batch')
- w_down_grad: float32 [3072, 768], P('batch')
- b_down_grad: float32 [768], P('batch')
- gain_ffn_grad: float32 [768], P('batch')
- shift_ffn_grad: float32 [768], P('batch')
- rel_table_grad: float32 [512, 768], P(('seq', 'batch'))
The draws below stay inside these ranges and needn't reach their ends.
Inputs may be any that keep to these rules, and one draw needn't show every extreme that they name: `segment_ids`: within each row the document number never falls; each document has 1 to 1024 positions, and some document has exactly that many.
All inputs are finite; a program needn't handle non-finite values.
Results may differ from the reference program's by a relative error of at most 0.03.
Values may be sent and summed in bfloat16 or wider, within the bound.
A program may use at most 320 MiB of HBM per device.

```python
import math
import jax
import jax.numpy as jnp
import numpy as np
from jax import lax

D = 768
HEADS = 12
HEAD_DIM = 64
FF = 3072
SPAN = 256
LENGTH = 2048
ROWS = 8


def strengthened(drawn, rng, source, target, parts, factor):
    def block_of(axis_at):
        return (jnp.arange(drawn.shape[axis_at]) // (drawn.shape[axis_at] // parts)).reshape((-1,) + (1,) * (drawn.ndim - 1 - axis_at))

    one_side = jax.random.permutation(rng, parts)[block_of(target)]
    other_side = (block_of(target) + parts // 2) % parts
    return jnp.where((block_of(source) == one_side) | (block_of(source) == other_side), factor * drawn, drawn)


def levels(rng, shape, cuts, smallest, largest):
    def one(position, blocks):
        steps = jax.random.uniform(jax.random.fold_in(jax.random.fold_in(rng, 6), position), (blocks,), jnp.float32, smallest / len(cuts), largest / len(cuts))
        return jnp.repeat(jnp.exp(steps), shape[position] // blocks).reshape((-1,) + (1,) * (len(shape) - position - 1))

    gain = one(*cuts[0])
    for cut in cuts[1:]:
        gain = gain * one(*cut)
    return gain


def length_profile(amount, total, limit, lean):
    loads = [(1 << 20) // math.isqrt(standing ** lean) + 1 for standing in range(2, amount + 1)]
    rest, counts = total - limit - (amount - 1), [1] * (amount - 1)
    while rest > 0:
        free = [i for i in range(amount - 1) if counts[i] < limit]
        pool, remaining = sum([loads[i] for i in free]), rest
        for i in free:
            extra = min(limit - counts[i], max(1, remaining * loads[i] // pool), rest)
            counts[i] = counts[i] + extra
            rest = rest - extra
    return np.array([limit] + counts)


def ragged_sizes(rng, amount, total, most, lean):
    if amount == 2:
        one = jax.random.randint(rng, (), max(1, total - most), min(most, total - 1) + 1)
        return jnp.stack([one, total - one])
    lengths = jnp.asarray(length_profile(amount, total, most, lean), jnp.int32)
    twos = (amount - 1) // 2
    donor, receiver = lengths[1:1 + 2 * twos:2], lengths[2:2 + 2 * twos:2]
    room = jnp.minimum(donor - 1, most - receiver)
    passed = jax.random.randint(jax.random.fold_in(rng, 1), (twos,), 0, 1 << 20) % (room + 1)
    lengths = lengths.at[1:1 + 2 * twos:2].set(donor - passed).at[2:2 + 2 * twos:2].set(receiver + passed)
    return lengths[jax.random.permutation(jax.random.fold_in(rng, 2), amount)]


def noise(key, dims, scale, most, shards=(), held_as=jnp.bfloat16):
    values = scale * jax.random.normal(key, dims, jnp.float32)
    if shards:
        values = values * levels(key, dims, shards, -0.22, 0.18)
    return jnp.clip(values, -most, most).astype(held_as)


def noise_with(own_key, dims, deviation, reach, cuts, heavy, kind=jnp.bfloat16):
    drawn = deviation * jax.random.normal(own_key, dims, jnp.float32)
    if cuts:
        drawn = drawn * levels(own_key, dims, cuts, -0.22, 0.18)
    return jnp.clip(strengthened(drawn, jax.random.fold_in(own_key, 3), *heavy), -reach, reach).astype(kind)


def setup_inputs(seed: int = 0) -> dict:
    seeds = jax.random.split(jax.random.key(seed), 21)
    return {
        "layer_input": noise(seeds[0], (ROWS, LENGTH, D), 1.0, 6.0, ((0, 8), (1, 4))),
        "w_query": noise(seeds[1], (D, D), (D // 2) ** -0.5, 0.3125),
        "b_query": noise(seeds[2], (D,), 0.5, 3.0),
        "w_key": noise(seeds[3], (D, D), (D // 2) ** -0.5, 0.3125),
        "b_key": noise(seeds[4], (D,), 0.5, 3.0),
        "w_value": noise(seeds[5], (D, D), D ** -0.5, 0.21875),
        "b_value": noise(seeds[6], (D,), 0.5, 3.0),
        "w_out": noise(seeds[7], (D, D), (D // 64) ** -0.5, 1.75),
        "b_out": noise(seeds[8], (D,), 0.5, 3.0),
        "gain_attn": jnp.clip(1.0 + 0.1 * jax.random.normal(seeds[9], (D,), jnp.float32), 0.5, 1.5).astype(jnp.bfloat16),
        "shift_attn": noise(seeds[10], (D,), 0.3, 1.75),
        "w_in": noise(seeds[11], (D, FF), D ** -0.5, 0.21875),
        "b_in": noise(seeds[12], (FF,), 0.5, 3.0),
        "w_down": noise(seeds[13], (FF, D), FF ** -0.5, 0.109375),
        "b_down": noise(seeds[14], (D,), 0.3, 1.75),
        "gain_ffn": jnp.clip(1.0 + 0.1 * jax.random.normal(seeds[15], (D,), jnp.float32), 0.5, 1.5).astype(jnp.bfloat16),
        "shift_ffn": noise(seeds[16], (D,), 0.3, 1.75),
        "rel_table": noise(seeds[17], (2 * SPAN, D), 1.0, 6.0),
        "segment_ids": jax.vmap(lambda own: jnp.searchsorted(jnp.cumsum(ragged_sizes(own, 4, LENGTH, LENGTH // 2, 0)), jnp.arange(LENGTH), side="right"))(jax.random.split(seeds[18], ROWS)).reshape((ROWS, LENGTH)).astype(jnp.int32),
        "cotangent": noise_with(seeds[19], (ROWS, LENGTH, D), 1.0, 8.0, ((0, 8), (1, 4)), (0, 2, 8, 2.0)),
    }


PRECISE = lax.Precision.HIGHEST
NORM_EPS = 1e-07

@jax.custom_vjp
def low(v):
    return lax.optimization_barrier(v.astype(jnp.bfloat16)).astype(jnp.float32)

@jax.custom_vjp
def low_back(v):
    return v

def low_keep(v):
    return (low(v), None)

def low_pass(kept, grad):
    return (grad,)

def back_keep(v):
    return (v, None)

def back_low(kept, grad):
    return (low(grad),)
low.defvjp(low_keep, low_pass)
low_back.defvjp(back_keep, back_low)

def matmul_hi(left, right):
    return jnp.einsum('...d,de->...e', left, right, precision=PRECISE)

def norm_rows(values):
    centred = values - lax.optimization_barrier(jnp.mean(values, axis=-1, keepdims=True))
    return centred * lax.rsqrt(lax.optimization_barrier(jnp.mean(centred * centred, axis=-1, keepdims=True)) + NORM_EPS)

def attend_row(queries, key_rows, value_rows, key_rel, query_rel, doc_ids):
    key_width = 3 * SPAN
    score_scale = (3.0 * HEAD_DIM) ** (-0.5)
    pad_keys = jnp.pad(key_rows, ((SPAN, SPAN), (0, 0), (0, 0)))
    pad_values = jnp.pad(value_rows, ((SPAN, SPAN), (0, 0), (0, 0)))
    pad_ids = jnp.pad(doc_ids, (SPAN, SPAN), constant_values=-1)
    distance = (jnp.arange(SPAN)[:, None] - jnp.arange(key_width)[None, :] + SPAN).astype(jnp.int32)
    query_index = jnp.broadcast_to(jnp.clip(distance + SPAN, 0, 2 * SPAN - 1)[None], (HEADS, SPAN, key_width)).astype(jnp.int32)
    key_index = jnp.broadcast_to(jnp.clip(SPAN - distance.T, 0, 2 * SPAN - 1)[None], (HEADS, key_width, SPAN)).astype(jnp.int32)

    def one_block(block_index):
        first_row = block_index * SPAN
        query_block = lax.dynamic_slice_in_dim(queries, first_row, SPAN, 0)
        key_window = lax.dynamic_slice_in_dim(pad_keys, first_row, key_width, 0)
        value_window = lax.dynamic_slice_in_dim(pad_values, first_row, key_width, 0)
        query_ids = lax.dynamic_slice_in_dim(doc_ids, first_row, SPAN, 0)
        key_ids = lax.dynamic_slice_in_dim(pad_ids, first_row, key_width, 0)
        allowed = (query_ids[:, None] == key_ids[None, :]) & (jnp.abs(distance) < SPAN)
        direct = jnp.einsum('qhe,whe->hqw', query_block, key_window, precision=PRECISE)
        toward = jnp.einsum('qhe,she->hqs', query_block, key_rel, precision=PRECISE)
        from_key = jnp.einsum('whe,she->hws', key_window, query_rel, precision=PRECISE)
        placed_query = jnp.take_along_axis(toward, query_index, axis=2)
        placed_key = jnp.transpose(jnp.take_along_axis(from_key, key_index, axis=2), (0, 2, 1))
        score_sum = low_back(direct + placed_query + placed_key)
        logits = jnp.where(allowed[None], score_sum * score_scale, -1e+30)
        row_max = lax.optimization_barrier(jnp.max(logits, axis=-1, keepdims=True))
        expos = jnp.exp(logits - row_max)
        attn_probs = expos / lax.optimization_barrier(jnp.sum(expos, axis=-1, keepdims=True))
        context = jnp.einsum('hqw,whe->qhe', low(attn_probs), value_window, precision=PRECISE)
        return low_back(low(context.reshape(SPAN, HEADS * HEAD_DIM)))
    blocks = lax.map(jax.checkpoint(one_block), jnp.arange(LENGTH // SPAN, dtype=jnp.int32))
    return blocks.reshape(LENGTH, HEADS * HEAD_DIM)

def whole_layer(inputs, w_query, b_query, w_key, b_key, w_value, b_value, w_out, b_out, gain_attn, shift_attn, w_in, b_in, w_down, b_down, gain_ffn, shift_ffn, rel_table, segment_ids):
    row_total = inputs.shape[0]
    head_shape = (row_total, LENGTH, HEADS, HEAD_DIM)
    rel_shape = (2 * SPAN, HEADS, HEAD_DIM)
    queries = low_back(low(matmul_hi(inputs, w_query) + b_query))
    key_rows = low_back(low(matmul_hi(inputs, w_key) + b_key))
    value_rows = low_back(low(matmul_hi(inputs, w_value) + b_value))
    key_rel = low_back(low(matmul_hi(rel_table, w_key) + b_key)).reshape(rel_shape)
    query_rel = low_back(low(matmul_hi(rel_table, w_query) + b_query)).reshape(rel_shape)
    context = lax.map(lambda row_items: attend_row(row_items[0], row_items[1], row_items[2], key_rel, query_rel, row_items[3]), (queries.reshape(head_shape), key_rows.reshape(head_shape), value_rows.reshape(head_shape), segment_ids))
    attn = low_back(matmul_hi(context, w_out) + b_out)
    hidden = norm_rows(inputs + attn) * gain_attn + shift_attn
    pre_act = low_back(matmul_hi(low(hidden), w_in) + b_in)
    act_low = low(jax.nn.gelu(pre_act, approximate=False))
    branch = low_back(matmul_hi(act_low, w_down) + b_down)
    return norm_rows(hidden + branch) * gain_ffn + shift_ffn

def reference(layer_input, w_query, b_query, w_key, b_key, w_value, b_value, w_out, b_out, gain_attn, shift_attn, w_in, b_in, w_down, b_down, gain_ffn, shift_ffn, rel_table, segment_ids, cotangent):
    params = tuple((array_in.astype(jnp.float32) for array_in in (layer_input, w_query, b_query, w_key, b_key, w_value, b_value, w_out, b_out, gain_attn, shift_attn, w_in, b_in, w_down, b_down, gain_ffn, shift_ffn, rel_table)))
    output, pullback = jax.vjp(lambda *weights: whole_layer(*weights, segment_ids), *params)
    grads = pullback(cotangent.astype(jnp.float32))
    return (output.astype(jnp.bfloat16), grads[0], grads[1], grads[2], grads[3], grads[4], grads[5], grads[6], grads[7], grads[8], grads[9], grads[10], grads[11], grads[12], grads[13], grads[14], grads[15], grads[16], grads[17])
```

```python
import functools
import math

import jax
import jax.numpy as jnp
from jax import lax
from jax.experimental import pallas as pl
from jax.experimental.pallas import tpu as pltpu
from jax.sharding import PartitionSpec as P

HEADS = 12
F32 = jnp.float32
BF = jnp.bfloat16
NN = (((1,), (0,)), ((), ()))
NT = (((1,), (1,)), ((), ()))
TN = (((0,), (0,)), ((), ()))


def dot(a, b, dims=NN):
    return lax.dot_general(a, b, dims, preferred_element_type=F32)


def head_lanes(x, hh):
    lane = lax.broadcasted_iota(jnp.int32, x.shape, len(x.shape) - 1)
    keep = (lane < 64) if hh == 0 else (lane >= 64)
    return jnp.where(keep, x.astype(F32), 0.0).astype(x.dtype)


def fwd_kernel(tq, span, scale, q_ref, k_ref, v_ref, rk_ref, rq_ref, qid_ref, kid_ref, ctx_ref, p_ref, bias_ref, rqm_ref):
    nq = q_ref.shape[0] // tq
    win = tq + 2 * span
    nw = win // tq
    factor = scale * math.log2(math.e)

    @pl.when(pl.program_id(0) == 0)
    def _():
        dist = (
            lax.broadcasted_iota(jnp.int32, (tq, win), 0)
            - lax.broadcasted_iota(jnp.int32, (tq, win), 1)
            + span
        )
        near = jnp.abs(dist) < span
        for qt in range(nq):
            qid = qid_ref[qt * tq : (qt + 1) * tq, :]
            kid = kid_ref[:, qt * tq : qt * tq + win]
            bias_ref[qt] = jnp.where(near & (qid == kid), 0.0, -1e30)

    for hh in range(2):
        rqm_ref[hh] = head_lanes(rq_ref[...], hh)

    def tile(qt, carry):
        row = pl.multiple_of(qt * tq, tq)
        qb = q_ref[pl.ds(row, tq), :]
        kwin = k_ref[pl.ds(row, win), :]
        vwin = v_ref[pl.ds(row, win), :]
        outs = []
        for hh in range(2):
            qm = head_lanes(qb, hh)
            logits = dot(qm, kwin, NT)
            toward = dot(qm, rk_ref[...], NT)
            logits = logits + pltpu.roll(toward, 1, 1, stride=1, stride_axis=0)
            parts = []
            for wt in range(nw):
                u = dot(
                    kwin[wt * tq : (wt + 1) * tq],
                    rqm_ref[hh, 2 * span - tq * wt : 2 * span - tq * wt + 2 * tq, :],
                    NT,
                )
                u = pltpu.roll(u, tq + 1, 1, stride=1, stride_axis=0)[:, :tq]
                parts.append(u.T)
            logits = (logits + jnp.concatenate(parts, axis=1)) * factor + bias_ref[qt]
            top = jnp.max(logits, axis=-1, keepdims=True)
            expos = jnp.exp2(logits - top)
            total = jnp.sum(expos, axis=-1, keepdims=True)
            probs = (expos * (1.0 / total)).astype(BF)
            p_ref[hh, pl.ds(row, tq), :] = probs
            outs.append(dot(probs, vwin))
        lane = lax.broadcasted_iota(jnp.int32, outs[0].shape, 1)
        ctx_ref[pl.ds(row, tq), :] = jnp.where(lane < 64, outs[0], outs[1]).astype(BF)
        return carry

    lax.fori_loop(0, nq, tile, 0)


def attn_fwd(tq, span, q, k, v, rk, rq, qid, kid):
    block, width = q.shape
    ext = k.shape[0]
    win = tq + 2 * span
    scale = (3.0 * 64) ** -0.5
    rk = jnp.pad(rk, ((0, tq), (0, 0)))
    rq = jnp.pad(rq, ((tq, tq), (0, 0)))
    col = lambda rows: pl.BlockSpec((rows, 128), lambda h: (0, h))
    whole = lambda shape: pl.BlockSpec(shape, lambda h: (0, 0))
    return pl.pallas_call(
        functools.partial(fwd_kernel, tq, span, scale),
        grid=(HEADS // 2,),
        out_shape=(
            jax.ShapeDtypeStruct((block, width), BF),
            jax.ShapeDtypeStruct((HEADS, block, win), BF),
        ),
        in_specs=[col(block), col(ext), col(ext), col(rk.shape[0]), col(rq.shape[0]), whole((block, 1)), whole((1, ext))],
        out_specs=(col(block), pl.BlockSpec((2, block, win), lambda h: (h, 0, 0))),
        scratch_shapes=[
            pltpu.VMEM((block // tq, tq, win), F32),
            pltpu.VMEM((2, rq.shape[0], 128), BF),
        ],
        compiler_params=pltpu.CompilerParams(vmem_limit_bytes=48 << 20),
        cost_estimate=pl.CostEstimate(flops=20_000_000_000, bytes_accessed=10 << 20, transcendentals=HEADS * block * win),
        name="attn_fwd",
    )(q, k, v, rk, rq, qid, kid)


def anti(n):
    r = lax.broadcasted_iota(jnp.int32, (n, n), 0)
    c = lax.broadcasted_iota(jnp.int32, (n, n), 1)
    return jnp.where(r + c == n - 1, 1.0, 0.0).astype(BF)


def bwd_kernel(tq, span, scale, q_ref, k_ref, v_ref, g_ref, rk_ref, rq_ref, p_ref,
               dq_ref, dk_ref, dv_ref, drk_ref, drq_ref,
               km_ref, vm_ref, rkm_ref, rqm_ref, kjt_ref, dk_acc, dvt_acc, drkt_acc, drqt_acc):
    nq = q_ref.shape[0] // tq
    ext = k_ref.shape[0]
    nk = ext // tq
    win = tq + 2 * span
    nw = win // tq
    flip = anti(tq)
    for hh in range(2):
        km_ref[hh] = head_lanes(k_ref[...], hh)
        rkm_ref[hh] = head_lanes(rk_ref[...], hh)
        rqm_ref[hh] = head_lanes(rq_ref[...], hh)
    for kt in range(nk):
        kjt_ref[kt] = dot(k_ref[kt * tq : (kt + 1) * tq, :], flip, TN).astype(BF)
    dk_acc[...] = jnp.zeros_like(dk_acc)
    dvt_acc[...] = jnp.zeros_like(dvt_acc)
    drkt_acc[...] = jnp.zeros_like(drkt_acc)
    drqt_acc[...] = jnp.zeros_like(drqt_acc)

    def tile(qt, carry):
        row = pl.multiple_of(qt * tq, tq)
        qb = q_ref[pl.ds(row, tq), :]
        gb = g_ref[pl.ds(row, tq), :]
        qjt = dot(qb, flip, TN).astype(BF)
        gt = gb.astype(F32).T.astype(BF)
        vwin = v_ref[pl.ds(row, win), :]
        dq_r = jnp.zeros((tq, 128), F32)
        for hh in range(2):
            lo, hi = 64 * hh, 64 * hh + 64
            qm = head_lanes(qb, hh)
            gm = head_lanes(gb, hh)
            probs = p_ref[hh, pl.ds(row, tq), :]
            gp = dot(gm, vwin, NT)
            p32 = probs.astype(F32)
            t = p32 * gp
            rows = jnp.sum(t, axis=-1, keepdims=True)
            ds = ((t - p32 * rows) * scale).astype(BF)
            dvt_acc[lo:hi, pl.ds(row, win)] += dot(gt[lo:hi], probs)
            dsj = dot(flip, ds)
            dt = pltpu.roll(dsj, win - tq, 1, stride=1, stride_axis=0).astype(BF)
            dq_r = dq_r + dot(dsj.astype(BF), km_ref[hh, pl.ds(row, win), :]) + dot(dt, rkm_ref[hh])
            drkt_acc[lo:hi, :] += dot(qjt[lo:hi], dt)
            for wt in range(nw):
                dst = dot(flip, ds[:, wt * tq : (wt + 1) * tq], NT)
                du = pltpu.roll(
                    jnp.concatenate([dst, jnp.zeros_like(dst)], axis=1), 0, 1, stride=1, stride_axis=0
                ).astype(BF)
                s0 = 2 * span - tq * wt
                dk_acc[qt + wt] += dot(dst.astype(BF), qm) + dot(du, rqm_ref[hh, s0 : s0 + 2 * tq, :])
                drqt_acc[lo:hi, s0 : s0 + 2 * tq] += dot(kjt_ref[qt + wt, lo:hi, :], du)
        dq_ref[pl.ds(row, tq), :] = dot(flip, dq_r.astype(BF)).astype(BF)
        return carry

    lax.fori_loop(0, nq, tile, 0)
    for kt in range(nk):
        dk_ref[kt * tq : (kt + 1) * tq, :] = dot(flip, dk_acc[kt].astype(BF)).astype(BF)
        dv_ref[kt * tq : (kt + 1) * tq, :] = dvt_acc[:, kt * tq : (kt + 1) * tq].T.astype(BF)
    for st in range(2 * span // 128):
        drk_ref[st * 128 : (st + 1) * 128, :] = drkt_acc[:, st * 128 : (st + 1) * 128].T.astype(BF)
        drq_ref[st * 128 : (st + 1) * 128, :] = drqt_acc[:, tq + st * 128 : tq + (st + 1) * 128].T.astype(BF)


def attn_bwd(tq, span, q, k, v, g, rk, rq, probs):
    block, width = q.shape
    ext = k.shape[0]
    win = tq + 2 * span
    scale = (3.0 * 64) ** -0.5
    rk = jnp.pad(rk, ((0, tq), (0, 0)))
    rq = jnp.pad(rq, ((tq, tq), (0, 0)))
    col = lambda rows: pl.BlockSpec((rows, 128), lambda h: (0, h))
    return pl.pallas_call(
        functools.partial(bwd_kernel, tq, span, scale),
        grid=(HEADS // 2,),
        out_shape=(
            jax.ShapeDtypeStruct((block, width), BF),
            jax.ShapeDtypeStruct((ext, width), BF),
            jax.ShapeDtypeStruct((ext, width), BF),
            jax.ShapeDtypeStruct((2 * span, width), BF),
            jax.ShapeDtypeStruct((2 * span, width), BF),
        ),
        in_specs=[col(block), col(ext), col(ext), col(block), col(rk.shape[0]), col(rq.shape[0]),
                  pl.BlockSpec((2, block, win), lambda h: (h, 0, 0))],
        out_specs=(col(block), col(ext), col(ext), col(2 * span), col(2 * span)),
        scratch_shapes=[
            pltpu.VMEM((2, ext, 128), BF),
            pltpu.VMEM((2, ext, 128), BF),
            pltpu.VMEM((2, rk.shape[0], 128), BF),
            pltpu.VMEM((2, rq.shape[0], 128), BF),
            pltpu.VMEM((ext // tq, 128, tq), BF),
            pltpu.VMEM((ext // tq, tq, 128), F32),
            pltpu.VMEM((128, ext), F32),
            pltpu.VMEM((128, rk.shape[0]), F32),
            pltpu.VMEM((128, rq.shape[0]), F32),
        ],
        compiler_params=pltpu.CompilerParams(vmem_limit_bytes=48 << 20),
        cost_estimate=pl.CostEstimate(flops=50_000_000_000, bytes_accessed=20 << 20, transcendentals=0),
        name="attn_bwd",
    )(q, k, v, g, rk, rq, probs)


NORM_EPS = 1e-07


def norm_rows(values):
    centred = values - jnp.mean(values, axis=-1, keepdims=True)
    inv_std = lax.rsqrt(jnp.mean(centred * centred, axis=-1, keepdims=True) + NORM_EPS)
    return centred * inv_std, inv_std


def norm_back(grads, normed, inv_std):
    first_mean = jnp.mean(grads, axis=-1, keepdims=True)
    second_mean = jnp.mean(grads * normed, axis=-1, keepdims=True)
    return inv_std * (grads - first_mean - normed * second_mean)


def reduced(grad):
    part = lax.psum_scatter(grad.astype(BF), "batch", scatter_dimension=0, tiled=True)
    return lax.psum(part, "seq").astype(F32)


def local(
    layer_input,
    w_query,
    b_query,
    w_key,
    b_key,
    w_value,
    b_value,
    w_out,
    b_out,
    gain_attn,
    shift_attn,
    w_in,
    b_in,
    w_down,
    b_down,
    gain_ffn,
    shift_ffn,
    rel_table,
    segment_ids,
    cotangent,
):
    rows, block, width = layer_input.shape
    span = rel_table.shape[0] // 2
    tq = span
    x = layer_input[0]
    count = lax.axis_size("seq")
    up = [(i, i + 1) for i in range(count - 1)]
    down = [(i + 1, i) for i in range(count - 1)]
    before = lax.ppermute(x[block - span :], "seq", up)
    after = lax.ppermute(x[:span], "seq", down)
    rel_flip = dot(anti(2 * span), rel_table).astype(BF)

    def project(rows_in, weight, bias):
        return (dot(rows_in, weight) + bias).astype(BF)

    q = project(x, w_query, b_query)
    rk = project(rel_flip, w_key, b_key)
    rq = project(rel_flip, w_query, b_query)
    x_ext = jnp.concatenate([before, x, after], axis=0)
    k = project(x_ext, w_key, b_key)
    v = project(x_ext, w_value, b_value)
    start = lax.axis_index("seq") * block
    padded = jnp.pad(segment_ids[0], (span, span), constant_values=-1)
    kid = lax.dynamic_slice_in_dim(padded, start, block + 2 * span, 0)
    qid = kid[span : span + block]
    context, probs = attn_fwd(tq, span, q, k, v, rk, rq, qid[:, None], kid[None])

    residual_one = x.astype(F32) + dot(context, w_out) + b_out
    normed_one, inv_one = norm_rows(residual_one)
    hidden = normed_one * gain_attn + shift_attn
    hidden_low = hidden.astype(BF)
    pre_act = dot(hidden_low, w_in) + b_in
    phi = 0.5 * (1.0 + lax.erf(pre_act * (0.5**0.5)))
    act_low = (pre_act * phi).astype(BF)
    slope = phi + pre_act * (jnp.exp(-0.5 * pre_act * pre_act) * ((2.0 * math.pi) ** -0.5))
    residual_two = hidden + dot(act_low, w_down) + b_down
    normed_two, inv_two = norm_rows(residual_two)
    output = (normed_two * gain_ffn + shift_ffn).astype(BF)

    grad_out = cotangent[0].astype(F32)
    gain_ffn_grad = jnp.sum(grad_out * normed_two, axis=0)
    shift_ffn_grad = jnp.sum(grad_out, axis=0)
    grad_two = norm_back(grad_out * gain_ffn, normed_two, inv_two)
    grad_branch = grad_two.astype(BF)
    down_grad = dot(act_low, grad_branch, TN)
    down_bias_grad = jnp.sum(grad_branch.astype(F32), axis=0)
    grad_pre = (dot(grad_branch, w_down, NT) * slope).astype(BF)
    in_grad = dot(hidden_low, grad_pre, TN)
    in_bias_grad = jnp.sum(grad_pre.astype(F32), axis=0)
    grad_hidden = grad_two + dot(grad_pre, w_in, NT)
    gain_attn_grad = jnp.sum(grad_hidden * normed_one, axis=0)
    shift_attn_grad = jnp.sum(grad_hidden, axis=0)
    grad_one = norm_back(grad_hidden * gain_attn, normed_one, inv_one)
    grad_attn = grad_one.astype(BF)
    out_grad = dot(context, grad_attn, TN)
    out_bias_grad = jnp.sum(grad_attn.astype(F32), axis=0)
    grad_context = dot(grad_attn, w_out, NT).astype(BF)

    dq, dk, dv, drk, drq = attn_bwd(tq, span, q, k, v, grad_context, rk, rq, probs)

    dx = dot(dk, w_key, NT) + dot(dv, w_value, NT)
    from_after = lax.ppermute(dx[:span].astype(BF), "seq", down)
    from_before = lax.ppermute(dx[span + block :].astype(BF), "seq", up)
    input_grad = grad_one + dx[span : span + block] + dot(dq, w_query, NT)
    edge = jnp.zeros((block - span, width), F32)
    input_grad = (
        input_grad
        + jnp.concatenate([from_before.astype(F32), edge], axis=0)
        + jnp.concatenate([edge, from_after.astype(F32)], axis=0)
    )
    query_grad = dot(x, dq, TN) + dot(rel_flip, drq, TN)
    key_grad = dot(x_ext, dk, TN) + dot(rel_flip, drk, TN)
    value_grad = dot(x_ext, dv, TN)

    def total(*parts):
        return sum(jnp.sum(part.astype(F32), axis=0) for part in parts)

    query_bias_grad = total(dq, drq)
    key_bias_grad = total(dk, drk)
    value_bias_grad = total(dv)
    rel_part = (dot(drk, w_key, NT) + dot(drq, w_query, NT)).astype(BF)
    rel_part = dot(anti(2 * span), rel_part).astype(BF)
    rel_grad = lax.psum_scatter(rel_part, ("seq", "batch"), scatter_dimension=0, tiled=True).astype(F32)
    small = [
        query_bias_grad, key_bias_grad, value_bias_grad, out_bias_grad, gain_attn_grad,
        shift_attn_grad, down_bias_grad, gain_ffn_grad, shift_ffn_grad, in_bias_grad,
    ]
    share = lax.axis_size("batch")
    packed = jnp.concatenate([vec.reshape(share, -1) for vec in small], axis=1)
    packed = reduced(packed)[0]
    cuts = []
    at = 0
    for vec in small:
        size = vec.shape[0] // share
        cuts.append(packed[at : at + size])
        at += size
    (qb, kb, vb, ob, ga, sa, db, gf, sf, ib) = cuts
    return (
        output[None],
        input_grad[None],
        reduced(query_grad),
        qb,
        reduced(key_grad),
        kb,
        reduced(value_grad),
        vb,
        reduced(out_grad),
        ob,
        ga,
        sa,
        reduced(in_grad),
        ib,
        reduced(down_grad),
        db,
        gf,
        sf,
        rel_grad,
    )


def solution(mesh):
    tokens = P("batch", "seq", None)
    in_specs = (tokens,) + (P(),) * 17 + (P("batch", None), tokens)
    matrix, vector = P("batch", None), P("batch")
    out_specs = (
        (tokens, tokens)
        + (matrix, vector) * 4
        + (vector, vector)
        + (matrix, vector) * 2
        + (vector, vector, P(("seq", "batch"), None))
    )
    return jax.shard_map(local, mesh=mesh, in_specs=in_specs, out_specs=out_specs, check_vma=False)
```

```python
import functools
import math

import jax
import jax.numpy as jnp
from jax import lax
from jax.experimental import pallas as pl
from jax.experimental.pallas import tpu as pltpu
from jax.sharding import PartitionSpec as P

HEADS = 12
F32 = jnp.float32
BF = jnp.bfloat16
NN = (((1,), (0,)), ((), ()))
NT = (((1,), (1,)), ((), ()))
TN = (((0,), (0,)), ((), ()))


def dot(a, b, dims=NN):
    return lax.dot_general(a, b, dims, preferred_element_type=F32)


def head_lanes(x, hh):
    lane = lax.broadcasted_iota(jnp.int32, x.shape, len(x.shape) - 1)
    keep = (lane < 64) if hh == 0 else (lane >= 64)
    return jnp.where(keep, x.astype(F32), 0.0).astype(x.dtype)


def fwd_kernel(tq, span, scale, q_ref, k_ref, v_ref, rk_ref, rq_ref, qid_ref, kid_ref, ctx_ref, p_ref, bias_ref, rqm_ref):
    nq = q_ref.shape[0] // tq
    win = tq + 2 * span
    nw = win // tq
    factor = scale * math.log2(math.e)

    @pl.when(pl.program_id(0) == 0)
    def _():
        dist = (
            lax.broadcasted_iota(jnp.int32, (tq, win), 0)
            - lax.broadcasted_iota(jnp.int32, (tq, win), 1)
            + span
        )
        near = jnp.abs(dist) < span
        for qt in range(nq):
            qid = qid_ref[qt * tq : (qt + 1) * tq, :]
            kid = kid_ref[:, qt * tq : qt * tq + win]
            bias_ref[qt] = jnp.where(near & (qid == kid), 0.0, -1e30)

    for hh in range(2):
        rqm_ref[hh] = head_lanes(rq_ref[...], hh)

    def tile(qt, carry):
        row = pl.multiple_of(qt * tq, tq)
        qb = q_ref[pl.ds(row, tq), :]
        kwin = k_ref[pl.ds(row, win), :]
        vwin = v_ref[pl.ds(row, win), :]
        outs = []
        for hh in range(2):
            qm = head_lanes(qb, hh)
            logits = dot(qm, kwin, NT)
            toward = dot(qm, rk_ref[...], NT)
            logits = logits + pltpu.roll(toward, 1, 1, stride=1, stride_axis=0)
            parts = []
            for wt in range(nw):
                u = dot(
                    kwin[wt * tq : (wt + 1) * tq],
                    rqm_ref[hh, 2 * span - tq * wt : 2 * span - tq * wt + 2 * tq, :],
                    NT,
                )
                u = pltpu.roll(u, tq + 1, 1, stride=1, stride_axis=0)[:, :tq]
                parts.append(u.T)
            logits = (logits + jnp.concatenate(parts, axis=1)) * factor + bias_ref[qt]
            top = jnp.max(logits, axis=-1, keepdims=True)
            expos = jnp.exp2(logits - top)
            total = jnp.sum(expos, axis=-1, keepdims=True)
            probs = (expos * (1.0 / total)).astype(BF)
            p_ref[hh, pl.ds(row, tq), :] = probs
            outs.append(dot(probs, vwin))
        lane = lax.broadcasted_iota(jnp.int32, outs[0].shape, 1)
        ctx_ref[pl.ds(row, tq), :] = jnp.where(lane < 64, outs[0], outs[1]).astype(BF)
        return carry

    lax.fori_loop(0, nq, tile, 0)


def attn_fwd(tq, span, q, k, v, rk, rq, qid, kid):
    block, width = q.shape
    ext = k.shape[0]
    win = tq + 2 * span
    scale = (3.0 * 64) ** -0.5
    rk = jnp.pad(rk, ((0, tq), (0, 0)))
    rq = jnp.pad(rq, ((tq, tq), (0, 0)))
    col = lambda rows: pl.BlockSpec((rows, 128), lambda h: (0, h))
    whole = lambda shape: pl.BlockSpec(shape, lambda h: (0, 0))
    return pl.pallas_call(
        functools.partial(fwd_kernel, tq, span, scale),
        grid=(HEADS // 2,),
        out_shape=(
            jax.ShapeDtypeStruct((block, width), BF),
            jax.ShapeDtypeStruct((HEADS, block, win), BF),
        ),
        in_specs=[col(block), col(ext), col(ext), col(rk.shape[0]), col(rq.shape[0]), whole((block, 1)), whole((1, ext))],
        out_specs=(col(block), pl.BlockSpec((2, block, win), lambda h: (h, 0, 0))),
        scratch_shapes=[
            pltpu.VMEM((block // tq, tq, win), F32),
            pltpu.VMEM((2, rq.shape[0], 128), BF),
        ],
        compiler_params=pltpu.CompilerParams(vmem_limit_bytes=48 << 20),
        cost_estimate=pl.CostEstimate(flops=20_000_000_000, bytes_accessed=10 << 20, transcendentals=HEADS * block * win),
        name="attn_fwd",
    )(q, k, v, rk, rq, qid, kid)


def anti(n):
    r = lax.broadcasted_iota(jnp.int32, (n, n), 0)
    c = lax.broadcasted_iota(jnp.int32, (n, n), 1)
    return jnp.where(r + c == n - 1, 1.0, 0.0).astype(BF)


def bwd_kernel(tq, span, scale, q_ref, k_ref, v_ref, g_ref, rk_ref, rq_ref, p_ref,
               dq_ref, dk_ref, dv_ref, drk_ref, drq_ref,
               km_ref, vm_ref, rkm_ref, rqm_ref, kjt_ref, dk_acc, dvt_acc, drkt_acc, drqt_acc):
    nq = q_ref.shape[0] // tq
    ext = k_ref.shape[0]
    nk = ext // tq
    win = tq + 2 * span
    nw = win // tq
    flip = anti(tq)
    for hh in range(2):
        km_ref[hh] = head_lanes(k_ref[...], hh)
        rkm_ref[hh] = head_lanes(rk_ref[...], hh)
        rqm_ref[hh] = head_lanes(rq_ref[...], hh)
    for kt in range(nk):
        kjt_ref[kt] = dot(k_ref[kt * tq : (kt + 1) * tq, :], flip, TN).astype(BF)
    dk_acc[...] = jnp.zeros_like(dk_acc)
    dvt_acc[...] = jnp.zeros_like(dvt_acc)
    drkt_acc[...] = jnp.zeros_like(drkt_acc)
    drqt_acc[...] = jnp.zeros_like(drqt_acc)

    def tile(qt, carry):
        row = pl.multiple_of(qt * tq, tq)
        qb = q_ref[pl.ds(row, tq), :]
        gb = g_ref[pl.ds(row, tq), :]
        qjt = dot(qb, flip, TN).astype(BF)
        gt = gb.astype(F32).T.astype(BF)
        vwin = v_ref[pl.ds(row, win), :]
        dq_r = jnp.zeros((tq, 128), F32)
        for hh in range(2):
            lo, hi = 64 * hh, 64 * hh + 64
            qm = head_lanes(qb, hh)
            gm = head_lanes(gb, hh)
            probs = p_ref[hh, pl.ds(row, tq), :]
            gp = dot(gm, vwin, NT)
            p32 = probs.astype(F32)
            t = p32 * gp
            rows = jnp.sum(t, axis=-1, keepdims=True)
            ds = ((t - p32 * rows) * scale).astype(BF)
            dvt_acc[lo:hi, pl.ds(row, win)] += dot(gt[lo:hi], probs)
            dsj = dot(flip, ds)
            dt = pltpu.roll(dsj, win - tq, 1, stride=1, stride_axis=0).astype(BF)
            dq_r = dq_r + dot(dsj.astype(BF), km_ref[hh, pl.ds(row, win), :]) + dot(dt, rkm_ref[hh])
            drkt_acc[lo:hi, :] += dot(qjt[lo:hi], dt)
            for wt in range(nw):
                dst = dot(flip, ds[:, wt * tq : (wt + 1) * tq], NT)
                du = pltpu.roll(
                    jnp.concatenate([dst, jnp.zeros_like(dst)], axis=1), 0, 1, stride=1, stride_axis=0
                ).astype(BF)
                s0 = 2 * span - tq * wt
                dk_acc[qt + wt] += dot(dst.astype(BF), qm) + dot(du, rqm_ref[hh, s0 : s0 + 2 * tq, :])
                drqt_acc[lo:hi, s0 : s0 + 2 * tq] += dot(kjt_ref[qt + wt, lo:hi, :], du)
        dq_ref[pl.ds(row, tq), :] = dot(flip, dq_r.astype(BF)).astype(BF)
        return carry

    lax.fori_loop(0, nq, tile, 0)
    for kt in range(nk):
        dk_ref[kt * tq : (kt + 1) * tq, :] = dot(flip, dk_acc[kt].astype(BF)).astype(BF)
        dv_ref[kt * tq : (kt + 1) * tq, :] = dvt_acc[:, kt * tq : (kt + 1) * tq].T.astype(BF)
    for st in range(2 * span // 128):
        drk_ref[st * 128 : (st + 1) * 128, :] = drkt_acc[:, st * 128 : (st + 1) * 128].T.astype(BF)
        drq_ref[st * 128 : (st + 1) * 128, :] = drqt_acc[:, tq + st * 128 : tq + (st + 1) * 128].T.astype(BF)


def attn_bwd(tq, span, q, k, v, g, rk, rq, probs):
    block, width = q.shape
    ext = k.shape[0]
    win = tq + 2 * span
    scale = (3.0 * 64) ** -0.5
    rk = jnp.pad(rk, ((0, tq), (0, 0)))
    rq = jnp.pad(rq, ((tq, tq), (0, 0)))
    col = lambda rows: pl.BlockSpec((rows, 128), lambda h: (0, h))
    return pl.pallas_call(
        functools.partial(bwd_kernel, tq, span, scale),
        grid=(HEADS // 2,),
        out_shape=(
            jax.ShapeDtypeStruct((block, width), BF),
            jax.ShapeDtypeStruct((ext, width), BF),
            jax.ShapeDtypeStruct((ext, width), BF),
            jax.ShapeDtypeStruct((2 * span, width), BF),
            jax.ShapeDtypeStruct((2 * span, width), BF),
        ),
        in_specs=[col(block), col(ext), col(ext), col(block), col(rk.shape[0]), col(rq.shape[0]),
                  pl.BlockSpec((2, block, win), lambda h: (h, 0, 0))],
        out_specs=(col(block), col(ext), col(ext), col(2 * span), col(2 * span)),
        scratch_shapes=[
            pltpu.VMEM((2, ext, 128), BF),
            pltpu.VMEM((2, ext, 128), BF),
            pltpu.VMEM((2, rk.shape[0], 128), BF),
            pltpu.VMEM((2, rq.shape[0], 128), BF),
            pltpu.VMEM((ext // tq, 128, tq), BF),
            pltpu.VMEM((ext // tq, tq, 128), F32),
            pltpu.VMEM((128, ext), F32),
            pltpu.VMEM((128, rk.shape[0]), F32),
            pltpu.VMEM((128, rq.shape[0]), F32),
        ],
        compiler_params=pltpu.CompilerParams(vmem_limit_bytes=48 << 20),
        cost_estimate=pl.CostEstimate(flops=50_000_000_000, bytes_accessed=20 << 20, transcendentals=0),
        name="attn_bwd",
    )(q, k, v, g, rk, rq, probs)


MESH = pl.DeviceIdType.MESH


class Reducer:
    def __init__(self, ns, nb, shapes, width):
        self.ns, self.nb, self.nz, self.width = ns, nb, nb // 2, width
        self.bits = ns.bit_length() - 1
        self.moves = []
        self.places = []
        at = 0
        for index, (share, cols) in enumerate(shapes):
            room = -(-share // 16) * 16
            self.places.append((at, room))
            for part in range(cols // width):
                self.moves.append((index, part, at, share))
                at += room
        unit = 16 * 2 * ns
        self.rows = -(-at // unit) * unit
        self.piece = self.rows // (2 * ns)

    def scratch(self):
        nz, rows, width, piece = self.nz, self.rows, self.width, self.piece
        shapes = [pltpu.VMEM((nz, rows, width), BF), pltpu.VMEM((nz, rows, width), BF)]
        for level in range(self.bits):
            shapes.append(pltpu.VMEM((2, nz, rows // 4 >> level, width), BF))
        shapes += [pltpu.VMEM((2, nz - 1, piece, width), BF), pltpu.VMEM((rows, width), BF)]
        moves = len(self.moves)
        dma = pltpu.SemaphoreType.DMA
        shapes += [dma((moves,)), dma((2, moves)), dma((2, 2, self.bits)), dma((2, 2, nz - 1)), dma((2, 2, self.ns - 1))]
        return shapes

    def bind(self, sources, scratch):
        self.sources = sources
        self.mine, self.first = scratch[0], scratch[1]
        self.halves = scratch[2 : 2 + self.bits]
        self.across, self.final = scratch[2 + self.bits : 4 + self.bits]
        self.own_sem, self.core_sem, self.seq_sem, self.z_sem, self.out_sem = scratch[4 + self.bits :]
        self.s = lax.axis_index("seq")
        self.b = lax.axis_index("batch")
        self.z = self.b // 2
        self.c = self.b % 2
        self.base = [0, self.rows // 2]
        self.size = self.rows // 2
        self.started = []

    def toggled(self, value, mask):
        out = value
        for bit in range(mask.bit_length()):
            if mask >> bit & 1:
                out = out + (1 - 2 * ((value // (1 << bit)) % 2)) * (1 << bit)
        return out

    def peers(self):
        yield (self.s, self.toggled(self.b, 1))
        for step in range(1, self.nz):
            yield (self.s, self.toggled(self.z, step) * 2 + self.c)
        for step in range(1, self.ns):
            yield (self.toggled(self.s, step), self.b)

    def greet(self):
        barrier = pltpu.get_barrier_semaphore()
        total = 0
        for s, b in self.peers():
            pl.semaphore_signal(barrier, inc=1, device_id={"seq": s, "batch": b}, device_id_type=MESH)
            total += 1
        pl.semaphore_wait(barrier, total)

    def own_copies(self):
        for n, (index, part, at, share) in enumerate(self.moves):
            columns = pl.ds(part * self.width, self.width)
            yield pltpu.make_async_copy(
                self.sources[index].at[:, self.c, :, columns], self.mine.at[:, pl.ds(at, share), :], self.own_sem.at[n]
            )

    def core_copies(self):
        for n, (index, part, at, share) in enumerate(self.moves):
            columns = pl.ds(part * self.width, self.width)
            yield pltpu.make_async_remote_copy(
                src_ref=self.sources[index].at[:, 1 - self.c, :, columns],
                dst_ref=self.first.at[:, pl.ds(at, share), :],
                send_sem=self.core_sem.at[0, n],
                recv_sem=self.core_sem.at[1, n],
                device_id={"seq": self.s, "batch": self.toggled(self.b, 1)},
                device_id_type=MESH,
            )

    def region(self, level, half):
        base, size = half * (self.rows // 2), self.rows // 2
        sent = base
        for at in range(level):
            bit = self.order(half, at)
            size = size // 2
            mine = (self.s // (1 << bit)) % 2
            sent = base + (1 - mine) * size
            base = base + mine * size
        return base, sent, size

    def order(self, half, level):
        return (level + half) % self.bits

    def rows_of(self, start, size):
        return pl.ds(pl.multiple_of(start, 16), size)

    def seq_copy(self, level, half):
        unused, sent, size = self.region(level + 1, half)
        return pltpu.make_async_remote_copy(
            src_ref=self.mine.at[:, self.rows_of(sent, size), :],
            dst_ref=self.halves[level].at[half],
            send_sem=self.seq_sem.at[0, half, level],
            recv_sem=self.seq_sem.at[1, half, level],
            device_id={"seq": self.toggled(self.s, 1 << self.order(half, level)), "batch": self.b},
            device_id_type=MESH,
        )

    def z_copies(self, half):
        kept, unused, size = self.region(self.bits, half)
        for step in range(1, self.nz):
            other = self.toggled(self.z, step)
            yield pltpu.make_async_remote_copy(
                src_ref=self.mine.at[other, self.rows_of(kept, size), :],
                dst_ref=self.across.at[half, step - 1],
                send_sem=self.z_sem.at[0, half, step - 1],
                recv_sem=self.z_sem.at[1, half, step - 1],
                device_id={"seq": self.s, "batch": other * 2 + self.c},
                device_id_type=MESH,
            )

    def out_copies(self, half):
        kept, unused, size = self.region(self.bits, half)
        for step in range(1, self.ns):
            yield pltpu.make_async_remote_copy(
                src_ref=self.final.at[self.rows_of(kept, size), :],
                dst_ref=self.final.at[self.rows_of(kept, size), :],
                send_sem=self.out_sem.at[0, half, step - 1],
                recv_sem=self.out_sem.at[1, half, step - 1],
                device_id={"seq": self.toggled(self.s, step), "batch": self.b},
                device_id_type=MESH,
            )

    def start_core(self):
        for copy in self.core_copies():
            copy.start()
        for copy in self.own_copies():
            copy.start()

    def add_core(self):
        for copy in self.own_copies():
            copy.wait()
        for copy in self.core_copies():
            copy.wait_recv()
        step = self.rows // 8

        def add(n, carry):
            z, at = n // 8, pl.multiple_of((n % 8) * step, 16)
            rows = pl.ds(at, step)
            self.mine[z, rows, :] = (self.mine[z, rows, :].astype(F32) + self.first[z, rows, :].astype(F32)).astype(BF)
            return carry

        lax.fori_loop(0, self.nz * 8, add, 0)

    def start_seq(self, level):
        for half in range(2):
            self.seq_copy(level, half).start()

    def add_seq(self, level):
        for half in range(2):
            self.seq_copy(level, half).wait_recv()
            kept, unused, size = self.region(level + 1, half)
            rows = self.rows_of(kept, size)

            def add(z, carry):
                got = self.halves[level][half, z].astype(F32)
                self.mine[z, rows, :] = (self.mine[z, rows, :].astype(F32) + got).astype(BF)
                return carry

            lax.fori_loop(0, self.nz, add, 0)

    def start_z(self):
        for half in range(2):
            for copy in self.z_copies(half):
                copy.start()

    def add_z(self):
        for half in range(2):
            for copy in self.z_copies(half):
                copy.wait_recv()
            kept, unused, size = self.region(self.bits, half)
            rows = self.rows_of(kept, size)
            total = self.mine[self.z, rows, :].astype(F32)
            for step in range(1, self.nz):
                total = total + self.across[half, step - 1].astype(F32)
            self.final[rows, :] = total.astype(BF)

    def start_out(self):
        for half in range(2):
            for copy in self.out_copies(half):
                copy.start()

    def finish(self):
        for half in range(2):
            for copy in self.out_copies(half):
                copy.wait()
            for copy in self.z_copies(half):
                copy.wait_send()
            for level in range(self.bits):
                self.seq_copy(level, half).wait_send()
        for copy in self.core_copies():
            copy.wait_send()

    def unpack(self, packed, index, share, cols):
        at, room = self.places[index]
        parts = [packed[at + n * room : at + n * room + share] for n in range(cols // self.width)]
        return parts[0] if len(parts) == 1 else jnp.concatenate(parts, axis=1)


def reduce_kernel(reducer, count, *refs):
    out = refs[count]
    reducer.bind(refs[:count], refs[count + 1 :])
    reducer.greet()
    reducer.start_core()
    reducer.add_core()
    for level in range(reducer.bits):
        reducer.start_seq(level)
        reducer.add_seq(level)
    reducer.start_z()
    reducer.add_z()
    reducer.start_out()
    reducer.finish()
    out[...] = reducer.final[...]


def reduce_all(grads, width):
    ns, nb = lax.axis_size("seq"), lax.axis_size("batch")
    shapes = [(grad.shape[0] // nb, grad.shape[1]) for grad in grads]
    reducer = Reducer(ns, nb, shapes, width)
    packed = pl.pallas_call(
        functools.partial(reduce_kernel, reducer, len(grads)),
        out_shape=jax.ShapeDtypeStruct((reducer.rows, width), BF),
        in_specs=[pl.BlockSpec(memory_space=pl.ANY)] * len(grads),
        out_specs=pl.BlockSpec(memory_space=pltpu.VMEM),
        scratch_shapes=reducer.scratch(),
        compiler_params=pltpu.CompilerParams(collective_id=0, has_side_effects=True, vmem_limit_bytes=56 << 20),
        name="reduce_all",
    )(*[grad.reshape(nb // 2, 2, shape[0], shape[1]) for grad, shape in zip(grads, shapes)])
    return [reducer.unpack(packed, n, *shape) for n, shape in enumerate(shapes)]


NORM_EPS = 1e-07


def norm_rows(values):
    centred = values - jnp.mean(values, axis=-1, keepdims=True)
    inv_std = lax.rsqrt(jnp.mean(centred * centred, axis=-1, keepdims=True) + NORM_EPS)
    return centred * inv_std, inv_std


def norm_back(grads, normed, inv_std):
    first_mean = jnp.mean(grads, axis=-1, keepdims=True)
    second_mean = jnp.mean(grads * normed, axis=-1, keepdims=True)
    return inv_std * (grads - first_mean - normed * second_mean)


def local(
    layer_input,
    w_query,
    b_query,
    w_key,
    b_key,
    w_value,
    b_value,
    w_out,
    b_out,
    gain_attn,
    shift_attn,
    w_in,
    b_in,
    w_down,
    b_down,
    gain_ffn,
    shift_ffn,
    rel_table,
    segment_ids,
    cotangent,
):
    rows, block, width = layer_input.shape
    span = rel_table.shape[0] // 2
    tq = span
    x = layer_input[0]
    count = lax.axis_size("seq")
    up = [(i, i + 1) for i in range(count - 1)]
    down = [(i + 1, i) for i in range(count - 1)]
    before = lax.ppermute(x[block - span :], "seq", up)
    after = lax.ppermute(x[:span], "seq", down)
    rel_flip = dot(anti(2 * span), rel_table).astype(BF)

    def project(rows_in, weight, bias):
        return (dot(rows_in, weight) + bias).astype(BF)

    q = project(x, w_query, b_query)
    rk = project(rel_flip, w_key, b_key)
    rq = project(rel_flip, w_query, b_query)
    x_ext = jnp.concatenate([before, x, after], axis=0)
    k = project(x_ext, w_key, b_key)
    v = project(x_ext, w_value, b_value)
    start = lax.axis_index("seq") * block
    padded = jnp.pad(segment_ids[0], (span, span), constant_values=-1)
    kid = lax.dynamic_slice_in_dim(padded, start, block + 2 * span, 0)
    qid = kid[span : span + block]
    context, probs = attn_fwd(tq, span, q, k, v, rk, rq, qid[:, None], kid[None])

    residual_one = x.astype(F32) + dot(context, w_out) + b_out
    normed_one, inv_one = norm_rows(residual_one)
    hidden = normed_one * gain_attn + shift_attn
    hidden_low = hidden.astype(BF)
    pre_act = dot(hidden_low, w_in) + b_in
    phi = 0.5 * (1.0 + lax.erf(pre_act * (0.5**0.5)))
    act_low = (pre_act * phi).astype(BF)
    slope = phi + pre_act * (jnp.exp(-0.5 * pre_act * pre_act) * ((2.0 * math.pi) ** -0.5))
    residual_two = hidden + dot(act_low, w_down) + b_down
    normed_two, inv_two = norm_rows(residual_two)
    output = (normed_two * gain_ffn + shift_ffn).astype(BF)

    grad_out = cotangent[0].astype(F32)
    gain_ffn_grad = jnp.sum(grad_out * normed_two, axis=0)
    shift_ffn_grad = jnp.sum(grad_out, axis=0)
    grad_two = norm_back(grad_out * gain_ffn, normed_two, inv_two)
    grad_branch = grad_two.astype(BF)
    down_grad = dot(act_low, grad_branch, TN)
    down_bias_grad = jnp.sum(grad_branch.astype(F32), axis=0)
    grad_pre = (dot(grad_branch, w_down, NT) * slope).astype(BF)
    in_grad = dot(hidden_low, grad_pre, TN)
    in_bias_grad = jnp.sum(grad_pre.astype(F32), axis=0)
    grad_hidden = grad_two + dot(grad_pre, w_in, NT)
    gain_attn_grad = jnp.sum(grad_hidden * normed_one, axis=0)
    shift_attn_grad = jnp.sum(grad_hidden, axis=0)
    grad_one = norm_back(grad_hidden * gain_attn, normed_one, inv_one)
    grad_attn = grad_one.astype(BF)
    out_grad = dot(context, grad_attn, TN)
    out_bias_grad = jnp.sum(grad_attn.astype(F32), axis=0)
    grad_context = dot(grad_attn, w_out, NT).astype(BF)

    dq, dk, dv, drk, drq = attn_bwd(tq, span, q, k, v, grad_context, rk, rq, probs)

    dx = dot(dk, w_key, NT) + dot(dv, w_value, NT)
    from_after = lax.ppermute(dx[:span].astype(BF), "seq", down)
    from_before = lax.ppermute(dx[span + block :].astype(BF), "seq", up)
    input_grad = grad_one + dx[span : span + block] + dot(dq, w_query, NT)
    edge = jnp.zeros((block - span, width), F32)
    input_grad = (
        input_grad
        + jnp.concatenate([from_before.astype(F32), edge], axis=0)
        + jnp.concatenate([edge, from_after.astype(F32)], axis=0)
    )
    query_grad = dot(x, dq, TN) + dot(rel_flip, drq, TN)
    key_grad = dot(x_ext, dk, TN) + dot(rel_flip, drk, TN)
    value_grad = dot(x_ext, dv, TN)

    def total(*parts):
        return sum(jnp.sum(part.astype(F32), axis=0) for part in parts)

    query_bias_grad = total(dq, drq)
    key_bias_grad = total(dk, drk)
    value_bias_grad = total(dv)
    rel_part = (dot(drk, w_key, NT) + dot(drq, w_query, NT)).astype(BF)
    share, lanes = lax.axis_size("batch"), lax.axis_size("seq")
    rel_rows = 2 * span // (share * lanes)
    order = jnp.arange(2 * span).reshape(lanes, share, rel_rows).transpose(1, 0, 2).reshape(-1)
    picks = (2 * span - 1 - order)[:, None] == jnp.arange(2 * span)[None]
    rel_part = dot(picks.astype(BF), rel_part).astype(BF)
    small = [
        query_bias_grad, key_bias_grad, value_bias_grad, out_bias_grad, gain_attn_grad,
        shift_attn_grad, down_bias_grad, gain_ffn_grad, shift_ffn_grad, in_bias_grad,
    ]
    packed = jnp.concatenate([vec.reshape(share, -1) for vec in small], axis=1)
    packed = jnp.pad(packed, ((0, 0), (0, 16 * width - packed.shape[1]))).reshape(share * 16, width)
    grads = [in_grad, down_grad, out_grad, query_grad, key_grad, value_grad, rel_part, packed]
    sums = reduce_all([grad.astype(BF) for grad in grads], width)
    (in_sum, down_sum, out_sum, query_sum, key_sum, value_sum, rel_sum, packed) = [part.astype(F32) for part in sums]
    rel_sum = lax.dynamic_slice_in_dim(rel_sum, lax.axis_index("seq") * rel_rows, rel_rows, 0)
    packed = packed.reshape(-1)
    cuts = []
    at = 0
    for vec in small:
        size = vec.shape[0] // share
        cuts.append(packed[at : at + size])
        at += size
    (qb, kb, vb, ob, ga, sa, db, gf, sf, ib) = cuts
    return (
        output[None], input_grad[None], query_sum, qb, key_sum, kb, value_sum, vb, out_sum, ob,
        ga, sa, in_sum, ib, down_sum, db, gf, sf, rel_sum,
    )


def solution(mesh):
    tokens = P("batch", "seq", None)
    in_specs = (tokens,) + (P(),) * 17 + (P("batch", None), tokens)
    matrix, vector = P("batch", None), P("batch")
    out_specs = (
        (tokens, tokens)
        + (matrix, vector) * 4
        + (vector, vector)
        + (matrix, vector) * 2
        + (vector, vector, P(("seq", "batch"), None))
    )
    return jax.shard_map(local, mesh=mesh, in_specs=in_specs, out_specs=out_specs, check_vma=False)
```

```python
import functools
import math

import jax
import jax.numpy as jnp
from jax import lax
from jax.experimental import pallas as pl
from jax.experimental.pallas import tpu as pltpu
from jax.sharding import PartitionSpec as P

HEADS = 12
F32 = jnp.float32
BF = jnp.bfloat16
NN = (((1,), (0,)), ((), ()))
NT = (((1,), (1,)), ((), ()))
TN = (((0,), (0,)), ((), ()))


def dot(a, b, dims=NN):
    return lax.dot_general(a, b, dims, preferred_element_type=F32)


def head_lanes(x, hh):
    lane = lax.broadcasted_iota(jnp.int32, x.shape, len(x.shape) - 1)
    keep = (lane < 64) if hh == 0 else (lane >= 64)
    return jnp.where(keep, x.astype(F32), 0.0).astype(x.dtype)


def both_heads(first, second):
    lane = lax.broadcasted_iota(jnp.int32, first.shape, 1)
    return jnp.where(lane < 64, first, second)


def grid_of(n):
    return lax.broadcasted_iota(jnp.int32, (n, n), 0), lax.broadcasted_iota(jnp.int32, (n, n), 1)


def anti(n):
    row, lane = grid_of(n)
    return jnp.where(row + lane == n - 1, 1.0, 0.0).astype(BF)


def sheared(x, shift):
    return pltpu.roll(x, shift, 1, stride=1, stride_axis=0)


def fwd_kernel(n, scale, q_ref, k_ref, v_ref, rk_ref, rq_ref, qid_ref, kid_ref, ctx_ref, p_ref, bias_ref, mask_ref, rqm_ref):
    nq = q_ref.shape[0] // n
    factor = scale * math.log2(math.e)
    row, lane = grid_of(n)
    right = lane > row

    @pl.when(pl.program_id(0) == 0)
    def _():
        for qt in range(nq):
            qid = qid_ref[qt * n : (qt + 1) * n, :]
            first, middle, third = [kid_ref[:, (qt + m) * n : (qt + m + 1) * n] for m in range(3)]
            side = (right & (qid == first)) | ((lane < row) & (qid == third))
            bias_ref[qt, :, 0:n] = jnp.where(side, 0.0, -1e30)
            bias_ref[qt, :, n:] = jnp.where(qid == middle, 0.0, -1e30)
        mask_ref[0] = jnp.where(right, 1.0, 0.0).astype(BF)
        mask_ref[1] = jnp.where(right, 0.0, 1.0).astype(BF)

    for hh in range(2):
        rqm_ref[hh] = head_lanes(rq_ref[...], hh)

    def tile(qt, carry):
        at = lambda m: pl.ds(pl.multiple_of((qt + m) * n, n), n)
        qb = q_ref[at(0), :]
        outs = []
        for hh in range(2):
            qm = head_lanes(qb, hh)
            low, high = rqm_ref[hh, 0:n], rqm_ref[hh, n:]
            to_low = sheared(dot(qm, rk_ref[0:n], NT), 1)
            to_high = sheared(dot(qm, rk_ref[n:], NT), 1)
            side = jnp.where(right, dot(qm, k_ref[at(0), :], NT) + to_low, dot(qm, k_ref[at(2), :], NT) + to_high)
            middle = dot(qm, k_ref[at(1), :], NT) + jnp.where(right, to_high, to_low)
            upper = row + lane >= n - 1
            key_side = jnp.where(upper, dot(k_ref[at(0), :], high, NT), dot(k_ref[at(2), :], low, NT))
            key_middle = jnp.where(upper, dot(k_ref[at(1), :], low, NT), dot(k_ref[at(1), :], high, NT))
            side = (side + sheared(key_side, 1).T) * factor + bias_ref[qt, :, 0:n]
            middle = (middle + sheared(key_middle, 1).T) * factor + bias_ref[qt, :, n:]
            top = jnp.max(jnp.maximum(side, middle), axis=-1, keepdims=True)
            side, middle = jnp.exp2(side - top), jnp.exp2(middle - top)
            inverse = 1.0 / jnp.sum(side + middle, axis=-1, keepdims=True)
            side, middle = (side * inverse).astype(BF), (middle * inverse).astype(BF)
            p_ref[hh, at(0), 0:n] = side
            p_ref[hh, at(0), n:] = middle
            out = dot(side * mask_ref[0], v_ref[at(0), :]) + dot(middle, v_ref[at(1), :])
            outs.append(out + dot(side * mask_ref[1], v_ref[at(2), :]))
        ctx_ref[at(0), :] = both_heads(*outs).astype(BF)
        return carry

    lax.fori_loop(0, nq, tile, 0)


def attn_fwd(span, q, k, v, rk, rq, qid, kid):
    block, width = q.shape
    ext = k.shape[0]
    scale = (3.0 * 64) ** -0.5
    col = lambda rows: pl.BlockSpec((rows, 128), lambda h: (0, h))
    whole = lambda shape: pl.BlockSpec(shape, lambda h: (0, 0))
    return pl.pallas_call(
        functools.partial(fwd_kernel, span, scale),
        grid=(HEADS // 2,),
        out_shape=(
            jax.ShapeDtypeStruct((block, width), BF),
            jax.ShapeDtypeStruct((HEADS, block, 2 * span), BF),
        ),
        in_specs=[col(block), col(ext), col(ext), col(2 * span), col(2 * span), whole((block, 1)), whole((1, ext))],
        out_specs=(col(block), pl.BlockSpec((2, block, 2 * span), lambda h: (h, 0, 0))),
        scratch_shapes=[
            pltpu.VMEM((block // span, span, 2 * span), F32),
            pltpu.VMEM((2, span, span), BF),
            pltpu.VMEM((2, 2 * span, 128), BF),
        ],
        compiler_params=pltpu.CompilerParams(vmem_limit_bytes=48 << 20),
        cost_estimate=pl.CostEstimate(flops=20_000_000_000, bytes_accessed=10 << 20, transcendentals=HEADS * block * 2 * span),
        name="attn_fwd",
    )(q, k, v, rk, rq, qid, kid)


def bwd_tile(n, scale, qt, q_ref, k_ref, v_ref, g_ref, rk_ref, rq_ref, p_ref, mask_ref, kjt_ref, dk_acc, dvt_acc, drkt_acc, drqt_acc):
    at = lambda m: pl.ds(pl.multiple_of((qt + m) * n, n), n)
    row, lane = grid_of(n)
    flip = anti(n)
    ahead, behind, above, below = [mask_ref[m] for m in range(4)]
    qb, gb = q_ref[at(0), :], g_ref[at(0), :]
    qjt = dot(qb, flip, TN).astype(BF)
    gt = gb.astype(F32).T.astype(BF)
    dqs, dks = [], []
    for hh in range(2):
        lo, hi = 64 * hh, 64 * hh + 64
        gm = head_lanes(gb, hh)
        side, middle = p_ref[hh, at(0), 0:n], p_ref[hh, at(0), n:]
        ps, pm = side.astype(F32) * scale, middle.astype(F32) * scale
        gs = jnp.where(lane > row, dot(gm, v_ref[at(0), :], NT), dot(gm, v_ref[at(2), :], NT))
        gd = dot(gm, v_ref[at(1), :], NT)
        ts, td = ps * gs, pm * gd
        total = jnp.sum(ts + td, axis=-1, keepdims=True) * (1.0 / scale)
        ds, dm = (ts - ps * total).astype(BF), (td - pm * total).astype(BF)
        for m, part in enumerate((side * ahead, middle, side * behind)):
            dvt_acc[lo:hi, at(m)] += dot(gt[lo:hi], part)

        sj, mj = dot(flip, ds), dot(flip, dm)
        right = row + lane >= n
        to_low = sheared(jnp.where(right, sj, mj), 0).astype(BF)
        to_high = sheared(jnp.where(right, mj, sj), 0).astype(BF)
        sj, mj = sj.astype(BF), mj.astype(BF)
        dq = dot(sj * above, k_ref[at(0), :]) + dot(mj, k_ref[at(1), :]) + dot(sj * below, k_ref[at(2), :])
        dqs.append(dq + dot(to_low, rk_ref[0:n]) + dot(to_high, rk_ref[n:]))
        drkt_acc[lo:hi, 0:n] += dot(qjt[lo:hi], to_low)
        drkt_acc[lo:hi, n:] += dot(qjt[lo:hi], to_high)

        st, mt = dot(flip, ds, NT), dot(flip, dm, NT)
        us, um = sheared(st, 0).astype(BF), sheared(mt, 0).astype(BF)
        st, mt = st.astype(BF), mt.astype(BF)
        high_first, low_third = us * ahead, us * behind
        low_middle, high_middle = um * ahead, um * behind
        low, high = rq_ref[0:n], rq_ref[n:]
        dks.append((
            dot(st * below, qb) + dot(high_first, high),
            dot(mt, qb) + dot(low_middle, low) + dot(high_middle, high),
            dot(st * above, qb) + dot(low_third, low),
        ))
        kjt = [kjt_ref[qt + m, lo:hi, :] for m in range(3)]
        drqt_acc[lo:hi, 0:n] += dot(kjt[1], low_middle) + dot(kjt[2], low_third)
        drqt_acc[lo:hi, n:] += dot(kjt[0], high_first) + dot(kjt[1], high_middle)
    for m in range(3):
        dk_acc[qt + m] += both_heads(dks[0][m], dks[1][m])
    return dot(flip, both_heads(*dqs).astype(BF)).astype(BF)


def bwd_masks(n, mask_ref):
    row, lane = grid_of(n)
    for m, keep in enumerate((lane >= row, lane < row, row + lane >= n, row + lane < n)):
        mask_ref[m] = jnp.where(keep, 1.0, 0.0).astype(BF)


MESH = pl.DeviceIdType.MESH


def toggled(value, mask):
    out = value
    for bit in range(mask.bit_length()):
        if mask >> bit & 1:
            out = out + (1 - 2 * ((value // (1 << bit)) % 2)) * (1 << bit)
    return out


class Mesh:
    def __init__(self, ns, nb):
        self.ns, self.nb, self.nz = ns, nb, nb // 2
        self.bits = ns.bit_length() - 1
        self.ways = 2 if ns <= 4 else 1

    def locate(self):
        self.s = lax.axis_index("seq")
        self.b = lax.axis_index("batch")
        self.z, self.c = self.b // 2, self.b % 2

    def at(self, s, b):
        return {"seq": s, "batch": b}

    def greet(self):
        barrier = pltpu.get_barrier_semaphore()
        peers = [self.at(self.s, toggled(self.b, 1))]
        peers += [self.at(self.s, toggled(self.z, step) * 2 + self.c) for step in range(1, self.nz)]
        peers += [self.at(toggled(self.s, step), self.b) for step in range(1, self.ns)]
        for peer in peers:
            pl.semaphore_signal(barrier, inc=1, device_id=peer, device_id_type=MESH)
        pl.semaphore_wait(barrier, len(peers))


class Chunk:
    def __init__(self, mesh, rows, lanes, moves, box=None, early_z=False):
        self.mesh, self.rows, self.moves, self.box, self.early_z = mesh, rows, moves, box, early_z
        unit = 128 * mesh.ways * mesh.ns
        self.lanes = -(-lanes // unit) * unit
        self.piece = self.lanes // (mesh.ways * mesh.ns)
        self.depth = 1 if early_z else mesh.nz

    def scratch(self):
        mesh, rows, lanes = self.mesh, self.rows, self.lanes
        full = pltpu.VMEM((mesh.nz, rows, lanes), BF)
        shapes = [full] if self.box else [full, full]
        for level in range(mesh.bits):
            shapes.append(pltpu.VMEM((mesh.ways, self.depth, rows, lanes // mesh.ways // 2 >> level), BF))
        wide = lanes // mesh.ways if self.early_z else self.piece
        shapes += [pltpu.VMEM((mesh.ways, mesh.nz - 1, rows, wide), BF), pltpu.VMEM((rows, lanes), BF)]
        dma = pltpu.SemaphoreType.DMA
        moves = len(self.moves)
        shapes += [] if self.box else [dma((moves,))]
        shapes += [dma((2, moves)), dma((2, 2, mesh.bits)), dma((2, 2, mesh.nz - 1)), dma((2, 2, mesh.ns - 1))]
        return shapes

    def bind(self, refs):
        bits = self.mesh.bits
        if self.box:
            self.mine = self.box(self.mesh.c)
        else:
            self.mine, refs = refs[0], refs[1:]
        self.first = refs[0]
        self.halves = refs[1 : 1 + bits]
        self.across, self.final = refs[1 + bits : 3 + bits]
        refs = refs[3 + bits :]
        if not self.box:
            self.own_sem, refs = refs[0], refs[1:]
        self.core_sem, self.seq_sem, self.z_sem, self.out_sem = refs[:4]
        return refs[4:]

    def copy(self, src, dst, sems, index, s, b):
        return pltpu.make_async_remote_copy(
            src_ref=src,
            dst_ref=dst,
            send_sem=sems.at[(0,) + index],
            recv_sem=sems.at[(1,) + index],
            device_id=self.mesh.at(s, b),
            device_id_type=MESH,
        )

    def own_copies(self):
        for n, (source, at, size) in enumerate([] if self.box else self.moves):
            yield pltpu.make_async_copy(source(self.mesh.c), self.mine.at[:, :, pl.ds(at, size)], self.own_sem.at[n])

    def core_copies(self):
        mesh = self.mesh
        for n, (source, at, size) in enumerate(self.moves):
            yield self.copy(
                source(1 - mesh.c), self.first.at[:, :, pl.ds(at, size)], self.core_sem, (n,), mesh.s, toggled(mesh.b, 1)
            )

    def order(self, half, level):
        return (level + half) % self.mesh.bits

    def region(self, level, half):
        size = self.lanes // self.mesh.ways
        base = half * size
        sent = base
        for at in range(level):
            mine = (self.mesh.s // (1 << self.order(half, at))) % 2
            size = size // 2
            sent = base + (1 - mine) * size
            base = base + mine * size
        return base, sent, size

    def span(self, start, size):
        return pl.ds(pl.multiple_of(start, 128), size)

    def planes(self):
        return pl.ds(self.mesh.z, 1) if self.early_z else slice(None)

    def seq_copy(self, level, half):
        unused, sent, size = self.region(level + 1, half)
        return self.copy(
            self.mine.at[self.planes(), :, self.span(sent, size)],
            self.halves[level].at[half],
            self.seq_sem,
            (half, level),
            toggled(self.mesh.s, 1 << self.order(half, level)),
            self.mesh.b,
        )

    def z_region(self, half):
        kept, unused, size = self.region(0 if self.early_z else self.mesh.bits, half)
        return self.span(kept, size)

    def z_copies(self, half):
        mesh = self.mesh
        for step in range(1, mesh.nz):
            other = toggled(mesh.z, step)
            yield self.copy(
                self.mine.at[other, :, self.z_region(half)],
                self.across.at[half, step - 1],
                self.z_sem,
                (half, step - 1),
                mesh.s,
                other * 2 + mesh.c,
            )

    def out_copies(self, half):
        kept, unused, size = self.region(self.mesh.bits, half)
        for step in range(1, self.mesh.ns):
            lanes = self.span(kept, size)
            yield self.copy(
                self.final.at[:, lanes], self.final.at[:, lanes], self.out_sem, (half, step - 1), toggled(self.mesh.s, step), self.mesh.b
            )

    def start_core(self):
        for copy in self.core_copies():
            copy.start()
        for copy in self.own_copies():
            copy.start()

    def add_core(self):
        for copy in self.own_copies():
            copy.wait()
        for copy in self.core_copies():
            copy.wait_recv()
        parts = 4
        size = self.lanes // parts

        def add(n, carry):
            z, lanes = n // parts, self.span((n % parts) * size, size)
            self.mine[z, :, lanes] = (self.mine[z, :, lanes].astype(F32) + self.first[z, :, lanes].astype(F32)).astype(BF)
            return carry

        lax.fori_loop(0, self.mesh.nz * parts, add, 0)

    def start_seq(self, level):
        for half in range(self.mesh.ways):
            self.seq_copy(level, half).start()

    def add_seq(self, level):
        for half in range(self.mesh.ways):
            self.seq_copy(level, half).wait_recv()
            kept, unused, size = self.region(level + 1, half)
            lanes = self.span(kept, size)

            def add(n, carry):
                z = self.mesh.z if self.early_z else n
                got = self.halves[level][half, n].astype(F32)
                self.mine[z, :, lanes] = (self.mine[z, :, lanes].astype(F32) + got).astype(BF)
                return carry

            lax.fori_loop(0, self.depth, add, 0)
            if self.early_z and level == self.mesh.bits - 1:
                self.final[:, lanes] = self.mine[self.mesh.z, :, lanes]

    def end_seq(self):
        self.add_seq(1)
        for level in range(2, self.mesh.bits):
            self.start_seq(level)
            self.add_seq(level)

    def start_z(self):
        for half in range(self.mesh.ways):
            for copy in self.z_copies(half):
                copy.start()

    def add_z(self):
        z = self.mesh.z
        for half in range(self.mesh.ways):
            for copy in self.z_copies(half):
                copy.wait_recv()
            lanes = self.z_region(half)
            total = self.mine[z, :, lanes].astype(F32)
            for step in range(1, self.mesh.nz):
                total = total + self.across[half, step - 1].astype(F32)
            if self.early_z:
                self.mine[z, :, lanes] = total.astype(BF)
            else:
                self.final[:, lanes] = total.astype(BF)

    def start_out(self):
        for half in range(self.mesh.ways):
            for copy in self.out_copies(half):
                copy.start()

    def core(self):
        self.start_core()

    def s0(self):
        if self.early_z:
            self.add_z()
        else:
            self.add_core()
        self.start_seq(0)

    def s1(self):
        self.add_seq(0)
        self.start_seq(1)

    def z(self):
        if self.early_z:
            self.add_core()
        else:
            self.end_seq()
        self.start_z()

    def out(self):
        if self.early_z:
            self.end_seq()
        else:
            self.add_z()
        self.start_out()

    def finish(self):
        for half in range(self.mesh.ways):
            for copy in self.out_copies(half):
                copy.wait()
            for copy in self.z_copies(half):
                copy.wait_send()
            for level in range(self.mesh.bits):
                self.seq_copy(level, half).wait_send()
        for copy in self.core_copies():
            copy.wait_send()


class Layout:
    def __init__(self, ns, nb, width, hidden, table):
        self.mesh = mesh = Mesh(ns, nb)
        self.width, self.hidden = width, hidden
        self.rows = rows = width // nb
        self.fold = hidden // nb // rows
        self.rel_rows = table // nb
        self.pairs = width // 128
        self.third = width // 3
        self.rel_at = 384
        self.small_at = 384 + 512
        self.stack = rows // 16
        small_lanes = -(-self.pairs // self.stack) * 128
        down = [
            (lambda c, n=n: self.down_ref.at[:, c, pl.ds(n * rows, rows), :], n * width, width) for n in range(self.fold)
        ]
        into = [(lambda c: self.in_ref.at[:, c], 0, hidden)]
        self.down = Chunk(mesh, rows, self.fold * width, down)
        self.into = Chunk(mesh, rows, hidden, into)
        lanes = Chunk(mesh, rows, 768 + self.third, []).lanes
        self.near = []
        for n in range(3):
            box = lambda c, n=n: self.near_ref.at[n, :, c]
            self.near.append(Chunk(mesh, rows, lanes, [(box, 0, lanes)], box, early_z=n < 0))
        lanes = Chunk(mesh, rows, self.small_at + small_lanes, []).lanes
        far = lambda c: self.far_ref.at[:, c]
        self.far = Chunk(mesh, rows, lanes, [(far, 0, lanes)], far)
        self.chunks = [self.down, self.into, *self.near, self.far]

    def scratch(self):
        mesh = self.mesh
        shapes = [
            pltpu.VMEM((3, mesh.nz, 2, self.rows, self.near[0].lanes), BF),
            pltpu.VMEM((mesh.nz, 2, self.rows, self.far.lanes), BF),
            pltpu.SemaphoreType.DMA((3,)),
        ]
        for chunk in self.chunks:
            shapes += chunk.scratch()
        return shapes

    def bind(self, down_ref, in_ref, out_ref, refs):
        self.mesh.locate()
        self.down_ref, self.in_ref, self.out_ref = down_ref, in_ref, out_ref
        self.near_ref, self.far_ref, self.out_sem = refs[:3]
        refs = refs[3:]
        for chunk in self.chunks:
            refs = chunk.bind(refs)
        return refs

    def out_copies(self):
        for n in range(3):
            yield pltpu.make_async_copy(
                self.out_ref.at[:, :, :, pl.ds(n * self.third, self.third)],
                self.near_ref.at[n, :, :, :, pl.ds(768, self.third)],
                self.out_sem.at[n],
            )

    def store_pair(self, pair, grads):
        rows = self.rows
        box = pair // 2
        lanes = pl.ds(pl.multiple_of((pair % 2) * 384, 128), 384)

        @pl.when(pair < self.pairs - 1)
        def _():
            for b in range(self.mesh.nb):
                self.near_ref[box, b // 2, b % 2, :, lanes] = grads[b * rows : (b + 1) * rows]

        @pl.when(pair == self.pairs - 1)
        def _():
            for b in range(self.mesh.nb):
                self.far_ref[b // 2, b % 2, :, 0:384] = grads[b * rows : (b + 1) * rows]

    def store_rest(self, rel, vectors):
        take, at, half = self.rel_rows, self.rel_at, self.rel_rows // 2
        for b in range(self.mesh.nb):
            part = rel[b * take : (b + 1) * take]
            put = self.far_ref.at[b // 2, b % 2]
            put[0:take, at : at + 512] = part[:, 0:512]
            put[take : take + half, at : at + 256] = part[0:half, 512:768]
            put[take : take + half, at + 256 : at + 512] = part[half:, 512:768]
            for n in range(self.pairs):
                row, lane = (n % self.stack) * 16, self.small_at + (n // self.stack) * 128
                put[row : row + 16, lane : lane + 128] = vectors[:, n * 128 : (n + 1) * 128]

    def rel_of(self, far):
        take, at, half = self.rel_rows, self.rel_at, self.rel_rows // 2
        low = [far[take : take + half, at : at + 256], far[take : take + half, at + 256 : at + 512]]
        return jnp.concatenate([far[0:take, at : at + 512], jnp.concatenate(low, axis=0)], axis=1)

    def vectors_of(self, far):
        parts = []
        for n in range(self.pairs):
            row, lane = (n % self.stack) * 16, self.small_at + (n // self.stack) * 128
            parts.append(far[row : row + 16, lane : lane + 128])
        return jnp.concatenate(parts, axis=1)

    def pairs_of(self, near, far, n):
        blocks = [side[:, m * 384 + n * 128 : m * 384 + (n + 1) * 128] for side in near for m in range(2)][: self.pairs - 1]
        return jnp.concatenate(blocks + [far[:, n * 128 : (n + 1) * 128]], axis=1)

    def schedule(self, edges):
        down, into, one, two, three, far = self.chunks

        def open_all():
            self.mesh.greet()
            for copy in self.out_copies():
                copy.start()
            down.core()
            into.core()

        def open_near():
            for copy in self.out_copies():
                copy.wait()
            one.core()

        steps = {
            0: [open_all],
            1: [down.s0],
            2: [into.s0],
            4: [down.s1, open_near],
            5: [one.s0],
            6: [into.s1],
            7: [down.z],
            8: [one.s1, two.core],
            9: [into.z, two.s0],
            10: [down.out, three.core, one.z],
            11: [three.s0, two.s1],
        }
        last = [far.core, into.out, one.out, two.z, three.s1, far.s0, edges.start, two.out, three.z, far.s1, three.out, far.z, far.out]
        last += [chunk.finish for chunk in self.chunks]
        return steps, last


class Edges:
    def __init__(self, mesh, refs):
        self.mesh = mesh
        self.sent, self.got, self.sems = refs

    def copy(self, side):
        other = self.mesh.s + (2 * side - 1)
        return pltpu.make_async_remote_copy(
            src_ref=self.sent.at[side],
            dst_ref=self.got.at[1 - side],
            send_sem=self.sems.at[0, side],
            recv_sem=self.sems.at[1, 1 - side],
            device_id=self.mesh.at(other, self.mesh.b),
            device_id_type=MESH,
        )

    def has(self, side):
        return self.mesh.s > 0 if side == 0 else self.mesh.s < self.mesh.ns - 1

    def start(self):
        for side in range(2):
            pl.when(self.has(side))(lambda side=side: self.copy(side).start())

    def finish(self, add):
        for side in range(2):

            @pl.when(self.has(side))
            def _(side=side):
                self.copy(side).wait_send()
                self.copy(1 - side).wait_recv()
                add(side, self.got[side])


def bwd_kernel(tq, scale, layout, q_ref, k_ref, v_ref, g_ref, rk_ref, rq_ref, p_ref, wk_ref, wq_ref, wv_ref,
               g_one_ref, x_ref, rel_ref, picks_ref, small_ref, down_ref, in_ref, out_ref,
               dx_ref, down_out, in_out, near0_out, near1_out, near2_out, far_out,
               mask_ref, kjt_ref, dk_acc, dvt_acc, drkt_acc, drqt_acc,
               xt_ref, d_ref, rel_acc, vec_ref, dx_acc, sent_ref, got_ref, edge_sem, *refs):
    block = q_ref.shape[0]
    nq = block // tq
    ext = k_ref.shape[0]
    nk = ext // tq
    span = tq
    table = 2 * span
    pair = pl.program_id(0)
    pairs = layout.pairs
    flip = anti(tq)
    layout.bind(down_ref, in_ref, out_ref, refs)
    edges = Edges(layout.mesh, (sent_ref, got_ref, edge_sem))
    steps, last = layout.schedule(edges)

    def run(actions):
        def all_of():
            for action in actions:
                action()
        return all_of

    @pl.when(pair == 0)
    def _():
        run(steps[0])()
        bwd_masks(tq, mask_ref)
        for n in range(ext // 128):
            xt_ref[:, n * 128 : (n + 1) * 128] = x_ref[n * 128 : (n + 1) * 128, :].astype(F32).T.astype(BF)
        for n in range(table // 128):
            xt_ref[:, ext + n * 128 : ext + (n + 1) * 128] = rel_ref[n * 128 : (n + 1) * 128, :].astype(F32).T.astype(BF)
        d_ref[...] = jnp.zeros_like(d_ref)
        rel_acc[...] = jnp.zeros_like(rel_acc)
        dx_acc[...] = jnp.zeros_like(dx_acc)
        vec_ref[...] = small_ref[...].astype(F32)

    for kt in range(nk):
        kjt_ref[kt] = dot(k_ref[kt * tq : (kt + 1) * tq, :], flip, TN).astype(BF)
    dk_acc[...] = jnp.zeros_like(dk_acc)
    dvt_acc[...] = jnp.zeros_like(dvt_acc)
    drkt_acc[...] = jnp.zeros_like(drkt_acc)
    drqt_acc[...] = jnp.zeros_like(drqt_acc)

    def tile(qt, carry):
        for step, actions in steps.items():
            if step:
                pl.when(pair * nq + qt == step * pairs * nq // 12)(run(actions))
        row = pl.multiple_of(qt * tq, tq)
        dq = bwd_tile(
            tq, scale, qt, q_ref, k_ref, v_ref, g_ref, rk_ref, rq_ref, p_ref, mask_ref, kjt_ref, dk_acc, dvt_acc, drkt_acc, drqt_acc
        )
        d_ref[pl.ds(span + row, tq), 0:128] = dq
        return carry

    lax.fori_loop(0, nq, tile, 0)
    for kt in range(nk):
        here = slice(kt * tq, (kt + 1) * tq)
        dk = dot(flip, dk_acc[kt].astype(BF)).astype(BF)
        dv = dvt_acc[:, here].T.astype(BF)
        d_ref[here, 128:256] = dk
        d_ref[here, 256:384] = dv
    for st in range(table // 128):
        here = slice(ext + st * 128, ext + (st + 1) * 128)
        d_ref[here, 0:128] = drqt_acc[:, st * 128 : (st + 1) * 128].T.astype(BF)
        d_ref[here, 128:256] = drkt_acc[:, st * 128 : (st + 1) * 128].T.astype(BF)

    grads = dot(xt_ref[...], d_ref[...]).astype(BF)
    layout.store_pair(pair, grads)
    weights = jnp.concatenate([wq_ref[...], wk_ref[...], wv_ref[...]], axis=1)
    dx_acc[...] += dot(d_ref[0:ext], weights, NT)
    rel_acc[...] += dot(d_ref[ext:, 0:128], wq_ref[...], NT) + dot(d_ref[ext:, 128:256], wk_ref[...], NT)
    sums = dot(jnp.ones((8, ext + table), BF), d_ref[...])[0:1]
    for n in range(3):
        vec_ref[10 + n : 11 + n, pl.ds(pl.multiple_of(pair * 128, 128), 128)] = sums[:, n * 128 : (n + 1) * 128]

    @pl.when(pair == pairs - 1)
    def _():
        rel = dot(picks_ref[...], rel_acc[...].astype(BF)).astype(BF)
        layout.store_rest(rel, vec_ref[...].astype(BF))
        sent_ref[0] = dx_acc[0:span].astype(BF)
        sent_ref[1] = dx_acc[ext - span :].astype(BF)
        run(last[:1])()
        dx_ref[...] = g_one_ref[...] + dx_acc[span : span + block]
        run(last[1:])()

        def take(side, rows):
            here = slice(0, span) if side == 0 else slice(block - span, block)
            dx_ref[here] += rows.astype(F32)

        edges.finish(take)
        outs = (down_out, in_out, near0_out, near1_out, near2_out, far_out)
        for out, chunk in zip(outs, layout.chunks):
            out[...] = chunk.final[...]


def attn_bwd(span, q, k, v, g, rk, rq, probs, w_key, w_query, w_value, grad_one, x_ext, rel_flip, picks, small, down_grad, in_grad, out_grad):
    block, width = q.shape
    ext = k.shape[0]
    table = 2 * span
    scale = (3.0 * 64) ** -0.5
    ns, nb = lax.axis_size("seq"), lax.axis_size("batch")
    layout = Layout(ns, nb, width, in_grad.shape[1], table)
    col = lambda rows: pl.BlockSpec((rows, 128), lambda h: (0, h))
    whole = lambda shape: pl.BlockSpec(shape, lambda h: (0, 0), pipeline_mode=pl.Buffered(1))
    any_spec = pl.BlockSpec(memory_space=pl.ANY)
    by_share = lambda grad: grad.reshape(nb // 2, 2, grad.shape[0] // nb, grad.shape[1])
    packed = [jax.ShapeDtypeStruct((layout.rows, chunk.lanes), BF) for chunk in layout.chunks]
    outs = pl.pallas_call(
        functools.partial(bwd_kernel, span, scale, layout),
        grid=(width // 128,),
        out_shape=(
            jax.ShapeDtypeStruct((block, width), F32),
            *packed,
        ),
        in_specs=[col(block), col(ext), col(ext), col(block), col(rk.shape[0]), col(rq.shape[0]),
                  pl.BlockSpec((2, block, table), lambda h: (h, 0, 0)), col(width), col(width), col(width),
                  whole(grad_one.shape), whole(x_ext.shape), whole(rel_flip.shape), whole(picks.shape), whole(small.shape),
                  any_spec, any_spec, any_spec],
        out_specs=(whole((block, width)),) + tuple(whole(part.shape) for part in packed),
        scratch_shapes=[
            pltpu.VMEM((4, span, span), BF),
            pltpu.VMEM((ext // span, 128, span), BF),
            pltpu.VMEM((ext // span, span, 128), F32),
            pltpu.VMEM((128, ext), F32),
            pltpu.VMEM((128, table), F32),
            pltpu.VMEM((128, table), F32),
            pltpu.VMEM((width, ext + table), BF),
            pltpu.VMEM((ext + table, 384), BF),
            pltpu.VMEM((table, width), F32),
            pltpu.VMEM((16, width), F32),
            pltpu.VMEM((ext, width), F32),
            pltpu.VMEM((2, span, width), BF),
            pltpu.VMEM((2, span, width), BF),
            pltpu.SemaphoreType.DMA((2, 2)),
        ] + layout.scratch(),
        compiler_params=pltpu.CompilerParams(collective_id=0, has_side_effects=True, vmem_limit_bytes=60 << 20),
        cost_estimate=pl.CostEstimate(flops=50_000_000_000, bytes_accessed=20 << 20, transcendentals=0),
        name="attn_bwd_reduce",
    )(q, k, v, g, rk, rq, probs, w_key, w_query, w_value, grad_one, x_ext, rel_flip, picks, small,
      by_share(down_grad), by_share(in_grad), by_share(out_grad))
    return layout, outs


NORM_EPS = 1e-07


def norm_rows(values):
    centred = values - jnp.mean(values, axis=-1, keepdims=True)
    inv_std = lax.rsqrt(jnp.mean(centred * centred, axis=-1, keepdims=True) + NORM_EPS)
    return centred * inv_std, inv_std


def norm_back(grads, normed, inv_std):
    first_mean = jnp.mean(grads, axis=-1, keepdims=True)
    second_mean = jnp.mean(grads * normed, axis=-1, keepdims=True)
    return inv_std * (grads - first_mean - normed * second_mean)


def local(
    layer_input,
    w_query,
    b_query,
    w_key,
    b_key,
    w_value,
    b_value,
    w_out,
    b_out,
    gain_attn,
    shift_attn,
    w_in,
    b_in,
    w_down,
    b_down,
    gain_ffn,
    shift_ffn,
    rel_table,
    segment_ids,
    cotangent,
):
    rows, block, width = layer_input.shape
    span = rel_table.shape[0] // 2
    x = layer_input[0]
    count = lax.axis_size("seq")
    up = [(i, i + 1) for i in range(count - 1)]
    down = [(i + 1, i) for i in range(count - 1)]
    before = lax.ppermute(x[block - span :], "seq", up)
    after = lax.ppermute(x[:span], "seq", down)
    rel_flip = dot(anti(2 * span), rel_table).astype(BF)

    def project(rows_in, weight, bias):
        return (dot(rows_in, weight) + bias).astype(BF)

    q = project(x, w_query, b_query)
    rk = project(rel_flip, w_key, b_key)
    rq = project(rel_flip, w_query, b_query)
    x_ext = jnp.concatenate([before, x, after], axis=0)
    k = project(x_ext, w_key, b_key)
    v = project(x_ext, w_value, b_value)
    start = lax.axis_index("seq") * block
    padded = jnp.pad(segment_ids[0], (span, span), constant_values=-1)
    kid = lax.dynamic_slice_in_dim(padded, start, block + 2 * span, 0)
    qid = kid[span : span + block]
    context, probs = attn_fwd(span, q, k, v, rk, rq, qid[:, None], kid[None])

    residual_one = x.astype(F32) + dot(context, w_out) + b_out
    normed_one, inv_one = norm_rows(residual_one)
    hidden = normed_one * gain_attn + shift_attn
    hidden_low = hidden.astype(BF)
    pre_act = dot(hidden_low, w_in) + b_in
    phi = 0.5 * (1.0 + lax.erf(pre_act * (0.5**0.5)))
    act_low = (pre_act * phi).astype(BF)
    slope = phi + pre_act * (jnp.exp(-0.5 * pre_act * pre_act) * ((2.0 * math.pi) ** -0.5))
    residual_two = hidden + dot(act_low, w_down) + b_down
    normed_two, inv_two = norm_rows(residual_two)
    output = (normed_two * gain_ffn + shift_ffn).astype(BF)

    grad_out = cotangent[0].astype(F32)
    gain_ffn_grad = jnp.sum(grad_out * normed_two, axis=0)
    shift_ffn_grad = jnp.sum(grad_out, axis=0)
    grad_two = norm_back(grad_out * gain_ffn, normed_two, inv_two)
    grad_branch = grad_two.astype(BF)
    down_grad = dot(act_low, grad_branch, TN)
    down_bias_grad = jnp.sum(grad_branch.astype(F32), axis=0)
    grad_pre = (dot(grad_branch, w_down, NT) * slope).astype(BF)
    in_grad = dot(hidden_low, grad_pre, TN)
    in_bias_grad = jnp.sum(grad_pre.astype(F32), axis=0)
    grad_hidden = grad_two + dot(grad_pre, w_in, NT)
    gain_attn_grad = jnp.sum(grad_hidden * normed_one, axis=0)
    shift_attn_grad = jnp.sum(grad_hidden, axis=0)
    grad_one = norm_back(grad_hidden * gain_attn, normed_one, inv_one)
    grad_attn = grad_one.astype(BF)
    out_grad = dot(context, grad_attn, TN)
    out_bias_grad = jnp.sum(grad_attn.astype(F32), axis=0)
    grad_context = dot(grad_attn, w_out, NT).astype(BF)

    share, lanes = lax.axis_size("batch"), lax.axis_size("seq")
    rel_rows = 2 * span // (share * lanes)
    order = jnp.arange(2 * span).reshape(lanes, share, rel_rows).transpose(1, 0, 2).reshape(-1)
    picks = ((2 * span - 1 - order)[:, None] == jnp.arange(2 * span)[None]).astype(BF)
    small = [out_bias_grad, gain_attn_grad, shift_attn_grad, down_bias_grad, gain_ffn_grad, shift_ffn_grad, in_bias_grad]
    small = jnp.concatenate([vec.reshape(-1, width) for vec in small], axis=0)
    small = jnp.pad(small, ((0, 16 - small.shape[0]), (0, 0))).astype(BF)
    layout, outs = attn_bwd(
        span, q, k, v, grad_context, rk, rq, probs, w_key, w_query, w_value, grad_one, x_ext, rel_flip, picks, small,
        down_grad.astype(BF), in_grad.astype(BF), out_grad.astype(BF),
    )
    input_grad, down_sum, in_sum, *near, far = outs
    fold = layout.fold
    down_sum = jnp.concatenate([down_sum[:, n * width : (n + 1) * width] for n in range(fold)], axis=0).astype(F32)
    in_sum = in_sum[:, : layout.hidden].astype(F32)
    out_sum = jnp.concatenate([side[:, 768 : 768 + layout.third] for side in near], axis=1).astype(F32)
    query_sum, key_sum, value_sum = [layout.pairs_of(near, far, n).astype(F32) for n in range(3)]
    rel_sum = layout.rel_of(far)
    rel_sum = lax.dynamic_slice_in_dim(rel_sum, lax.axis_index("seq") * rel_rows, rel_rows, 0).astype(F32)
    vectors = layout.vectors_of(far).astype(F32)
    mine = lax.axis_index("batch") * layout.rows
    cut = lambda n: lax.dynamic_slice_in_dim(vectors[n], mine, layout.rows, 0)
    ob, ga, sa, db, gf, sf = [cut(n) for n in range(6)]
    wide = layout.hidden // share
    ib = lax.dynamic_slice_in_dim(vectors[6:10].reshape(-1), lax.axis_index("batch") * wide, wide, 0)
    qb, kb, vb = [cut(n) for n in range(10, 13)]
    return (
        output[None], input_grad[None], query_sum, qb, key_sum, kb, value_sum, vb, out_sum, ob,
        ga, sa, in_sum, ib, down_sum, db, gf, sf, rel_sum,
    )


def solution(mesh):
    tokens = P("batch", "seq", None)
    in_specs = (tokens,) + (P(),) * 17 + (P("batch", None), tokens)
    matrix, vector = P("batch", None), P("batch")
    out_specs = (
        (tokens, tokens)
        + (matrix, vector) * 4
        + (vector, vector)
        + (matrix, vector) * 2
        + (vector, vector, P(("seq", "batch"), None))
    )
    return jax.shard_map(local, mesh=mesh, in_specs=in_specs, out_specs=out_specs, check_vma=False)
```

```python
import functools
import math

import jax
import jax.numpy as jnp
import numpy as np
from jax import lax
from jax.experimental import pallas as pl
from jax.experimental.pallas import tpu as pltpu
from jax.sharding import PartitionSpec as P

F32 = jnp.float32
BF = jnp.bfloat16
NN = (((1,), (0,)), ((), ()))
NT = (((1,), (1,)), ((), ()))
TN = (((0,), (0,)), ((), ()))
MESH = pl.DeviceIdType.MESH


def toggled(value, mask):
    out = value
    for bit in range(mask.bit_length()):
        if mask >> bit & 1:
            out = out + (1 - 2 * ((value // (1 << bit)) % 2)) * (1 << bit)
    return out


def dot(a, b, dims=NN):
    return lax.dot_general(a, b, dims, preferred_element_type=F32)


def head_lanes(x, hh):
    lane = lax.broadcasted_iota(jnp.int32, x.shape, len(x.shape) - 1)
    keep = (lane < 64) if hh == 0 else (lane >= 64)
    return jnp.where(keep, x.astype(F32), 0.0).astype(x.dtype)


def both_heads(first, second):
    lane = lax.broadcasted_iota(jnp.int32, first.shape, 1)
    return jnp.where(lane < 64, first, second)


def grid_of(n):
    return lax.broadcasted_iota(jnp.int32, (n, n), 0), lax.broadcasted_iota(jnp.int32, (n, n), 1)


def anti(n):
    row, lane = grid_of(n)
    return jnp.where(row + lane == n - 1, 1.0, 0.0).astype(BF)


def sheared(x, shift):
    return pltpu.roll(x, shift, 1, stride=1, stride_axis=0)


def fwd_tile(n, scale, pair, qt, q_ref, k_ref, v_ref, rk_ref, rqm_ref, bias_ref, mask_ref, p_ref):
    factor = scale * math.log2(math.e)
    row, lane = grid_of(n)
    right, upper = lane > row, row + lane >= n - 1
    lanes = pl.ds(pl.multiple_of(pair * 128, 128), 128)
    at = lambda m: (pl.ds(pl.multiple_of((qt + m) * n, n), n), lanes)
    qb = q_ref[at(0)]
    rk_low, rk_high = rk_ref[0:n, lanes], rk_ref[n:, lanes]
    outs = []
    for hh in range(2):
        qm = head_lanes(qb, hh)
        low, high = rqm_ref[hh, 0:n, lanes], rqm_ref[hh, n:, lanes]
        to_low = sheared(dot(qm, rk_low, NT), 1)
        to_high = sheared(dot(qm, rk_high, NT), 1)
        side = jnp.where(right, dot(qm, k_ref[at(0)], NT) + to_low, dot(qm, k_ref[at(2)], NT) + to_high)
        middle = dot(qm, k_ref[at(1)], NT) + jnp.where(right, to_high, to_low)
        key_side = jnp.where(upper, dot(k_ref[at(0)], high, NT), dot(k_ref[at(2)], low, NT))
        key_middle = jnp.where(upper, dot(k_ref[at(1)], low, NT), dot(k_ref[at(1)], high, NT))
        side = (side + sheared(key_side, 1).T) * factor + bias_ref[:, 0:n]
        middle = (middle + sheared(key_middle, 1).T) * factor + bias_ref[:, n:]
        top = jnp.max(jnp.maximum(side, middle), axis=-1, keepdims=True)
        side, middle = jnp.exp2(side - top), jnp.exp2(middle - top)
        inverse = 1.0 / jnp.sum(side + middle, axis=-1, keepdims=True)
        side, middle = (side * inverse).astype(BF), (middle * inverse).astype(BF)
        p_ref[hh, :, 0:n] = side
        p_ref[hh, :, n:] = middle
        out = dot(side * mask_ref[0], v_ref[at(0)]) + dot(middle, v_ref[at(1)])
        outs.append(out + dot(side * mask_ref[1], v_ref[at(2)]))
    return both_heads(*outs).astype(BF)


class Halo:
    def __init__(self, span, block, ext_ref, sems):
        self.span, self.block, self.ext_ref, self.sems = span, block, ext_ref, sems
        self.s, self.b, self.ns = lax.axis_index("seq"), lax.axis_index("batch"), lax.axis_size("seq")

    def greet(self):
        barrier = pltpu.get_barrier_semaphore()
        for step in range(1, self.ns):
            peer = {"seq": toggled(self.s, step), "batch": self.b}
            pl.semaphore_signal(barrier, inc=1, device_id=peer, device_id_type=MESH)
        pl.semaphore_wait(barrier, self.ns - 1)

    def copy(self, up):
        span, block = self.span, self.block
        src, dst = (block, 0) if up else (span, span + block)
        return pltpu.make_async_remote_copy(
            src_ref=self.ext_ref.at[pl.ds(src, span)],
            dst_ref=self.ext_ref.at[pl.ds(dst, span)],
            send_sem=self.sems.at[0, int(up)],
            recv_sem=self.sems.at[1, int(up)],
            device_id={"seq": self.s + (1 if up else -1), "batch": self.b},
            device_id_type=MESH,
        )

    def sends(self, up):
        return self.s < self.ns - 1 if up else self.s > 0

    def gets(self, up):
        return self.s > 0 if up else self.s < self.ns - 1

    def start(self, up):
        pl.when(self.sends(up))(lambda: self.copy(up).start())

    def wait(self, up):
        at = pl.ds(0 if up else self.span + self.block, self.span)
        pl.when(self.gets(up))(lambda: self.copy(up).wait_recv())

        @pl.when(jnp.logical_not(self.gets(up)))
        def _():
            self.ext_ref[at] = jnp.zeros((self.span, self.ext_ref.shape[1]), BF)

    def finish(self):
        for up in (True, False):
            pl.when(self.sends(up))(lambda up=up: self.copy(up).wait_send())


def fwd_kernel(n, scale, x_hbm, rel_hbm, wk_hbm, wq_hbm, wv_hbm, bq_ref, bk_ref, bv_ref, qid_ref, kid_ref,
               ctx_ref, p_ref, q_out, k_out, v_out, rk_out, rq_out, xt_out,
               q_ref, k_ref, v_ref, rk_ref, rq_ref, xt_ref, ext_ref, rel_ref, flip_ref, wk_ref, wq_ref, wv_ref,
               rqm_ref, bias_ref, mask_ref, halo_sem, in_sem, out_sem):
    block = x_hbm.shape[0]
    ext = block + 2 * n
    qt, pair = pl.program_id(0), pl.program_id(1)
    last = (qt == pl.num_programs(0) - 1) & (pair == pl.num_programs(1) - 1)
    halo = Halo(n, block, ext_ref, halo_sem)
    row, lane = grid_of(n)
    bias_of = lambda ref: ref[...].astype(F32)[None]
    own = slice(n, n + block)
    kept = ((q_ref, q_out), (rk_ref, rk_out), (rq_ref, rq_out), (k_ref, k_out), (v_ref, v_out), (xt_ref, xt_out))
    loads = ((x_hbm, ext_ref.at[pl.ds(n, block)]), (rel_hbm, rel_ref), (wk_hbm, wk_ref), (wq_hbm, wq_ref), (wv_hbm, wv_ref))

    def load(m):
        return pltpu.make_async_copy(*loads[m], in_sem.at[m])

    def keep(first, end):
        for m in range(first, end):
            yield pltpu.make_async_copy(*kept[m], out_sem.at[m])

    def keys(rows):
        k_ref[rows] = (dot(ext_ref[rows], wk_ref[...]) + bias_of(bk_ref)).astype(BF)
        v_ref[rows] = (dot(ext_ref[rows], wv_ref[...]) + bias_of(bv_ref)).astype(BF)

    def turn(ref, first, size, at):
        for m in range(0, size, 128):
            xt_ref[:, at + m : at + m + 128] = ref[first + m : first + m + 128, :].astype(F32).T.astype(BF)

    def get_after():
        halo.wait(False)
        keys(slice(n + block, ext))
        turn(ext_ref, n + block, n, n + block)
        for copy in keep(3, 6):
            copy.start()

    @pl.when((qt == 0) & (pair == 0))
    def _():
        for m in range(5):
            load(m).start()
        halo.greet()
        load(0).wait()
        halo.start(True)
        load(1).wait()
        flip_ref[...] = dot(anti(2 * n), rel_ref[...]).astype(BF)
        load(2).wait()
        rk_ref[...] = (dot(flip_ref[...], wk_ref[...]) + bias_of(bk_ref)).astype(BF)
        load(3).wait()
        rq_ref[...] = (dot(flip_ref[...], wq_ref[...]) + bias_of(bq_ref)).astype(BF)
        q_ref[...] = (dot(ext_ref[own], wq_ref[...]) + bias_of(bq_ref)).astype(BF)
        for copy in keep(0, 3):
            copy.start()
        load(4).wait()
        keys(own)
        head = (lax.broadcasted_iota(jnp.int32, rq_ref.shape, 1) // 64) % 2
        for hh in range(2):
            rqm_ref[hh] = jnp.where(head == hh, rq_ref[...].astype(F32), 0.0).astype(BF)
        mask_ref[0] = jnp.where(lane > row, 1.0, 0.0).astype(BF)
        mask_ref[1] = jnp.where(lane > row, 0.0, 1.0).astype(BF)
        turn(ext_ref, n, block, n)
        turn(flip_ref, 0, 2 * n, ext)
        halo.wait(True)
        halo.start(False)
        keys(slice(0, n))
        turn(ext_ref, 0, n, 0)
        if block == n:
            get_after()

    if block > n:
        pl.when((qt == 1) & (pair == 0))(get_after)

    @pl.when(pair == 0)
    def _():
        at = lambda m: pl.ds(pl.multiple_of((qt + m) * n, n), n)
        qid = qid_ref[at(0), :]
        first, middle, third = [kid_ref[:, at(m)] for m in range(3)]
        side = ((lane > row) & (qid == first)) | ((lane < row) & (qid == third))
        bias_ref[:, 0:n] = jnp.where(side, 0.0, -1e30)
        bias_ref[:, n:] = jnp.where(qid == middle, 0.0, -1e30)

    ctx_ref[...] = fwd_tile(n, scale, pair, qt, q_ref, k_ref, v_ref, rk_ref, rqm_ref, bias_ref, mask_ref, p_ref)

    @pl.when(last)
    def _():
        halo.finish()
        for copy in keep(0, 6):
            copy.wait()


def attn_fwd(span, x, rel_table, w_query, w_key, w_value, b_query, b_key, b_value, qid, kid):
    block, width = x.shape
    ext, table = block + 2 * span, 2 * span
    scale = (3.0 * 64) ** -0.5
    heads = width // 64
    whole = lambda shape: pl.BlockSpec(shape, lambda t, h: (0,) * len(shape), pipeline_mode=pl.Buffered(1))
    far = pl.BlockSpec(memory_space=pltpu.HBM)
    small = [b_query, b_key, b_value, qid, kid]
    kept = [(rows, width) for rows in (block, ext, ext, table, table)] + [(width, ext + table)]
    more = [(ext, width), (table, width), (table, width)] + [(width, width)] * 3
    return pl.pallas_call(
        functools.partial(fwd_kernel, span, scale),
        grid=(block // span, width // 128),
        out_shape=[jax.ShapeDtypeStruct((block, width), BF), jax.ShapeDtypeStruct((heads, block, table), BF)]
        + [pltpu.HBM(shape, BF) for shape in kept],
        in_specs=[far] * 5 + [whole(arg.shape) for arg in small],
        out_specs=[pl.BlockSpec((span, 128), lambda t, h: (t, h)), pl.BlockSpec((2, span, table), lambda t, h: (h, t, 0))]
        + [far] * 6,
        scratch_shapes=[pltpu.VMEM(shape, BF) for shape in kept + more]
        + [
            pltpu.VMEM((2, table, width), BF),
            pltpu.VMEM((span, table), F32),
            pltpu.VMEM((2, span, span), BF),
            pltpu.SemaphoreType.DMA((2, 2)),
            pltpu.SemaphoreType.DMA((5,)),
            pltpu.SemaphoreType.DMA((6,)),
        ],
        compiler_params=pltpu.CompilerParams(collective_id=1, has_side_effects=True, vmem_limit_bytes=44 << 20),
        cost_estimate=pl.CostEstimate(flops=20_000_000_000, bytes_accessed=20 << 20, transcendentals=heads * block * table),
        name="attn_fwd",
    )(*[pltpu.with_memory_space_constraint(arg, pltpu.HBM) for arg in (x, rel_table, w_key, w_query, w_value)], *small)


def bwd_tile(n, scale, qt, q_ref, k_ref, v_ref, g_ref, rk_ref, rq_ref, p_ref, mask_ref, kjt_ref, dk_acc, dvt_acc, drkt_acc, drqt_acc):
    at = lambda m: pl.ds(pl.multiple_of((qt + m) * n, n), n)
    row, lane = grid_of(n)
    flip = anti(n)
    ahead, behind, above, below = [mask_ref[m] for m in range(4)]
    qb, gb = q_ref[at(0), :], g_ref[at(0), :]
    qjt = dot(qb, flip, TN).astype(BF)
    gt = gb.astype(F32).T.astype(BF)
    dqs, dks = [], []
    for hh in range(2):
        lo, hi = 64 * hh, 64 * hh + 64
        gm = head_lanes(gb, hh)
        side, middle = p_ref[hh, at(0), 0:n], p_ref[hh, at(0), n:]
        ps, pm = side.astype(F32) * scale, middle.astype(F32) * scale
        gs = jnp.where(lane > row, dot(gm, v_ref[at(0), :], NT), dot(gm, v_ref[at(2), :], NT))
        gd = dot(gm, v_ref[at(1), :], NT)
        ts, td = ps * gs, pm * gd
        total = jnp.sum(ts + td, axis=-1, keepdims=True) * (1.0 / scale)
        ds, dm = (ts - ps * total).astype(BF), (td - pm * total).astype(BF)
        for m, part in enumerate((side * ahead, middle, side * behind)):
            dvt_acc[lo:hi, at(m)] += dot(gt[lo:hi], part)

        sj, mj = dot(flip, ds), dot(flip, dm)
        right = row + lane >= n
        to_low = sheared(jnp.where(right, sj, mj), 0).astype(BF)
        to_high = sheared(jnp.where(right, mj, sj), 0).astype(BF)
        sj, mj = sj.astype(BF), mj.astype(BF)
        dq = dot(sj * above, k_ref[at(0), :]) + dot(mj, k_ref[at(1), :]) + dot(sj * below, k_ref[at(2), :])
        dqs.append(dq + dot(to_low, rk_ref[0:n]) + dot(to_high, rk_ref[n:]))
        drkt_acc[lo:hi, 0:n] += dot(qjt[lo:hi], to_low)
        drkt_acc[lo:hi, n:] += dot(qjt[lo:hi], to_high)

        st, mt = dot(flip, ds, NT), dot(flip, dm, NT)
        us, um = sheared(st, 0).astype(BF), sheared(mt, 0).astype(BF)
        st, mt = st.astype(BF), mt.astype(BF)
        high_first, low_third = us * ahead, us * behind
        low_middle, high_middle = um * ahead, um * behind
        low, high = rq_ref[0:n], rq_ref[n:]
        dks.append((
            dot(st * below, qb) + dot(high_first, high),
            dot(mt, qb) + dot(low_middle, low) + dot(high_middle, high),
            dot(st * above, qb) + dot(low_third, low),
        ))
        kjt = [kjt_ref[qt + m, lo:hi, :] for m in range(3)]
        drqt_acc[lo:hi, 0:n] += dot(kjt[1], low_middle) + dot(kjt[2], low_third)
        drqt_acc[lo:hi, n:] += dot(kjt[0], high_first) + dot(kjt[1], high_middle)
    for m in range(3):
        dk_acc[qt + m] += both_heads(dks[0][m], dks[1][m])
    return dot(flip, both_heads(*dqs).astype(BF)).astype(BF)


def bwd_masks(n, mask_ref):
    row, lane = grid_of(n)
    for m, keep in enumerate((lane >= row, lane < row, row + lane >= n, row + lane < n)):
        mask_ref[m] = jnp.where(keep, 1.0, 0.0).astype(BF)


class Mesh:
    def __init__(self, ns, nb):
        self.ns, self.nb, self.nz = ns, nb, nb // 2
        self.bits = ns.bit_length() - 1
        self.ways = 2 if ns <= 4 else 1

    def locate(self):
        self.s = lax.axis_index("seq")
        self.b = lax.axis_index("batch")
        self.z, self.c = self.b // 2, self.b % 2

    def at(self, s, b):
        return {"seq": s, "batch": b}

    def greet(self):
        barrier = pltpu.get_barrier_semaphore()
        peers = [self.at(self.s, toggled(self.b, 1))]
        peers += [self.at(self.s, toggled(self.z, step) * 2 + self.c) for step in range(1, self.nz)]
        peers += [self.at(toggled(self.s, step), self.b) for step in range(1, self.ns)]
        for peer in peers:
            pl.semaphore_signal(barrier, inc=1, device_id=peer, device_id_type=MESH)
        pl.semaphore_wait(barrier, len(peers))


class Chunk:
    def __init__(self, mesh, rows, lanes, moves, box=None, early_z=False):
        self.mesh, self.rows, self.moves, self.box, self.early_z = mesh, rows, moves, box, early_z
        unit = 128 * mesh.ways * mesh.ns
        self.lanes = -(-lanes // unit) * unit
        self.piece = self.lanes // (mesh.ways * mesh.ns)
        self.depth = 1 if early_z else mesh.nz

    def scratch(self):
        mesh, rows, lanes = self.mesh, self.rows, self.lanes
        full = pltpu.VMEM((mesh.nz, rows, lanes), BF)
        shapes = [full] if self.box else [full, full]
        for level in range(mesh.bits):
            shapes.append(pltpu.VMEM((mesh.ways, self.depth, rows, lanes // mesh.ways // 2 >> level), BF))
        wide = lanes // mesh.ways if self.early_z else self.piece
        shapes += [pltpu.VMEM((mesh.ways, mesh.nz - 1, rows, wide), BF), pltpu.VMEM((rows, lanes), BF)]
        dma = pltpu.SemaphoreType.DMA
        moves = len(self.moves)
        shapes += [] if self.box else [dma((moves,))]
        shapes += [dma((2, moves)), dma((2, 2, mesh.bits)), dma((2, 2, mesh.nz - 1)), dma((2, 2, mesh.bits))]
        return shapes

    def bind(self, refs):
        bits = self.mesh.bits
        if self.box:
            self.mine = self.box(self.mesh.c)
        else:
            self.mine, refs = refs[0], refs[1:]
        self.first = refs[0]
        self.halves = refs[1 : 1 + bits]
        self.across, self.final = refs[1 + bits : 3 + bits]
        refs = refs[3 + bits :]
        if not self.box:
            self.own_sem, refs = refs[0], refs[1:]
        self.core_sem, self.seq_sem, self.z_sem, self.out_sem = refs[:4]
        return refs[4:]

    def copy(self, src, dst, sems, index, s, b):
        return pltpu.make_async_remote_copy(
            src_ref=src,
            dst_ref=dst,
            send_sem=sems.at[(0,) + index],
            recv_sem=sems.at[(1,) + index],
            device_id=self.mesh.at(s, b),
            device_id_type=MESH,
        )

    def own_copies(self):
        for n, (source, at, size) in enumerate([] if self.box else self.moves):
            yield pltpu.make_async_copy(source(self.mesh.c), self.mine.at[:, :, pl.ds(at, size)], self.own_sem.at[n])

    def core_copies(self):
        mesh = self.mesh
        for n, (source, at, size) in enumerate(self.moves):
            yield self.copy(
                source(1 - mesh.c), self.first.at[:, :, pl.ds(at, size)], self.core_sem, (n,), mesh.s, toggled(mesh.b, 1)
            )

    def order(self, half, level):
        return (level + half) % self.mesh.bits

    def region(self, level, half):
        size = self.lanes // self.mesh.ways
        base = half * size
        sent = base
        for at in range(level):
            mine = (self.mesh.s // (1 << self.order(half, at))) % 2
            size = size // 2
            sent = base + (1 - mine) * size
            base = base + mine * size
        return base, sent, size

    def span(self, start, size):
        return pl.ds(pl.multiple_of(start, 128), size)

    def planes(self):
        return pl.ds(self.mesh.z, 1) if self.early_z else slice(None)

    def seq_copy(self, level, half):
        unused, sent, size = self.region(level + 1, half)
        return self.copy(
            self.mine.at[self.planes(), :, self.span(sent, size)],
            self.halves[level].at[half],
            self.seq_sem,
            (half, level),
            toggled(self.mesh.s, 1 << self.order(half, level)),
            self.mesh.b,
        )

    def z_region(self, half):
        kept, unused, size = self.region(0 if self.early_z else self.mesh.bits, half)
        return self.span(kept, size)

    def z_copies(self, half):
        mesh = self.mesh
        for step in range(1, mesh.nz):
            other = toggled(mesh.z, step)
            yield self.copy(
                self.mine.at[other, :, self.z_region(half)],
                self.across.at[half, step - 1],
                self.z_sem,
                (half, step - 1),
                mesh.s,
                other * 2 + mesh.c,
            )

    def out_copy(self, level, half):
        kept, unused, size = self.region(level + 1, half)
        lanes = self.span(kept, size)
        return self.copy(
            self.final.at[:, lanes],
            self.final.at[:, lanes],
            self.out_sem,
            (half, level),
            toggled(self.mesh.s, 1 << self.order(half, level)),
            self.mesh.b,
        )

    def start_core(self):
        for copy in self.core_copies():
            copy.start()
        for copy in self.own_copies():
            copy.start()

    def add_core(self):
        for copy in self.own_copies():
            copy.wait()
        for copy in self.core_copies():
            copy.wait_recv()
        parts = 4
        size = self.lanes // parts

        def add(n, carry):
            z, lanes = n // parts, self.span((n % parts) * size, size)
            self.mine[z, :, lanes] = (self.mine[z, :, lanes].astype(F32) + self.first[z, :, lanes].astype(F32)).astype(BF)
            return carry

        lax.fori_loop(0, self.mesh.nz * parts, add, 0)

    def start_seq(self, level):
        for half in range(self.mesh.ways):
            self.seq_copy(level, half).start()

    def add_seq(self, level):
        for half in range(self.mesh.ways):
            self.seq_copy(level, half).wait_recv()
            kept, unused, size = self.region(level + 1, half)
            lanes = self.span(kept, size)

            def add(n, carry):
                z = self.mesh.z if self.early_z else n
                got = self.halves[level][half, n].astype(F32)
                self.mine[z, :, lanes] = (self.mine[z, :, lanes].astype(F32) + got).astype(BF)
                return carry

            lax.fori_loop(0, self.depth, add, 0)
            if self.early_z and level == self.mesh.bits - 1:
                self.final[:, lanes] = self.mine[self.mesh.z, :, lanes]

    def end_seq(self):
        self.add_seq(1)
        for level in range(2, self.mesh.bits):
            self.start_seq(level)
            self.add_seq(level)

    def start_z(self):
        for half in range(self.mesh.ways):
            for copy in self.z_copies(half):
                copy.start()

    def add_z(self):
        z = self.mesh.z
        for half in range(self.mesh.ways):
            for copy in self.z_copies(half):
                copy.wait_recv()
            lanes = self.z_region(half)
            total = self.mine[z, :, lanes].astype(F32)
            for step in range(1, self.mesh.nz):
                total = total + self.across[half, step - 1].astype(F32)
            if self.early_z:
                self.mine[z, :, lanes] = total.astype(BF)
            else:
                self.final[:, lanes] = total.astype(BF)

    def start_out(self, level):
        for half in range(self.mesh.ways):
            self.out_copy(level, half).start()

    def core(self):
        self.start_core()

    def s0(self):
        if self.early_z:
            self.add_z()
        else:
            self.add_core()
        self.start_seq(0)

    def s1(self):
        self.add_seq(0)
        self.start_seq(1)

    def z(self):
        if self.early_z:
            self.add_core()
        else:
            self.end_seq()
        self.start_z()

    def out(self):
        if self.early_z:
            self.end_seq()
        else:
            self.add_z()
        self.start_out(self.mesh.bits - 1)

    def out2(self):
        for level in reversed(range(self.mesh.bits - 1)):
            for half in range(self.mesh.ways):
                self.out_copy(level + 1, half).wait_recv()
            self.start_out(level)

    def finish(self):
        for half in range(self.mesh.ways):
            self.out_copy(0, half).wait()
            for level in range(1, self.mesh.bits):
                self.out_copy(level, half).wait_send()
            for copy in self.z_copies(half):
                copy.wait_send()
            for level in range(self.mesh.bits):
                self.seq_copy(level, half).wait_send()
        for copy in self.core_copies():
            copy.wait_send()


class Layout:
    def __init__(self, ns, nb, width, hidden, table):
        self.mesh = mesh = Mesh(ns, nb)
        self.width, self.hidden = width, hidden
        self.rows = rows = width // nb
        self.fold = hidden // nb // rows
        self.rel_rows = table // nb
        self.pairs = width // 128
        self.third = width // 3
        self.rel_at = 384
        self.small_at = 384 + 512
        self.stack = rows // 16
        small_lanes = -(-self.pairs // self.stack) * 128
        self.split = split = hidden // 3
        whole = lambda name, lanes: self.boxed(lambda c: getattr(self, name).at[:, c], lanes)
        self.down = whole("down_ref", self.fold * width)
        self.into = whole("into_ref", hidden - split)
        self.rest = whole("rest_ref", split)
        lanes = Chunk(mesh, rows, 768 + self.third, []).lanes
        self.near = [self.boxed(lambda c, n=n: self.near_ref.at[n, :, c], lanes) for n in range(3)]
        self.far = whole("far_ref", self.small_at + small_lanes)
        self.chunks = [self.down, self.into, self.rest, *self.near, self.far]

    def boxed(self, box, lanes):
        chunk = Chunk(self.mesh, self.rows, lanes, [])
        chunk.box, chunk.moves = box, [(box, 0, chunk.lanes)]
        return chunk

    def starts(self):
        at = 0
        for chunk in self.chunks:
            yield at
            at += chunk.lanes

    def scratch(self):
        mesh = self.mesh
        box = lambda lanes: pltpu.VMEM((mesh.nz, 2, self.rows, lanes), BF)
        shapes = [box(chunk.lanes) for chunk in (self.down, self.into, self.rest, self.far)]
        shapes.append(pltpu.VMEM((3, mesh.nz, 2, self.rows, self.near[0].lanes), BF))
        for chunk in self.chunks:
            shapes += chunk.scratch()
        return shapes

    def bind(self, refs):
        self.mesh.locate()
        self.down_ref, self.into_ref, self.rest_ref, self.far_ref, self.near_ref = refs[:5]
        refs = refs[5:]
        for chunk in self.chunks:
            refs = chunk.bind(refs)
        return refs

    def store_down(self, m, grads):
        rows, share = self.rows, self.rows * self.fold
        for n in range(self.width // rows):
            b, part = divmod(m * self.width + n * rows, share)
            lanes = slice(part // rows * self.width, (part // rows + 1) * self.width)
            self.down_ref[b // 2, b % 2, :, lanes] = grads[n * rows : (n + 1) * rows]

    def store_into(self, m, grads):
        rows, split = self.rows, self.split
        ref, lanes = (self.rest_ref, slice(0, split)) if m == 0 else (self.into_ref, slice((m - 1) * split, m * split))
        for b in range(self.mesh.nb):
            ref[b // 2, b % 2, :, lanes] = grads[b * rows : (b + 1) * rows]

    def store_out(self, grads):
        rows, third = self.rows, self.third
        for b in range(self.mesh.nb):
            for n in range(3):
                part = grads[b * rows : (b + 1) * rows, n * third : (n + 1) * third]
                self.near_ref[n, b // 2, b % 2, :, 768 : 768 + third] = part

    def store_pair(self, pair, grads):
        rows = self.rows
        box = pair // 2
        lanes = pl.ds(pl.multiple_of((pair % 2) * 384, 128), 384)

        @pl.when(pair < self.pairs - 1)
        def _():
            for b in range(self.mesh.nb):
                self.near_ref[box, b // 2, b % 2, :, lanes] = grads[b * rows : (b + 1) * rows]

        @pl.when(pair == self.pairs - 1)
        def _():
            for b in range(self.mesh.nb):
                self.far_ref[b // 2, b % 2, :, 0:384] = grads[b * rows : (b + 1) * rows]

    def store_rest(self, rel, vectors):
        take, at, half = self.rel_rows, self.rel_at, self.rel_rows // 2
        for b in range(self.mesh.nb):
            part = rel[b * take : (b + 1) * take]
            put = self.far_ref.at[b // 2, b % 2]
            put[0:take, at : at + 512] = part[:, 0:512]
            put[take : take + half, at : at + 256] = part[0:half, 512:768]
            put[take : take + half, at + 256 : at + 512] = part[half:, 512:768]
            for n in range(self.pairs):
                row, lane = (n % self.stack) * 16, self.small_at + (n // self.stack) * 128
                put[row : row + 16, lane : lane + 128] = vectors[:, n * 128 : (n + 1) * 128]

    def schedule(self, edges):
        down, into, rest, one, two, three, far = self.chunks

        steps = {
            0: [],
            1: [down.s0],
            3: [into.s0, rest.s0],
            6: [down.s1, one.core],
            7: [one.s0],
            9: [into.s1, rest.s1],
            10: [down.z],
            12: [one.s1, two.core],
            13: [into.z, rest.z, two.s0],
            15: [down.out, three.core, one.z],
            16: [three.s0, two.s1],
        }
        last = [
            far.core,
            down.out2,
            into.out,
            rest.out,
            one.out,
            two.z,
            three.s1,
            far.s0,
            edges.start,
            into.out2,
            rest.out2,
            one.out2,
            two.out,
            three.z,
            far.s1,
            two.out2,
            three.out,
            far.z,
            three.out2,
            far.out,
            far.out2,
        ]
        last += [chunk.finish for chunk in self.chunks]
        return steps, last


class Edges:
    def __init__(self, mesh, refs):
        self.mesh = mesh
        self.sent, self.got, self.sems = refs

    def copy(self, side):
        other = self.mesh.s + (2 * side - 1)
        return pltpu.make_async_remote_copy(
            src_ref=self.sent.at[side],
            dst_ref=self.got.at[1 - side],
            send_sem=self.sems.at[0, side],
            recv_sem=self.sems.at[1, 1 - side],
            device_id=self.mesh.at(other, self.mesh.b),
            device_id_type=MESH,
        )

    def has(self, side):
        return self.mesh.s > 0 if side == 0 else self.mesh.s < self.mesh.ns - 1

    def start(self):
        for side in range(2):
            pl.when(self.has(side))(lambda side=side: self.copy(side).start())

    def finish(self, add):
        for side in range(2):

            @pl.when(self.has(side))
            def _(side=side):
                self.copy(side).wait_send()
                self.copy(1 - side).wait_recv()
                add(side, self.got[side])


def bwd_kernel(tq, scale, layout, q_ref, k_ref, v_ref, g_ref, rk_ref, rq_ref, p_ref, wk_ref, wq_ref, wv_ref,
               act_hbm, branch_ref, hidden_ref, pre_hbm, ctx_hbm, attn_hbm, g_one_hbm, xt_hbm, picks_ref, *rest):
    small_refs, rest = rest[:7], rest[7:]
    (dx_ref, packed_hbm,
               mask_ref, kjt_ref, dk_acc, dvt_acc, drkt_acc, drqt_acc,
               xt_ref, d_ref, rel_acc, vec_ref, dx_acc, sent_ref, got_ref, edge_sem,
     load_ref, load_sem, side_sem, packed_sem, *refs) = rest
    block = q_ref.shape[0]
    nq = block // tq
    ext = k_ref.shape[0]
    nk = ext // tq
    span = tq
    table = 2 * span
    pair = pl.program_id(0)
    pairs = layout.pairs
    flip = anti(tq)
    layout.bind(refs)
    edges = Edges(layout.mesh, (sent_ref, got_ref, edge_sem))
    steps, last = layout.schedule(edges)

    def run(actions):
        def all_of():
            for action in actions:
                action()
        return all_of

    loads = [act_hbm.at[:, pl.ds(m * layout.width, layout.width)] for m in range(layout.fold)]
    loads += [pre_hbm.at[:, pl.ds(m * layout.split, layout.split)] for m in range(3)]
    loads += [ctx_hbm, attn_hbm]

    def load(m):
        size = loads[m].shape
        return pltpu.make_async_copy(loads[m], load_ref.at[m % 3, pl.ds(0, size[0]), pl.ds(0, size[1])], load_sem.at[m % 3])

    def loaded(m):
        size = loads[m].shape
        load(m).wait()
        return load_ref[m % 3, 0 : size[0], 0 : size[1]]

    def dx_copy():
        return pltpu.make_async_copy(g_one_hbm, dx_ref, side_sem.at[0])

    def xt_copy():
        return pltpu.make_async_copy(xt_hbm, xt_ref, side_sem.at[1])

    @pl.when(pair == 0)
    def _():
        for m in range(2):
            load(m).start()
        layout.mesh.greet()
        m = 0
        for n in range(layout.fold):
            load(m + 2).start()
            layout.store_down(n, dot(loaded(m), branch_ref[...], TN).astype(BF))
            m += 1
        layout.down.core()
        for n in range(3):
            if m + 2 < len(loads):
                load(m + 2).start()
            layout.store_into(n, dot(hidden_ref[...], loaded(m), TN).astype(BF))
            if n == 0:
                layout.rest.core()
            m += 1
        xt_copy().start()
        dx_copy().start()
        layout.into.core()
        run(steps[0])()
        layout.store_out(dot(loaded(m), loaded(m + 1), TN).astype(BF))
        bwd_masks(tq, mask_ref)
        d_ref[...] = jnp.zeros_like(d_ref)
        rel_acc[...] = jnp.zeros_like(rel_acc)
        dx_acc[...] = jnp.zeros_like(dx_acc)
        vec_ref[...] = jnp.zeros_like(vec_ref)
        for n, ref in enumerate(small_refs[:6]):
            vec_ref[n : n + 1, :] = ref[...][None]
        for n in range(layout.fold):
            vec_ref[6 + n : 7 + n, :] = small_refs[6][n * layout.width : (n + 1) * layout.width][None]

    for kt in range(nk):
        kjt_ref[kt] = dot(k_ref[kt * tq : (kt + 1) * tq, :], flip, TN).astype(BF)
    dk_acc[...] = jnp.zeros_like(dk_acc)
    dvt_acc[...] = jnp.zeros_like(dvt_acc)
    drkt_acc[...] = jnp.zeros_like(drkt_acc)
    drqt_acc[...] = jnp.zeros_like(drqt_acc)

    def tile(qt, carry):
        for step, actions in steps.items():
            if step and step % 3 < min(nq, 2):
                pl.when((pair == step // 3) & (qt == step % 3))(run(actions))
        row = pl.multiple_of(qt * tq, tq)
        dq = bwd_tile(
            tq, scale, qt, q_ref, k_ref, v_ref, g_ref, rk_ref, rq_ref, p_ref, mask_ref, kjt_ref, dk_acc, dvt_acc, drkt_acc, drqt_acc
        )
        d_ref[pl.ds(span + row, tq), 0:128] = dq
        return carry

    lax.fori_loop(0, nq, tile, 0)
    for step, actions in steps.items():
        if step % 3 >= min(nq, 2):
            pl.when(pair == step // 3)(run(actions))
    for kt in range(nk):
        here = slice(kt * tq, (kt + 1) * tq)
        dk = dot(flip, dk_acc[kt].astype(BF)).astype(BF)
        dv = dvt_acc[:, here].T.astype(BF)
        d_ref[here, 128:256] = dk
        d_ref[here, 256:384] = dv
    for st in range(table // 128):
        here = slice(ext + st * 128, ext + (st + 1) * 128)
        d_ref[here, 0:128] = drqt_acc[:, st * 128 : (st + 1) * 128].T.astype(BF)
        d_ref[here, 128:256] = drkt_acc[:, st * 128 : (st + 1) * 128].T.astype(BF)

    pl.when(pair == 0)(lambda: xt_copy().wait())
    grads = dot(xt_ref[...], d_ref[...]).astype(BF)
    layout.store_pair(pair, grads)
    weights = jnp.concatenate([wq_ref[...], wk_ref[...], wv_ref[...]], axis=1)
    dx_acc[...] += dot(d_ref[0:ext], weights, NT)
    rel_acc[...] += dot(d_ref[ext:, 0:128], wq_ref[...], NT) + dot(d_ref[ext:, 128:256], wk_ref[...], NT)
    sums = dot(jnp.ones((8, ext + table), BF), d_ref[...])[0:1]
    for n in range(3):
        vec_ref[10 + n : 11 + n, pl.ds(pl.multiple_of(pair * 128, 128), 128)] = sums[:, n * 128 : (n + 1) * 128]

    @pl.when(pair == pairs - 1)
    def _():
        rel = dot(picks_ref[...], rel_acc[...].astype(BF)).astype(BF)
        layout.store_rest(rel, vec_ref[...].astype(BF))
        sent_ref[0] = dx_acc[0:span].astype(BF)
        sent_ref[1] = dx_acc[ext - span :].astype(BF)
        run(last[:1])()
        dx_copy().wait()
        dx_ref[...] += dx_acc[span : span + block]
        run(last[1:])()

        packed_copies = []
        for n, (at, chunk) in enumerate(zip(layout.starts(), layout.chunks)):
            packed_copies.append(pltpu.make_async_copy(chunk.final, packed_hbm.at[:, pl.ds(at, chunk.lanes)], packed_sem.at[n]))
            packed_copies[-1].start()

        def take(side, rows):
            here = slice(0, span) if side == 0 else slice(block - span, block)
            dx_ref[here] += rows.astype(F32)

        edges.finish(take)
        for copy in packed_copies:
            copy.wait()


def attn_bwd(span, q, k, v, g, rk, rq, probs, w_key, w_query, w_value, act, branch, hidden, pre, context, g_attn, g_one, xt, picks, small):
    block, width = q.shape
    ext = k.shape[0]
    table = 2 * span
    scale = (3.0 * 64) ** -0.5
    ns, nb = lax.axis_size("seq"), lax.axis_size("batch")
    layout = Layout(ns, nb, width, act.shape[1], table)
    col = lambda rows: pl.BlockSpec((rows, 128), lambda h: (0, h))
    whole = lambda shape: pl.BlockSpec(shape, lambda h: (0, 0), pipeline_mode=pl.Buffered(1))
    any_spec = pl.BlockSpec(memory_space=pltpu.HBM)
    packed = jax.ShapeDtypeStruct((layout.rows, sum(chunk.lanes for chunk in layout.chunks)), BF)
    outs = pl.pallas_call(
        functools.partial(bwd_kernel, span, scale, layout),
        grid=(width // 128,),
        out_shape=(
            jax.ShapeDtypeStruct((block, width), F32),
            packed,
        ),
        in_specs=[col(block), col(ext), col(ext), col(block), col(rk.shape[0]), col(rq.shape[0]),
                  pl.BlockSpec((2, block, table), lambda h: (h, 0, 0)), col(width), col(width), col(width),
                  any_spec, whole(branch.shape), whole(hidden.shape), any_spec, any_spec, any_spec, any_spec, any_spec,
                  whole(picks.shape)] + [pl.BlockSpec(part.shape, lambda h: (0,)) for part in small],
        out_specs=(whole((block, width)), any_spec),
        scratch_shapes=[
            pltpu.VMEM((4, span, span), BF),
            pltpu.VMEM((ext // span, 128, span), BF),
            pltpu.VMEM((ext // span, span, 128), F32),
            pltpu.VMEM((128, ext), F32),
            pltpu.VMEM((128, table), F32),
            pltpu.VMEM((128, table), F32),
            pltpu.VMEM((width, ext + table), BF),
            pltpu.VMEM((ext + table, 384), BF),
            pltpu.VMEM((table, width), F32),
            pltpu.VMEM((16, width), F32),
            pltpu.VMEM((ext, width), F32),
            pltpu.VMEM((2, span, width), BF),
            pltpu.VMEM((2, span, width), BF),
            pltpu.SemaphoreType.DMA((2, 2)),
            pltpu.VMEM((3, block, layout.split), BF),
            pltpu.SemaphoreType.DMA((3,)),
            pltpu.SemaphoreType.DMA((2,)),
            pltpu.SemaphoreType.DMA((len(layout.chunks),)),
        ] + layout.scratch(),
        compiler_params=pltpu.CompilerParams(collective_id=0, has_side_effects=True, vmem_limit_bytes=60 << 20),
        cost_estimate=pl.CostEstimate(flops=50_000_000_000, bytes_accessed=20 << 20, transcendentals=0),
        name="attn_bwd_reduce",
    )(*[pltpu.with_memory_space_constraint(arg, pltpu.HBM) for arg in (q, k, v)], g, *[pltpu.with_memory_space_constraint(arg, pltpu.HBM) for arg in (rk, rq, probs)], w_key, w_query, w_value, act, branch, hidden, pre, context, g_attn, g_one, pltpu.with_memory_space_constraint(xt, pltpu.HBM), picks, *small)
    return layout, outs


def unpack_kernel(layout, packed_ref,
                  down_out, into_out, out_out, query_out, key_out, value_out, rel_out, *refs):
    vec_outs, wide_out, (rel_ref, vec_ref) = refs[:-3], refs[-3], refs[-2:]
    rows, width, pairs = layout.rows, layout.width, layout.pairs
    parts = [packed_ref.at[:, at : at + chunk.lanes] for at, chunk in zip(layout.starts(), layout.chunks)]
    down_ref, into_ref, rest_ref, *near, far_ref = parts
    split = layout.hidden // 3
    into_out[:, :split] = rest_ref[:, :split].astype(F32)
    into_out[:, split:] = into_ref[:, : layout.hidden - split].astype(F32)
    for n in range(layout.fold):
        down_out[n * rows : (n + 1) * rows, :] = down_ref[:, n * width : (n + 1) * width].astype(F32)
    for n, side in enumerate(near):
        out_out[:, n * layout.third : (n + 1) * layout.third] = side[:, 768 : 768 + layout.third].astype(F32)
    for m in range(pairs):
        side, at = (far_ref, 0) if m == pairs - 1 else (near[m // 2], m % 2 * 384)
        for n, out in enumerate((query_out, key_out, value_out)):
            out[:, m * 128 : (m + 1) * 128] = side[:, at + n * 128 : at + (n + 1) * 128].astype(F32)
    take, at, half = layout.rel_rows, layout.rel_at, layout.rel_rows // 2
    rel_ref[:, 0:512] = far_ref[0:take, at : at + 512].astype(F32)
    for n in range(2):
        rel_ref[n * half : (n + 1) * half, 512:768] = far_ref[take : take + half, at + n * 256 : at + (n + 1) * 256].astype(F32)
    own = take // layout.mesh.ns
    rel_out[...] = pltpu.roll(rel_ref[...], take - lax.axis_index("seq") * own, 0)[:own]
    for n in range(pairs):
        row, lane = (n % layout.stack) * 16, layout.small_at + (n // layout.stack) * 128
        vec_ref[:, n * 128 : (n + 1) * 128] = far_ref[row : row + 16, lane : lane + 128].astype(F32)
    b = lax.axis_index("batch")
    mine = pltpu.roll(vec_ref[...], width - b * rows, 1)
    for out, n in zip(vec_outs, (0, 1, 2, 3, 4, 5, 10, 11, 12)):
        out[...] = mine[n, :rows]
    wide = wide_out.shape[0]
    fit = width // wide
    line = pltpu.roll(pltpu.roll(vec_ref[...], width - (b % fit) * wide, 1), 10 - b // fit, 0)
    wide_out[...] = line[0, :wide]


def unpack(layout, packed):
    rows, width = layout.rows, layout.width
    shape = lambda *dims: jax.ShapeDtypeStruct(dims, F32)
    shapes = [shape(layout.fold * rows, width), shape(rows, layout.hidden)] + [shape(rows, width)] * 4
    shapes += [shape(layout.rel_rows // layout.mesh.ns, width)] + [shape(rows)] * 9 + [shape(layout.fold * rows)]
    return pl.pallas_call(
        functools.partial(unpack_kernel, layout),
        out_shape=shapes,
        scratch_shapes=[pltpu.VMEM((layout.rel_rows, width), F32), pltpu.VMEM((16, width), F32)],
        compiler_params=pltpu.CompilerParams(vmem_limit_bytes=32 << 20),
        name="unpack",
    )(packed)


NORM_EPS = 1e-07


def norm_rows(values):
    centred = values - jnp.mean(values, axis=-1, keepdims=True)
    inv_std = lax.rsqrt(jnp.mean(centred * centred, axis=-1, keepdims=True) + NORM_EPS)
    return centred * inv_std, inv_std


def norm_back(grads, normed, inv_std):
    first_mean = jnp.mean(grads, axis=-1, keepdims=True)
    second_mean = jnp.mean(grads * normed, axis=-1, keepdims=True)
    return inv_std * (grads - first_mean - normed * second_mean)


def local(
    layer_input,
    w_query,
    b_query,
    w_key,
    b_key,
    w_value,
    b_value,
    w_out,
    b_out,
    gain_attn,
    shift_attn,
    w_in,
    b_in,
    w_down,
    b_down,
    gain_ffn,
    shift_ffn,
    rel_table,
    segment_ids,
    cotangent,
):
    rows, block, width = layer_input.shape
    span = rel_table.shape[0] // 2
    x = layer_input[0]
    start = lax.axis_index("seq") * block
    padded = jnp.pad(segment_ids[0], (span, span), constant_values=-1)
    kid = lax.dynamic_slice_in_dim(padded, start, block + 2 * span, 0)
    qid = kid[span : span + block]
    context, probs, q, k, v, rk, rq, xt = attn_fwd(
        span, x, rel_table, w_query, w_key, w_value, b_query, b_key, b_value, qid[:, None], kid[None]
    )

    residual_one = x.astype(F32) + dot(context, w_out) + b_out
    normed_one, inv_one = norm_rows(residual_one)
    hidden = normed_one * gain_attn + shift_attn
    hidden_low = hidden.astype(BF)
    pre_act = dot(hidden_low, w_in) + b_in
    phi = 0.5 * (1.0 + lax.erf(pre_act * (0.5**0.5)))
    act_low = (pre_act * phi).astype(BF)
    slope = phi + pre_act * (jnp.exp(-0.5 * pre_act * pre_act) * ((2.0 * math.pi) ** -0.5))
    residual_two = hidden + dot(act_low, w_down) + b_down
    normed_two, inv_two = norm_rows(residual_two)
    output = (normed_two * gain_ffn + shift_ffn).astype(BF)

    grad_out = cotangent[0].astype(F32)
    gain_ffn_grad = jnp.sum(grad_out * normed_two, axis=0)
    shift_ffn_grad = jnp.sum(grad_out, axis=0)
    grad_two = norm_back(grad_out * gain_ffn, normed_two, inv_two)
    grad_branch = grad_two.astype(BF)
    down_bias_grad = jnp.sum(grad_branch.astype(F32), axis=0)
    grad_pre = (dot(grad_branch, w_down, NT) * slope).astype(BF)
    in_bias_grad = jnp.sum(grad_pre.astype(F32), axis=0)
    grad_hidden = grad_two + dot(grad_pre, w_in, NT)
    gain_attn_grad = jnp.sum(grad_hidden * normed_one, axis=0)
    shift_attn_grad = jnp.sum(grad_hidden, axis=0)
    grad_one = norm_back(grad_hidden * gain_attn, normed_one, inv_one)
    grad_attn = grad_one.astype(BF)
    out_bias_grad = jnp.sum(grad_attn.astype(F32), axis=0)
    grad_context = dot(grad_attn, w_out, NT).astype(BF)

    share, lanes = lax.axis_size("batch"), lax.axis_size("seq")
    rel_rows = 2 * span // (share * lanes)
    order = np.arange(2 * span).reshape(lanes, share, rel_rows).transpose(1, 0, 2).reshape(-1)
    picks = jnp.asarray((2 * span - 1 - order)[:, None] == np.arange(2 * span)[None], BF)
    small = [out_bias_grad, gain_attn_grad, shift_attn_grad, down_bias_grad, gain_ffn_grad, shift_ffn_grad, in_bias_grad]
    layout, outs = attn_bwd(
        span, q, k, v, grad_context, rk, rq, probs, w_key, w_query, w_value, act_low, grad_branch, hidden_low, grad_pre,
        context, grad_attn, grad_one, xt, picks, small,
    )
    input_grad, packed = outs
    down_sum, in_sum, out_sum, query_sum, key_sum, value_sum, rel_sum, *vectors = unpack(layout, packed)
    ob, ga, sa, db, gf, sf, qb, kb, vb, ib = vectors
    return (
        output[None], input_grad[None], query_sum, qb, key_sum, kb, value_sum, vb, out_sum, ob,
        ga, sa, in_sum, ib, down_sum, db, gf, sf, rel_sum,
    )


def solution(mesh):
    tokens = P("batch", "seq", None)
    in_specs = (tokens,) + (P(),) * 17 + (P("batch", None), tokens)
    matrix, vector = P("batch", None), P("batch")
    out_specs = (
        (tokens, tokens)
        + (matrix, vector) * 4
        + (vector, vector)
        + (matrix, vector) * 2
        + (vector, vector, P(("seq", "batch"), None))
    )
    return jax.shard_map(local, mesh=mesh, in_specs=in_specs, out_specs=out_specs, check_vma=False)
```

```python
import functools
import math

import jax
import jax.numpy as jnp
import numpy as np
from jax import lax
from jax.experimental import pallas as pl
from jax.experimental.pallas import tpu as pltpu
from jax.sharding import PartitionSpec as P

F32 = jnp.float32
BF = jnp.bfloat16
NN = (((1,), (0,)), ((), ()))
NT = (((1,), (1,)), ((), ()))
TN = (((0,), (0,)), ((), ()))
MESH = pl.DeviceIdType.MESH


def toggled(value, mask):
    out = value
    for bit in range(mask.bit_length()):
        if mask >> bit & 1:
            out = out + (1 - 2 * ((value // (1 << bit)) % 2)) * (1 << bit)
    return out


def dot(a, b, dims=NN):
    return lax.dot_general(a, b, dims, preferred_element_type=F32)


def head_lanes(x, hh):
    lane = lax.broadcasted_iota(jnp.int32, x.shape, len(x.shape) - 1)
    keep = (lane < 64) if hh == 0 else (lane >= 64)
    return jnp.where(keep, x.astype(F32), 0.0).astype(x.dtype)


def both_heads(first, second):
    lane = lax.broadcasted_iota(jnp.int32, first.shape, 1)
    return jnp.where(lane < 64, first, second)


def grid_of(n):
    return lax.broadcasted_iota(jnp.int32, (n, n), 0), lax.broadcasted_iota(jnp.int32, (n, n), 1)


def anti(n):
    row, lane = grid_of(n)
    return jnp.where(row + lane == n - 1, 1.0, 0.0).astype(BF)


def sheared(x, shift):
    return pltpu.roll(x, shift, 1, stride=1, stride_axis=0)


def fwd_tile(n, scale, pair, qt, q_ref, k_ref, v_ref, rk_ref, rqm_ref, bias_ref, mask_ref, p_ref):
    factor = scale * math.log2(math.e)
    row, lane = grid_of(n)
    right, upper = lane > row, row + lane >= n - 1
    lanes = pl.ds(pl.multiple_of(pair * 128, 128), 128)
    at = lambda m: (pl.ds(pl.multiple_of((qt + m) * n, n), n), lanes)
    qb = q_ref[at(0)]
    rk_low, rk_high = rk_ref[0:n, lanes], rk_ref[n:, lanes]
    outs = []
    for hh in range(2):
        qm = head_lanes(qb, hh)
        low, high = rqm_ref[hh, 0:n, lanes], rqm_ref[hh, n:, lanes]
        to_low = sheared(dot(qm, rk_low, NT), 1)
        to_high = sheared(dot(qm, rk_high, NT), 1)
        side = jnp.where(right, dot(qm, k_ref[at(0)], NT) + to_low, dot(qm, k_ref[at(2)], NT) + to_high)
        middle = dot(qm, k_ref[at(1)], NT) + jnp.where(right, to_high, to_low)
        key_side = jnp.where(upper, dot(k_ref[at(0)], high, NT), dot(k_ref[at(2)], low, NT))
        key_middle = jnp.where(upper, dot(k_ref[at(1)], low, NT), dot(k_ref[at(1)], high, NT))
        side = (side + sheared(key_side, 1).T) * factor + bias_ref[:, 0:n]
        middle = (middle + sheared(key_middle, 1).T) * factor + bias_ref[:, n:]
        top = jnp.max(jnp.maximum(side, middle), axis=-1, keepdims=True)
        side, middle = jnp.exp2(side - top), jnp.exp2(middle - top)
        inverse = 1.0 / jnp.sum(side + middle, axis=-1, keepdims=True)
        side, middle = (side * inverse).astype(BF), (middle * inverse).astype(BF)
        p_ref[hh, :, 0:n] = side
        p_ref[hh, :, n:] = middle
        out = dot(side * mask_ref[0], v_ref[at(0)]) + dot(middle, v_ref[at(1)])
        outs.append(out + dot(side * mask_ref[1], v_ref[at(2)]))
    return both_heads(*outs).astype(BF)


class Halo:
    def __init__(self, span, block, ext_ref, sems):
        self.span, self.block, self.ext_ref, self.sems = span, block, ext_ref, sems
        self.s, self.b, self.ns = lax.axis_index("seq"), lax.axis_index("batch"), lax.axis_size("seq")

    def greet(self):
        barrier = pltpu.get_barrier_semaphore()
        for step in range(1, self.ns):
            peer = {"seq": toggled(self.s, step), "batch": self.b}
            pl.semaphore_signal(barrier, inc=1, device_id=peer, device_id_type=MESH)
        pl.semaphore_wait(barrier, self.ns - 1)

    def copy(self, up):
        span, block = self.span, self.block
        src, dst = (block, 0) if up else (span, span + block)
        return pltpu.make_async_remote_copy(
            src_ref=self.ext_ref.at[pl.ds(src, span)],
            dst_ref=self.ext_ref.at[pl.ds(dst, span)],
            send_sem=self.sems.at[0, int(up)],
            recv_sem=self.sems.at[1, int(up)],
            device_id={"seq": self.s + (1 if up else -1), "batch": self.b},
            device_id_type=MESH,
        )

    def sends(self, up):
        return self.s < self.ns - 1 if up else self.s > 0

    def gets(self, up):
        return self.s > 0 if up else self.s < self.ns - 1

    def start(self, up):
        pl.when(self.sends(up))(lambda: self.copy(up).start())

    def wait(self, up):
        at = pl.ds(0 if up else self.span + self.block, self.span)
        pl.when(self.gets(up))(lambda: self.copy(up).wait_recv())

        @pl.when(jnp.logical_not(self.gets(up)))
        def _():
            self.ext_ref[at] = jnp.zeros((self.span, self.ext_ref.shape[1]), BF)

    def finish(self):
        for up in (True, False):
            pl.when(self.sends(up))(lambda up=up: self.copy(up).wait_send())


def fwd_kernel(n, scale, x_hbm, rel_hbm, wk_hbm, wq_hbm, wv_hbm, bq_ref, bk_ref, bv_ref, qid_ref, kid_ref,
               ctx_ref, p_ref, q_out, k_out, v_out, rk_out, rq_out, xt_out,
               q_ref, k_ref, v_ref, rk_ref, rq_ref, xt_ref, ext_ref, rel_ref, flip_ref, wk_ref, wq_ref, wv_ref,
               rqm_ref, bias_ref, mask_ref, halo_sem, in_sem, out_sem):
    block = x_hbm.shape[0]
    ext = block + 2 * n
    qt, pair = pl.program_id(0), pl.program_id(1)
    last = (qt == pl.num_programs(0) - 1) & (pair == pl.num_programs(1) - 1)
    halo = Halo(n, block, ext_ref, halo_sem)
    row, lane = grid_of(n)
    bias_of = lambda ref: ref[...].astype(F32)[None]
    own = slice(n, n + block)
    kept = ((q_ref, q_out), (rk_ref, rk_out), (rq_ref, rq_out), (k_ref, k_out), (v_ref, v_out), (xt_ref, xt_out))
    loads = ((x_hbm, ext_ref.at[pl.ds(n, block)]), (rel_hbm, rel_ref), (wk_hbm, wk_ref), (wq_hbm, wq_ref), (wv_hbm, wv_ref))

    def load(m):
        return pltpu.make_async_copy(*loads[m], in_sem.at[m])

    def keep(first, end):
        for m in range(first, end):
            yield pltpu.make_async_copy(*kept[m], out_sem.at[m])

    def keys(rows):
        k_ref[rows] = (dot(ext_ref[rows], wk_ref[...]) + bias_of(bk_ref)).astype(BF)
        v_ref[rows] = (dot(ext_ref[rows], wv_ref[...]) + bias_of(bv_ref)).astype(BF)

    def turn(ref, first, size, at):
        for m in range(0, size, 128):
            xt_ref[:, at + m : at + m + 128] = ref[first + m : first + m + 128, :].astype(F32).T.astype(BF)

    def get_after():
        halo.wait(False)
        keys(slice(n + block, ext))
        turn(ext_ref, n + block, n, n + block)
        for copy in keep(3, 6):
            copy.start()

    @pl.when((qt == 0) & (pair == 0))
    def _():
        for m in range(5):
            load(m).start()
        halo.greet()
        load(0).wait()
        halo.start(True)
        load(1).wait()
        flip_ref[...] = dot(anti(2 * n), rel_ref[...]).astype(BF)
        load(2).wait()
        rk_ref[...] = (dot(flip_ref[...], wk_ref[...]) + bias_of(bk_ref)).astype(BF)
        load(3).wait()
        rq_ref[...] = (dot(flip_ref[...], wq_ref[...]) + bias_of(bq_ref)).astype(BF)
        q_ref[...] = (dot(ext_ref[own], wq_ref[...]) + bias_of(bq_ref)).astype(BF)
        for copy in keep(0, 3):
            copy.start()
        load(4).wait()
        keys(own)
        head = (lax.broadcasted_iota(jnp.int32, rq_ref.shape, 1) // 64) % 2
        for hh in range(2):
            rqm_ref[hh] = jnp.where(head == hh, rq_ref[...].astype(F32), 0.0).astype(BF)
        mask_ref[0] = jnp.where(lane > row, 1.0, 0.0).astype(BF)
        mask_ref[1] = jnp.where(lane > row, 0.0, 1.0).astype(BF)
        turn(ext_ref, n, block, n)
        turn(flip_ref, 0, 2 * n, ext)
        halo.wait(True)
        halo.start(False)
        keys(slice(0, n))
        turn(ext_ref, 0, n, 0)
        if block == n:
            get_after()

    if block > n:
        pl.when((qt == 1) & (pair == 0))(get_after)

    @pl.when(pair == 0)
    def _():
        at = lambda m: pl.ds(pl.multiple_of((qt + m) * n, n), n)
        qid = qid_ref[at(0), :]
        first, middle, third = [kid_ref[:, at(m)] for m in range(3)]
        side = ((lane > row) & (qid == first)) | ((lane < row) & (qid == third))
        bias_ref[:, 0:n] = jnp.where(side, 0.0, -1e30)
        bias_ref[:, n:] = jnp.where(qid == middle, 0.0, -1e30)

    ctx_ref[...] = fwd_tile(n, scale, pair, qt, q_ref, k_ref, v_ref, rk_ref, rqm_ref, bias_ref, mask_ref, p_ref)

    @pl.when(last)
    def _():
        halo.finish()
        for copy in keep(0, 6):
            copy.wait()


def attn_fwd(span, x, rel_table, w_query, w_key, w_value, b_query, b_key, b_value, qid, kid):
    block, width = x.shape
    ext, table = block + 2 * span, 2 * span
    scale = (3.0 * 64) ** -0.5
    heads = width // 64
    whole = lambda shape: pl.BlockSpec(shape, lambda t, h: (0,) * len(shape), pipeline_mode=pl.Buffered(1))
    far = pl.BlockSpec(memory_space=pltpu.HBM)
    small = [b_query, b_key, b_value, qid, kid]
    kept = [(rows, width) for rows in (block, ext, ext, table, table)] + [(width, ext + table)]
    more = [(ext, width), (table, width), (table, width)] + [(width, width)] * 3
    return pl.pallas_call(
        functools.partial(fwd_kernel, span, scale),
        grid=(block // span, width // 128),
        out_shape=[jax.ShapeDtypeStruct((block, width), BF), jax.ShapeDtypeStruct((heads, block, table), BF)]
        + [pltpu.HBM(shape, BF) for shape in kept],
        in_specs=[far] * 5 + [whole(arg.shape) for arg in small],
        out_specs=[pl.BlockSpec((span, 128), lambda t, h: (t, h)), pl.BlockSpec((2, span, table), lambda t, h: (h, t, 0))]
        + [far] * 6,
        scratch_shapes=[pltpu.VMEM(shape, BF) for shape in kept + more]
        + [
            pltpu.VMEM((2, table, width), BF),
            pltpu.VMEM((span, table), F32),
            pltpu.VMEM((2, span, span), BF),
            pltpu.SemaphoreType.DMA((2, 2)),
            pltpu.SemaphoreType.DMA((5,)),
            pltpu.SemaphoreType.DMA((6,)),
        ],
        compiler_params=pltpu.CompilerParams(collective_id=1, has_side_effects=True, vmem_limit_bytes=44 << 20),
        cost_estimate=pl.CostEstimate(flops=20_000_000_000, bytes_accessed=20 << 20, transcendentals=heads * block * table),
        name="attn_fwd",
    )(*[pltpu.with_memory_space_constraint(arg, pltpu.HBM) for arg in (x, rel_table, w_key, w_query, w_value)], *small)


def bwd_tile(n, scale, qt, q_ref, k_ref, v_ref, g_ref, rk_ref, rq_ref, p_ref, mask_ref, kjt_ref, dk_acc, dvt_acc, drkt_acc, drqt_acc):
    at = lambda m: pl.ds(pl.multiple_of((qt + m) * n, n), n)
    row, lane = grid_of(n)
    flip = anti(n)
    ahead, behind, above, below = [mask_ref[m] for m in range(4)]
    qb, gb = q_ref[at(0), :], g_ref[at(0), :]
    qjt = dot(qb, flip, TN).astype(BF)
    gt = gb.astype(F32).T.astype(BF)
    dqs, dks = [], []
    for hh in range(2):
        lo, hi = 64 * hh, 64 * hh + 64
        gm = head_lanes(gb, hh)
        side, middle = p_ref[hh, at(0), 0:n], p_ref[hh, at(0), n:]
        ps, pm = side.astype(F32) * scale, middle.astype(F32) * scale
        gs = jnp.where(lane > row, dot(gm, v_ref[at(0), :], NT), dot(gm, v_ref[at(2), :], NT))
        gd = dot(gm, v_ref[at(1), :], NT)
        ts, td = ps * gs, pm * gd
        total = jnp.sum(ts + td, axis=-1, keepdims=True) * (1.0 / scale)
        ds, dm = (ts - ps * total).astype(BF), (td - pm * total).astype(BF)
        for m, part in enumerate((side * ahead, middle, side * behind)):
            dvt_acc[lo:hi, at(m)] += dot(gt[lo:hi], part)

        sj, mj = dot(flip, ds), dot(flip, dm)
        right = row + lane >= n
        to_low = sheared(jnp.where(right, sj, mj), 0).astype(BF)
        to_high = sheared(jnp.where(right, mj, sj), 0).astype(BF)
        sj, mj = sj.astype(BF), mj.astype(BF)
        dq = dot(sj * above, k_ref[at(0), :]) + dot(mj, k_ref[at(1), :]) + dot(sj * below, k_ref[at(2), :])
        dqs.append(dq + dot(to_low, rk_ref[0:n]) + dot(to_high, rk_ref[n:]))
        drkt_acc[lo:hi, 0:n] += dot(qjt[lo:hi], to_low)
        drkt_acc[lo:hi, n:] += dot(qjt[lo:hi], to_high)

        st, mt = dot(flip, ds, NT), dot(flip, dm, NT)
        us, um = sheared(st, 0).astype(BF), sheared(mt, 0).astype(BF)
        st, mt = st.astype(BF), mt.astype(BF)
        high_first, low_third = us * ahead, us * behind
        low_middle, high_middle = um * ahead, um * behind
        low, high = rq_ref[0:n], rq_ref[n:]
        dks.append((
            dot(st * below, qb) + dot(high_first, high),
            dot(mt, qb) + dot(low_middle, low) + dot(high_middle, high),
            dot(st * above, qb) + dot(low_third, low),
        ))
        kjt = [kjt_ref[qt + m, lo:hi, :] for m in range(3)]
        drqt_acc[lo:hi, 0:n] += dot(kjt[1], low_middle) + dot(kjt[2], low_third)
        drqt_acc[lo:hi, n:] += dot(kjt[0], high_first) + dot(kjt[1], high_middle)
    for m in range(3):
        dk_acc[qt + m] += both_heads(dks[0][m], dks[1][m])
    return dot(flip, both_heads(*dqs).astype(BF)).astype(BF)


def bwd_masks(n, mask_ref):
    row, lane = grid_of(n)
    for m, keep in enumerate((lane >= row, lane < row, row + lane >= n, row + lane < n)):
        mask_ref[m] = jnp.where(keep, 1.0, 0.0).astype(BF)


class Mesh:
    def __init__(self, ns, nb):
        self.ns, self.nb, self.nz = ns, nb, nb // 2
        self.bits = ns.bit_length() - 1
        self.ways = 2 if ns <= 4 else 1

    def locate(self):
        self.s = lax.axis_index("seq")
        self.b = lax.axis_index("batch")
        self.z, self.c = self.b // 2, self.b % 2

    def at(self, s, b):
        return {"seq": s, "batch": b}

    def greet(self):
        barrier = pltpu.get_barrier_semaphore()
        peers = [self.at(self.s, toggled(self.b, 1))]
        peers += [self.at(self.s, toggled(self.z, step) * 2 + self.c) for step in range(1, self.nz)]
        peers += [self.at(toggled(self.s, step), self.b) for step in range(1, self.ns)]
        for peer in peers:
            pl.semaphore_signal(barrier, inc=1, device_id=peer, device_id_type=MESH)
        pl.semaphore_wait(barrier, len(peers))


class Chunk:
    def __init__(self, mesh, rows, lanes, moves, box=None, early_z=False):
        self.mesh, self.rows, self.moves, self.box, self.early_z = mesh, rows, moves, box, early_z
        unit = 128 * mesh.ways * mesh.ns
        self.lanes = -(-lanes // unit) * unit
        self.piece = self.lanes // (mesh.ways * mesh.ns)
        self.depth = 1 if early_z else mesh.nz

    def scratch(self):
        mesh, rows, lanes = self.mesh, self.rows, self.lanes
        full = pltpu.VMEM((mesh.nz, rows, lanes), BF)
        shapes = [full] if self.box else [full, full]
        for level in range(mesh.bits):
            shapes.append(pltpu.VMEM((mesh.ways, self.depth, rows, lanes // mesh.ways // 2 >> level), BF))
        wide = lanes // mesh.ways if self.early_z else self.piece
        shapes += [pltpu.VMEM((mesh.ways, mesh.nz - 1, rows, wide), BF), pltpu.VMEM((rows, lanes), BF)]
        dma = pltpu.SemaphoreType.DMA
        moves = len(self.moves)
        shapes += [] if self.box else [dma((moves,))]
        shapes += [dma((2, moves)), dma((2, 2, mesh.bits)), dma((2, 2, mesh.nz - 1)), dma((2, 2, mesh.bits))]
        return shapes

    def bind(self, refs):
        bits = self.mesh.bits
        if self.box:
            self.mine = self.box(self.mesh.c)
        else:
            self.mine, refs = refs[0], refs[1:]
        self.first = refs[0]
        self.halves = refs[1 : 1 + bits]
        self.across, self.final = refs[1 + bits : 3 + bits]
        refs = refs[3 + bits :]
        if not self.box:
            self.own_sem, refs = refs[0], refs[1:]
        self.core_sem, self.seq_sem, self.z_sem, self.out_sem = refs[:4]
        return refs[4:]

    def copy(self, src, dst, sems, index, s, b):
        return pltpu.make_async_remote_copy(
            src_ref=src,
            dst_ref=dst,
            send_sem=sems.at[(0,) + index],
            recv_sem=sems.at[(1,) + index],
            device_id=self.mesh.at(s, b),
            device_id_type=MESH,
        )

    def own_copies(self):
        for n, (source, at, size) in enumerate([] if self.box else self.moves):
            yield pltpu.make_async_copy(source(self.mesh.c), self.mine.at[:, :, pl.ds(at, size)], self.own_sem.at[n])

    def core_copies(self):
        mesh = self.mesh
        for n, (source, at, size) in enumerate(self.moves):
            yield self.copy(
                source(1 - mesh.c), self.first.at[:, :, pl.ds(at, size)], self.core_sem, (n,), mesh.s, toggled(mesh.b, 1)
            )

    def order(self, half, level):
        return (level + half) % self.mesh.bits

    def region(self, level, half):
        size = self.lanes // self.mesh.ways
        base = half * size
        sent = base
        for at in range(level):
            mine = (self.mesh.s // (1 << self.order(half, at))) % 2
            size = size // 2
            sent = base + (1 - mine) * size
            base = base + mine * size
        return base, sent, size

    def span(self, start, size):
        return pl.ds(pl.multiple_of(start, 128), size)

    def planes(self):
        return pl.ds(self.mesh.z, 1) if self.early_z else slice(None)

    def seq_copy(self, level, half):
        unused, sent, size = self.region(level + 1, half)
        return self.copy(
            self.mine.at[self.planes(), :, self.span(sent, size)],
            self.halves[level].at[half],
            self.seq_sem,
            (half, level),
            toggled(self.mesh.s, 1 << self.order(half, level)),
            self.mesh.b,
        )

    def z_region(self, half):
        kept, unused, size = self.region(0 if self.early_z else self.mesh.bits, half)
        return self.span(kept, size)

    def z_copies(self, half):
        mesh = self.mesh
        for step in range(1, mesh.nz):
            other = toggled(mesh.z, step)
            yield self.copy(
                self.mine.at[other, :, self.z_region(half)],
                self.across.at[half, step - 1],
                self.z_sem,
                (half, step - 1),
                mesh.s,
                other * 2 + mesh.c,
            )

    def out_copy(self, level, half):
        kept, unused, size = self.region(level + 1, half)
        lanes = self.span(kept, size)
        return self.copy(
            self.final.at[:, lanes],
            self.final.at[:, lanes],
            self.out_sem,
            (half, level),
            toggled(self.mesh.s, 1 << self.order(half, level)),
            self.mesh.b,
        )

    def start_core(self):
        for copy in self.core_copies():
            copy.start()
        for copy in self.own_copies():
            copy.start()

    def add_core(self):
        for copy in self.own_copies():
            copy.wait()
        for copy in self.core_copies():
            copy.wait_recv()
        parts = 4
        size = self.lanes // parts

        def add(n, carry):
            z, lanes = n // parts, self.span((n % parts) * size, size)
            self.mine[z, :, lanes] = (self.mine[z, :, lanes].astype(F32) + self.first[z, :, lanes].astype(F32)).astype(BF)
            return carry

        lax.fori_loop(0, self.mesh.nz * parts, add, 0)

    def start_seq(self, level):
        for half in range(self.mesh.ways):
            self.seq_copy(level, half).start()

    def add_seq(self, level):
        for half in range(self.mesh.ways):
            self.seq_copy(level, half).wait_recv()
            kept, unused, size = self.region(level + 1, half)
            lanes = self.span(kept, size)

            def add(n, carry):
                z = self.mesh.z if self.early_z else n
                got = self.halves[level][half, n].astype(F32)
                self.mine[z, :, lanes] = (self.mine[z, :, lanes].astype(F32) + got).astype(BF)
                return carry

            lax.fori_loop(0, self.depth, add, 0)
            if self.early_z and level == self.mesh.bits - 1:
                self.final[:, lanes] = self.mine[self.mesh.z, :, lanes]

    def end_seq(self):
        self.add_seq(1)
        for level in range(2, self.mesh.bits):
            self.start_seq(level)
            self.add_seq(level)

    def start_z(self):
        for half in range(self.mesh.ways):
            for copy in self.z_copies(half):
                copy.start()

    def add_z(self):
        z = self.mesh.z
        for half in range(self.mesh.ways):
            for copy in self.z_copies(half):
                copy.wait_recv()
            lanes = self.z_region(half)
            total = self.mine[z, :, lanes].astype(F32)
            for step in range(1, self.mesh.nz):
                total = total + self.across[half, step - 1].astype(F32)
            if self.early_z:
                self.mine[z, :, lanes] = total.astype(BF)
            else:
                self.final[:, lanes] = total.astype(BF)

    def start_out(self, level):
        for half in range(self.mesh.ways):
            self.out_copy(level, half).start()

    def core(self):
        self.start_core()

    def s0(self):
        if self.early_z:
            self.add_z()
        else:
            self.add_core()
        self.start_seq(0)

    def s1(self):
        self.add_seq(0)
        self.start_seq(1)

    def z(self):
        if self.early_z:
            self.add_core()
        else:
            self.end_seq()
        self.start_z()

    def out(self):
        if self.early_z:
            self.end_seq()
        else:
            self.add_z()
        self.start_out(self.mesh.bits - 1)

    def out2(self):
        for level in reversed(range(self.mesh.bits - 1)):
            for half in range(self.mesh.ways):
                self.out_copy(level + 1, half).wait_recv()
            self.start_out(level)

    def finish(self):
        for half in range(self.mesh.ways):
            self.out_copy(0, half).wait()
            for level in range(1, self.mesh.bits):
                self.out_copy(level, half).wait_send()
            for copy in self.z_copies(half):
                copy.wait_send()
            for level in range(self.mesh.bits):
                self.seq_copy(level, half).wait_send()
        for copy in self.core_copies():
            copy.wait_send()


class Layout:
    def __init__(self, ns, nb, width, hidden, table):
        self.mesh = mesh = Mesh(ns, nb)
        self.width, self.hidden = width, hidden
        self.rows = rows = width // nb
        self.fold = hidden // nb // rows
        self.rel_rows = table // nb
        self.pairs = width // 128
        self.third = width // 3
        self.rel_at = 384
        self.small_at = 384 + 512
        self.stack = rows // 16
        small_lanes = -(-self.pairs // self.stack) * 128
        self.split = split = hidden // 3
        whole = lambda name, lanes, early=False: self.boxed(lambda c: getattr(self, name).at[:, c], lanes, early)
        self.down = whole("down_ref", self.fold * width)
        self.into = whole("into_ref", hidden - split)
        self.rest = whole("rest_ref", split, False)
        lanes = Chunk(mesh, rows, 768 + self.third, []).lanes
        self.near = [self.boxed(lambda c, n=n: self.near_ref.at[n, :, c], lanes, n in (2,)) for n in range(3)]
        self.far = whole("far_ref", self.small_at + small_lanes)
        self.chunks = [self.down, self.into, self.rest, *self.near, self.far]

    def boxed(self, box, lanes, early=False):
        chunk = Chunk(self.mesh, self.rows, lanes, [], early_z=early)
        chunk.box, chunk.moves = box, [(box, 0, chunk.lanes)]
        return chunk

    def starts(self):
        at = 0
        for chunk in self.chunks:
            yield at
            at += chunk.lanes

    def scratch(self):
        mesh = self.mesh
        box = lambda lanes: pltpu.VMEM((mesh.nz, 2, self.rows, lanes), BF)
        shapes = [box(chunk.lanes) for chunk in (self.down, self.into, self.rest, self.far)]
        shapes.append(pltpu.VMEM((3, mesh.nz, 2, self.rows, self.near[0].lanes), BF))
        for chunk in self.chunks:
            shapes += chunk.scratch()
        return shapes

    def bind(self, refs):
        self.mesh.locate()
        self.down_ref, self.into_ref, self.rest_ref, self.far_ref, self.near_ref = refs[:5]
        refs = refs[5:]
        for chunk in self.chunks:
            refs = chunk.bind(refs)
        return refs

    def store_down(self, m, grads):
        rows, share = self.rows, self.rows * self.fold
        for n in range(self.width // rows):
            b, part = divmod(m * self.width + n * rows, share)
            lanes = slice(part // rows * self.width, (part // rows + 1) * self.width)
            self.down_ref[b // 2, b % 2, :, lanes] = grads[n * rows : (n + 1) * rows]

    def store_into(self, m, grads):
        rows, split = self.rows, self.split
        ref, lanes = (self.rest_ref, slice(0, split)) if m == 0 else (self.into_ref, slice((m - 1) * split, m * split))
        for b in range(self.mesh.nb):
            ref[b // 2, b % 2, :, lanes] = grads[b * rows : (b + 1) * rows]

    def store_out(self, grads):
        rows, third = self.rows, self.third
        for b in range(self.mesh.nb):
            for n in range(3):
                part = grads[b * rows : (b + 1) * rows, n * third : (n + 1) * third]
                self.near_ref[n, b // 2, b % 2, :, 768 : 768 + third] = part

    def store_pair(self, pair, grads):
        rows = self.rows
        box = pair // 2
        lanes = pl.ds(pl.multiple_of((pair % 2) * 384, 128), 384)

        @pl.when(pair < self.pairs - 1)
        def _():
            for b in range(self.mesh.nb):
                self.near_ref[box, b // 2, b % 2, :, lanes] = grads[b * rows : (b + 1) * rows]

        @pl.when(pair == self.pairs - 1)
        def _():
            for b in range(self.mesh.nb):
                self.far_ref[b // 2, b % 2, :, 0:384] = grads[b * rows : (b + 1) * rows]

    def store_rest(self, rel, vectors):
        take, at, half = self.rel_rows, self.rel_at, self.rel_rows // 2
        for b in range(self.mesh.nb):
            part = rel[b * take : (b + 1) * take]
            put = self.far_ref.at[b // 2, b % 2]
            put[0:take, at : at + 512] = part[:, 0:512]
            put[take : take + half, at : at + 256] = part[0:half, 512:768]
            put[take : take + half, at + 256 : at + 512] = part[half:, 512:768]
            for n in range(self.pairs):
                row, lane = (n % self.stack) * 16, self.small_at + (n // self.stack) * 128
                put[row : row + 16, lane : lane + 128] = vectors[:, n * 128 : (n + 1) * 128]

    def schedule(self):
        down, into, rest, one, two, three, far = self.chunks

        steps = {
            1: [rest.s0],
            2: [into.s0],
            3: [down.s0],
            7: [one.core],
            8: [into.s1],
            9: [down.s1, rest.s1],
            11: [into.z],
            12: [one.s0, two.core],
            13: [rest.z, two.s0],
            14: [down.z, into.out, one.s1],
            15: [two.s1],
            16: [into.out2, rest.out, three.core, one.z],
            17: [two.z],
        }
        last = [
            far.core,
            three.z,
            far.s0,
            down.out,
            two.out,
            far.s1,
            one.out,
            three.s0,
            down.out2,
            far.z,
            three.s1,
            two.out2,
            one.out2,
            three.out,
            far.out,
            rest.out2,
            three.out2,
            far.out2,
        ]
        last += [chunk.finish for chunk in self.chunks]
        return steps, last


class Edges:
    def __init__(self, mesh, refs):
        self.mesh = mesh
        self.sent, self.got, self.sems = refs

    def copy(self, side):
        other = self.mesh.s + (2 * side - 1)
        return pltpu.make_async_remote_copy(
            src_ref=self.sent.at[side],
            dst_ref=self.got.at[1 - side],
            send_sem=self.sems.at[0, side],
            recv_sem=self.sems.at[1, 1 - side],
            device_id=self.mesh.at(other, self.mesh.b),
            device_id_type=MESH,
        )

    def has(self, side):
        return self.mesh.s > 0 if side == 0 else self.mesh.s < self.mesh.ns - 1

    def start(self):
        for side in range(2):
            pl.when(self.has(side))(lambda side=side: self.copy(side).start())

    def finish(self, add):
        for side in range(2):

            @pl.when(self.has(side))
            def _(side=side):
                self.copy(side).wait_send()
                self.copy(1 - side).wait_recv()
                add(side, self.got[side])


def bwd_kernel(tq, scale, layout, q_ref, k_ref, v_ref, g_ref, rk_ref, rq_ref, p_ref, wk_ref, wq_ref, wv_ref,
               act_hbm, branch_ref, hidden_ref, pre_hbm, ctx_hbm, attn_hbm, g_one_hbm, xt_hbm, picks_ref, *rest):
    small_refs, rest = rest[:7], rest[7:]
    (dx_ref, packed_hbm,
               mask_ref, kjt_ref, dk_acc, dvt_acc, drkt_acc, drqt_acc,
               xt_ref, d_ref, rel_acc, vec_ref, dx_acc, sent_ref, got_ref, edge_sem,
     load_ref, load_sem, side_sem, packed_sem, *refs) = rest
    block = q_ref.shape[0]
    nq = block // tq
    ext = k_ref.shape[0]
    nk = ext // tq
    span = tq
    table = 2 * span
    pair = pl.program_id(0)
    pairs = layout.pairs
    flip = anti(tq)
    layout.bind(refs)
    edges = Edges(layout.mesh, (sent_ref, got_ref, edge_sem))
    steps, last = layout.schedule()

    def run(actions):
        def all_of():
            for action in actions:
                action()
        return all_of

    loads = [act_hbm.at[:, pl.ds(m * layout.width, layout.width)] for m in range(layout.fold)]
    loads += [pre_hbm.at[:, pl.ds(m * layout.split, layout.split)] for m in range(3)]
    loads += [ctx_hbm, attn_hbm]

    def load(m):
        size = loads[m].shape
        return pltpu.make_async_copy(loads[m], load_ref.at[m % 3, pl.ds(0, size[0]), pl.ds(0, size[1])], load_sem.at[m % 3])

    def loaded(m):
        size = loads[m].shape
        load(m).wait()
        return load_ref[m % 3, 0 : size[0], 0 : size[1]]

    def dx_copy():
        return pltpu.make_async_copy(g_one_hbm, dx_ref, side_sem.at[0])

    def xt_copy():
        return pltpu.make_async_copy(xt_hbm, xt_ref, side_sem.at[1])

    @pl.when(pair == 0)
    def _():
        for m in range(2):
            load(m).start()
        layout.mesh.greet()
        m = 0
        for n in range(layout.fold):
            load(m + 2).start()
            layout.store_down(n, dot(loaded(m), branch_ref[...], TN).astype(BF))
            m += 1
        layout.down.core()
        for n in range(3):
            if m + 2 < len(loads):
                load(m + 2).start()
            layout.store_into(n, dot(hidden_ref[...], loaded(m), TN).astype(BF))
            if n == 0:
                layout.rest.core()
            m += 1
        xt_copy().start()
        dx_copy().start()
        layout.into.core()
        run(steps.get(0, []))()
        layout.store_out(dot(loaded(m), loaded(m + 1), TN).astype(BF))
        bwd_masks(tq, mask_ref)
        d_ref[...] = jnp.zeros_like(d_ref)
        rel_acc[...] = jnp.zeros_like(rel_acc)
        dx_acc[...] = jnp.zeros_like(dx_acc)
        vec_ref[...] = jnp.zeros_like(vec_ref)
        for n, ref in enumerate(small_refs[:6]):
            vec_ref[n : n + 1, :] = ref[...][None]
        for n in range(layout.fold):
            vec_ref[6 + n : 7 + n, :] = small_refs[6][n * layout.width : (n + 1) * layout.width][None]

    for kt in range(nk):
        kjt_ref[kt] = dot(k_ref[kt * tq : (kt + 1) * tq, :], flip, TN).astype(BF)
    dk_acc[...] = jnp.zeros_like(dk_acc)
    dvt_acc[...] = jnp.zeros_like(dvt_acc)
    drkt_acc[...] = jnp.zeros_like(drkt_acc)
    drqt_acc[...] = jnp.zeros_like(drqt_acc)

    def tile(qt, carry):
        for step, actions in steps.items():
            if step and step % 3 < min(nq, 2):
                pl.when((pair == step // 3) & (qt == step % 3))(run(actions))
        row = pl.multiple_of(qt * tq, tq)
        dq = bwd_tile(
            tq, scale, qt, q_ref, k_ref, v_ref, g_ref, rk_ref, rq_ref, p_ref, mask_ref, kjt_ref, dk_acc, dvt_acc, drkt_acc, drqt_acc
        )
        d_ref[pl.ds(span + row, tq), 0:128] = dq
        return carry

    lax.fori_loop(0, nq, tile, 0)
    for step, actions in steps.items():
        if step % 3 >= min(nq, 2):
            pl.when(pair == step // 3)(run(actions))
    for kt in range(nk):
        here = slice(kt * tq, (kt + 1) * tq)
        dk = dot(flip, dk_acc[kt].astype(BF)).astype(BF)
        dv = dvt_acc[:, here].T.astype(BF)
        d_ref[here, 128:256] = dk
        d_ref[here, 256:384] = dv
    for st in range(table // 128):
        here = slice(ext + st * 128, ext + (st + 1) * 128)
        d_ref[here, 0:128] = drqt_acc[:, st * 128 : (st + 1) * 128].T.astype(BF)
        d_ref[here, 128:256] = drkt_acc[:, st * 128 : (st + 1) * 128].T.astype(BF)

    weights = jnp.concatenate([wq_ref[...], wk_ref[...], wv_ref[...]], axis=1)
    dx_acc[...] += dot(d_ref[0:ext], weights, NT)

    @pl.when(pair == pairs - 1)
    def _():
        sent_ref[0] = dx_acc[0:span].astype(BF)
        sent_ref[1] = dx_acc[ext - span :].astype(BF)
        edges.start()

    pl.when(pair == 0)(lambda: xt_copy().wait())
    grads = dot(xt_ref[...], d_ref[...]).astype(BF)
    layout.store_pair(pair, grads)
    rel_acc[...] += dot(d_ref[ext:, 0:128], wq_ref[...], NT) + dot(d_ref[ext:, 128:256], wk_ref[...], NT)
    sums = dot(jnp.ones((8, ext + table), BF), d_ref[...])[0:1]
    for n in range(3):
        vec_ref[10 + n : 11 + n, pl.ds(pl.multiple_of(pair * 128, 128), 128)] = sums[:, n * 128 : (n + 1) * 128]

    @pl.when(pair == pairs - 1)
    def _():
        rel = dot(picks_ref[...], rel_acc[...].astype(BF)).astype(BF)
        layout.store_rest(rel, vec_ref[...].astype(BF))
        run(last[:1])()
        dx_copy().wait()
        dx_ref[...] += dx_acc[span : span + block]
        run(last[1:])()

        packed_copies = []
        for n, (at, chunk) in enumerate(zip(layout.starts(), layout.chunks)):
            packed_copies.append(pltpu.make_async_copy(chunk.final, packed_hbm.at[:, pl.ds(at, chunk.lanes)], packed_sem.at[n]))
            packed_copies[-1].start()

        def take(side, rows):
            here = slice(0, span) if side == 0 else slice(block - span, block)
            dx_ref[here] += rows.astype(F32)

        edges.finish(take)
        for copy in packed_copies:
            copy.wait()


def attn_bwd(span, q, k, v, g, rk, rq, probs, w_key, w_query, w_value, act, branch, hidden, pre, context, g_attn, g_one, xt, picks, small):
    block, width = q.shape
    ext = k.shape[0]
    table = 2 * span
    scale = (3.0 * 64) ** -0.5
    ns, nb = lax.axis_size("seq"), lax.axis_size("batch")
    layout = Layout(ns, nb, width, act.shape[1], table)
    col = lambda rows: pl.BlockSpec((rows, 128), lambda h: (0, h))
    whole = lambda shape: pl.BlockSpec(shape, lambda h: (0, 0), pipeline_mode=pl.Buffered(1))
    any_spec = pl.BlockSpec(memory_space=pltpu.HBM)
    packed = jax.ShapeDtypeStruct((layout.rows, sum(chunk.lanes for chunk in layout.chunks)), BF)
    outs = pl.pallas_call(
        functools.partial(bwd_kernel, span, scale, layout),
        grid=(width // 128,),
        out_shape=(
            jax.ShapeDtypeStruct((block, width), F32),
            packed,
        ),
        in_specs=[col(block), col(ext), col(ext), col(block), col(rk.shape[0]), col(rq.shape[0]),
                  pl.BlockSpec((2, block, table), lambda h: (h, 0, 0)), col(width), col(width), col(width),
                  any_spec, whole(branch.shape), whole(hidden.shape), any_spec, any_spec, any_spec, any_spec, any_spec,
                  whole(picks.shape)] + [pl.BlockSpec(part.shape, lambda h: (0,)) for part in small],
        out_specs=(whole((block, width)), any_spec),
        scratch_shapes=[
            pltpu.VMEM((4, span, span), BF),
            pltpu.VMEM((ext // span, 128, span), BF),
            pltpu.VMEM((ext // span, span, 128), F32),
            pltpu.VMEM((128, ext), F32),
            pltpu.VMEM((128, table), F32),
            pltpu.VMEM((128, table), F32),
            pltpu.VMEM((width, ext + table), BF),
            pltpu.VMEM((ext + table, 384), BF),
            pltpu.VMEM((table, width), F32),
            pltpu.VMEM((16, width), F32),
            pltpu.VMEM((ext, width), F32),
            pltpu.VMEM((2, span, width), BF),
            pltpu.VMEM((2, span, width), BF),
            pltpu.SemaphoreType.DMA((2, 2)),
            pltpu.VMEM((3, block, layout.split), BF),
            pltpu.SemaphoreType.DMA((3,)),
            pltpu.SemaphoreType.DMA((2,)),
            pltpu.SemaphoreType.DMA((len(layout.chunks),)),
        ] + layout.scratch(),
        compiler_params=pltpu.CompilerParams(collective_id=0, has_side_effects=True, vmem_limit_bytes=60 << 20),
        cost_estimate=pl.CostEstimate(flops=50_000_000_000, bytes_accessed=20 << 20, transcendentals=0),
        name="attn_bwd_reduce",
    )(*[pltpu.with_memory_space_constraint(arg, pltpu.HBM) for arg in (q, k, v)], g, *[pltpu.with_memory_space_constraint(arg, pltpu.HBM) for arg in (rk, rq, probs)], w_key, w_query, w_value, act, branch, hidden, pre, context, g_attn, g_one, pltpu.with_memory_space_constraint(xt, pltpu.HBM), picks, *small)
    return layout, outs


def unpack_kernel(layout, packed_hbm, dx_hbm,
                  dx_out, down_out, into_out, out_out, query_out, key_out, value_out, rel_out, *refs):
    vec_outs, wide_out, (packed_ref, rel_ref, vec_ref, sems) = refs[:-5], refs[-5], refs[-4:]
    packed_copy = pltpu.make_async_copy(packed_hbm, packed_ref, sems.at[0])
    dx_copy = pltpu.make_async_copy(dx_hbm, dx_out, sems.at[1])
    packed_copy.start()
    dx_copy.start()
    packed_copy.wait()
    rows, width, pairs = layout.rows, layout.width, layout.pairs
    parts = [packed_ref.at[:, at : at + chunk.lanes] for at, chunk in zip(layout.starts(), layout.chunks)]
    down_ref, into_ref, rest_ref, *near, far_ref = parts
    split = layout.hidden // 3
    into_out[:, :split] = rest_ref[:, :split].astype(F32)
    into_out[:, split:] = into_ref[:, : layout.hidden - split].astype(F32)
    for n in range(layout.fold):
        down_out[n * rows : (n + 1) * rows, :] = down_ref[:, n * width : (n + 1) * width].astype(F32)
    for n, side in enumerate(near):
        out_out[:, n * layout.third : (n + 1) * layout.third] = side[:, 768 : 768 + layout.third].astype(F32)
    for m in range(pairs):
        side, at = (far_ref, 0) if m == pairs - 1 else (near[m // 2], m % 2 * 384)
        for n, out in enumerate((query_out, key_out, value_out)):
            out[:, m * 128 : (m + 1) * 128] = side[:, at + n * 128 : at + (n + 1) * 128].astype(F32)
    take, at, half = layout.rel_rows, layout.rel_at, layout.rel_rows // 2
    rel_ref[:, 0:512] = far_ref[0:take, at : at + 512].astype(F32)
    for n in range(2):
        rel_ref[n * half : (n + 1) * half, 512:768] = far_ref[take : take + half, at + n * 256 : at + (n + 1) * 256].astype(F32)
    own = take // layout.mesh.ns
    rel_out[...] = pltpu.roll(rel_ref[...], take - lax.axis_index("seq") * own, 0)[:own]
    for n in range(pairs):
        row, lane = (n % layout.stack) * 16, layout.small_at + (n // layout.stack) * 128
        vec_ref[:, n * 128 : (n + 1) * 128] = far_ref[row : row + 16, lane : lane + 128].astype(F32)
    b = lax.axis_index("batch")
    mine = pltpu.roll(vec_ref[...], width - b * rows, 1)
    for out, n in zip(vec_outs, (0, 1, 2, 3, 4, 5, 10, 11, 12)):
        out[...] = mine[n, :rows]
    wide = wide_out.shape[0]
    fit = width // wide
    line = pltpu.roll(pltpu.roll(vec_ref[...], width - (b % fit) * wide, 1), 10 - b // fit, 0)
    wide_out[...] = line[0, :wide]
    dx_copy.wait()


def unpack(layout, packed, dx):
    rows, width = layout.rows, layout.width
    shape = lambda *dims: jax.ShapeDtypeStruct(dims, F32)
    shapes = [shape(*dx.shape), shape(layout.fold * rows, width), shape(rows, layout.hidden)] + [shape(rows, width)] * 4
    shapes += [shape(layout.rel_rows // layout.mesh.ns, width)] + [shape(rows)] * 9 + [shape(layout.fold * rows)]
    vmem, far = pl.BlockSpec(memory_space=pltpu.VMEM), pl.BlockSpec(memory_space=pltpu.HBM)
    return pl.pallas_call(
        functools.partial(unpack_kernel, layout),
        out_shape=shapes,
        in_specs=[far, far],
        out_specs=[vmem] * len(shapes),
        scratch_shapes=[
            pltpu.VMEM(packed.shape, BF),
            pltpu.VMEM((layout.rel_rows, width), F32),
            pltpu.VMEM((16, width), F32),
            pltpu.SemaphoreType.DMA((2,)),
        ],
        compiler_params=pltpu.CompilerParams(vmem_limit_bytes=32 << 20),
        name="unpack",
    )(*[pltpu.with_memory_space_constraint(arg, pltpu.HBM) for arg in (packed, dx)])


NORM_EPS = 1e-07


def norm_rows(values):
    centred = values - jnp.mean(values, axis=-1, keepdims=True)
    inv_std = lax.rsqrt(jnp.mean(centred * centred, axis=-1, keepdims=True) + NORM_EPS)
    return centred * inv_std, inv_std


def norm_back(grads, normed, inv_std):
    first_mean = jnp.mean(grads, axis=-1, keepdims=True)
    second_mean = jnp.mean(grads * normed, axis=-1, keepdims=True)
    return inv_std * (grads - first_mean - normed * second_mean)


def local(
    layer_input,
    w_query,
    b_query,
    w_key,
    b_key,
    w_value,
    b_value,
    w_out,
    b_out,
    gain_attn,
    shift_attn,
    w_in,
    b_in,
    w_down,
    b_down,
    gain_ffn,
    shift_ffn,
    rel_table,
    segment_ids,
    cotangent,
):
    rows, block, width = layer_input.shape
    span = rel_table.shape[0] // 2
    x = layer_input[0]
    start = lax.axis_index("seq") * block
    padded = jnp.pad(segment_ids[0], (span, span), constant_values=-1)
    kid = lax.dynamic_slice_in_dim(padded, start, block + 2 * span, 0)
    qid = kid[span : span + block]
    context, probs, q, k, v, rk, rq, xt = attn_fwd(
        span, x, rel_table, w_query, w_key, w_value, b_query, b_key, b_value, qid[:, None], kid[None]
    )

    residual_one = x.astype(F32) + dot(context, w_out) + b_out
    normed_one, inv_one = norm_rows(residual_one)
    hidden = normed_one * gain_attn + shift_attn
    hidden_low = hidden.astype(BF)
    pre_act = dot(hidden_low, w_in) + b_in
    phi = 0.5 * (1.0 + lax.erf(pre_act * (0.5**0.5)))
    act_low = (pre_act * phi).astype(BF)
    slope = phi + pre_act * (jnp.exp(-0.5 * pre_act * pre_act) * ((2.0 * math.pi) ** -0.5))
    residual_two = hidden + dot(act_low, w_down) + b_down
    normed_two, inv_two = norm_rows(residual_two)
    output = (normed_two * gain_ffn + shift_ffn).astype(BF)

    grad_out = cotangent[0].astype(F32)
    gain_ffn_grad = jnp.sum(grad_out * normed_two, axis=0)
    shift_ffn_grad = jnp.sum(grad_out, axis=0)
    grad_two = norm_back(grad_out * gain_ffn, normed_two, inv_two)
    grad_branch = grad_two.astype(BF)
    down_bias_grad = jnp.sum(grad_branch.astype(F32), axis=0)
    grad_pre = (dot(grad_branch, w_down, NT) * slope).astype(BF)
    in_bias_grad = jnp.sum(grad_pre.astype(F32), axis=0)
    grad_hidden = grad_two + dot(grad_pre, w_in, NT)
    gain_attn_grad = jnp.sum(grad_hidden * normed_one, axis=0)
    shift_attn_grad = jnp.sum(grad_hidden, axis=0)
    grad_one = norm_back(grad_hidden * gain_attn, normed_one, inv_one)
    grad_attn = grad_one.astype(BF)
    out_bias_grad = jnp.sum(grad_attn.astype(F32), axis=0)
    grad_context = dot(grad_attn, w_out, NT).astype(BF)

    share, lanes = lax.axis_size("batch"), lax.axis_size("seq")
    rel_rows = 2 * span // (share * lanes)
    order = np.arange(2 * span).reshape(lanes, share, rel_rows).transpose(1, 0, 2).reshape(-1)
    picks = jnp.asarray((2 * span - 1 - order)[:, None] == np.arange(2 * span)[None], BF)
    small = [out_bias_grad, gain_attn_grad, shift_attn_grad, down_bias_grad, gain_ffn_grad, shift_ffn_grad, in_bias_grad]
    layout, outs = attn_bwd(
        span, q, k, v, grad_context, rk, rq, probs, w_key, w_query, w_value, act_low, grad_branch, hidden_low, grad_pre,
        context, grad_attn, grad_one, xt, picks, small,
    )
    input_grad, packed = outs
    input_grad, down_sum, in_sum, out_sum, query_sum, key_sum, value_sum, rel_sum, *vectors = unpack(layout, packed, input_grad)
    ob, ga, sa, db, gf, sf, qb, kb, vb, ib = vectors
    return (
        output[None], input_grad[None], query_sum, qb, key_sum, kb, value_sum, vb, out_sum, ob,
        ga, sa, in_sum, ib, down_sum, db, gf, sf, rel_sum,
    )


def solution(mesh):
    tokens = P("batch", "seq", None)
    in_specs = (tokens,) + (P(),) * 17 + (P("batch", None), tokens)
    matrix, vector = P("batch", None), P("batch")
    out_specs = (
        (tokens, tokens)
        + (matrix, vector) * 4
        + (vector, vector)
        + (matrix, vector) * 2
        + (vector, vector, P(("seq", "batch"), None))
    )
    return jax.shard_map(local, mesh=mesh, in_specs=in_specs, out_specs=out_specs, check_vma=False)
```

```python
import functools
import math

import jax
import jax.numpy as jnp
import numpy as np
from jax import lax
from jax.experimental import pallas as pl
from jax.experimental.pallas import tpu as pltpu
from jax.sharding import PartitionSpec as P

F32 = jnp.float32
BF = jnp.bfloat16
NN = (((1,), (0,)), ((), ()))
NT = (((1,), (1,)), ((), ()))
TN = (((0,), (0,)), ((), ()))
MESH = pl.DeviceIdType.MESH


def toggled(value, mask):
    out = value
    for bit in range(mask.bit_length()):
        if mask >> bit & 1:
            out = out + (1 - 2 * ((value // (1 << bit)) % 2)) * (1 << bit)
    return out


def dot(a, b, dims=NN):
    return lax.dot_general(a, b, dims, preferred_element_type=F32)


def head_lanes(x, hh):
    lane = lax.broadcasted_iota(jnp.int32, x.shape, len(x.shape) - 1)
    keep = (lane < 64) if hh == 0 else (lane >= 64)
    return jnp.where(keep, x.astype(F32), 0.0).astype(x.dtype)


def both_heads(first, second):
    lane = lax.broadcasted_iota(jnp.int32, first.shape, 1)
    return jnp.where(lane < 64, first, second)


def grid_of(n):
    return lax.broadcasted_iota(jnp.int32, (n, n), 0), lax.broadcasted_iota(jnp.int32, (n, n), 1)


def anti(n):
    row, lane = grid_of(n)
    return jnp.where(row + lane == n - 1, 1.0, 0.0).astype(BF)


def sheared(x, shift):
    return pltpu.roll(x, shift, 1, stride=1, stride_axis=0)


def fwd_tile(n, scale, pair, qt, q_ref, k_ref, v_ref, rk_ref, rqm_ref, bias_ref, mask_ref, p_ref):
    factor = scale * math.log2(math.e)
    row, lane = grid_of(n)
    right, upper = lane > row, row + lane >= n - 1
    lanes = pl.ds(pl.multiple_of(pair * 128, 128), 128)
    at = lambda m: (pl.ds(pl.multiple_of((qt + m) * n, n), n), lanes)
    qb = q_ref[at(0)]
    rk_low, rk_high = rk_ref[0:n, lanes], rk_ref[n:, lanes]
    outs = []
    for hh in range(2):
        qm = head_lanes(qb, hh)
        low, high = rqm_ref[hh, 0:n, lanes], rqm_ref[hh, n:, lanes]
        to_low = sheared(dot(qm, rk_low, NT), 1)
        to_high = sheared(dot(qm, rk_high, NT), 1)
        side = jnp.where(right, dot(qm, k_ref[at(0)], NT) + to_low, dot(qm, k_ref[at(2)], NT) + to_high)
        middle = dot(qm, k_ref[at(1)], NT) + jnp.where(right, to_high, to_low)
        key_side = jnp.where(upper, dot(k_ref[at(0)], high, NT), dot(k_ref[at(2)], low, NT))
        key_middle = jnp.where(upper, dot(k_ref[at(1)], low, NT), dot(k_ref[at(1)], high, NT))
        side = (side + sheared(key_side, 1).T) * factor + bias_ref[:, 0:n]
        middle = (middle + sheared(key_middle, 1).T) * factor + bias_ref[:, n:]
        top = jnp.max(jnp.maximum(side, middle), axis=-1, keepdims=True)
        side, middle = jnp.exp2(side - top), jnp.exp2(middle - top)
        inverse = 1.0 / jnp.sum(side + middle, axis=-1, keepdims=True)
        side, middle = (side * inverse).astype(BF), (middle * inverse).astype(BF)
        p_ref[hh, :, 0:n] = side
        p_ref[hh, :, n:] = middle
        out = dot(side * mask_ref[0], v_ref[at(0)]) + dot(middle, v_ref[at(1)])
        outs.append(out + dot(side * mask_ref[1], v_ref[at(2)]))
    return both_heads(*outs).astype(BF)


class Halo:
    def __init__(self, span, block, ext_ref, sems):
        self.span, self.block, self.ext_ref, self.sems = span, block, ext_ref, sems
        self.s, self.b, self.ns = lax.axis_index("seq"), lax.axis_index("batch"), lax.axis_size("seq")

    def greet(self):
        barrier = pltpu.get_barrier_semaphore()
        for step in range(1, self.ns):
            peer = {"seq": toggled(self.s, step), "batch": self.b}
            pl.semaphore_signal(barrier, inc=1, device_id=peer, device_id_type=MESH)
        pl.semaphore_wait(barrier, self.ns - 1)

    def copy(self, up):
        span, block = self.span, self.block
        src, dst = (block, 0) if up else (span, span + block)
        return pltpu.make_async_remote_copy(
            src_ref=self.ext_ref.at[pl.ds(src, span)],
            dst_ref=self.ext_ref.at[pl.ds(dst, span)],
            send_sem=self.sems.at[0, int(up)],
            recv_sem=self.sems.at[1, int(up)],
            device_id={"seq": self.s + (1 if up else -1), "batch": self.b},
            device_id_type=MESH,
        )

    def sends(self, up):
        return self.s < self.ns - 1 if up else self.s > 0

    def gets(self, up):
        return self.s > 0 if up else self.s < self.ns - 1

    def start(self, up):
        pl.when(self.sends(up))(lambda: self.copy(up).start())

    def wait(self, up):
        at = pl.ds(0 if up else self.span + self.block, self.span)
        pl.when(self.gets(up))(lambda: self.copy(up).wait_recv())

        @pl.when(jnp.logical_not(self.gets(up)))
        def _():
            self.ext_ref[at] = jnp.zeros((self.span, self.ext_ref.shape[1]), BF)

    def finish(self):
        for up in (True, False):
            pl.when(self.sends(up))(lambda up=up: self.copy(up).wait_send())


def fwd_kernel(n, scale, x_hbm, rel_hbm, wk_hbm, wq_hbm, wv_hbm, bq_ref, bk_ref, bv_ref, qid_ref, kid_ref,
               ctx_ref, p_ref, q_out, k_out, v_out, rk_out, rq_out, xt_out,
               q_ref, k_ref, v_ref, rk_ref, rq_ref, xt_ref, ext_ref, rel_ref, flip_ref, wk_ref, wq_ref, wv_ref,
               rqm_ref, bias_ref, mask_ref, halo_sem, in_sem, out_sem):
    block = x_hbm.shape[0]
    ext = block + 2 * n
    qt, pair = pl.program_id(0), pl.program_id(1)
    last = (qt == pl.num_programs(0) - 1) & (pair == pl.num_programs(1) - 1)
    halo = Halo(n, block, ext_ref, halo_sem)
    row, lane = grid_of(n)
    bias_of = lambda ref: ref[...].astype(F32)[None]
    own = slice(n, n + block)
    kept = ((q_ref, q_out), (rk_ref, rk_out), (rq_ref, rq_out), (k_ref, k_out), (v_ref, v_out), (xt_ref, xt_out))
    loads = ((x_hbm, ext_ref.at[pl.ds(n, block)]), (rel_hbm, rel_ref), (wk_hbm, wk_ref), (wq_hbm, wq_ref), (wv_hbm, wv_ref))

    def load(m):
        return pltpu.make_async_copy(*loads[m], in_sem.at[m])

    def keep(first, end):
        for m in range(first, end):
            yield pltpu.make_async_copy(*kept[m], out_sem.at[m])

    def keys(rows):
        k_ref[rows] = (dot(ext_ref[rows], wk_ref[...]) + bias_of(bk_ref)).astype(BF)
        v_ref[rows] = (dot(ext_ref[rows], wv_ref[...]) + bias_of(bv_ref)).astype(BF)

    def turn(ref, first, size, at):
        for m in range(0, size, 128):
            xt_ref[:, at + m : at + m + 128] = ref[first + m : first + m + 128, :].astype(F32).T.astype(BF)

    def get_after():
        halo.wait(False)
        keys(slice(n + block, ext))
        turn(ext_ref, n + block, n, n + block)
        for copy in keep(3, 6):
            copy.start()

    @pl.when((qt == 0) & (pair == 0))
    def _():
        for m in range(5):
            load(m).start()
        halo.greet()
        load(0).wait()
        halo.start(True)
        load(1).wait()
        flip_ref[...] = dot(anti(2 * n), rel_ref[...]).astype(BF)
        load(2).wait()
        rk_ref[...] = (dot(flip_ref[...], wk_ref[...]) + bias_of(bk_ref)).astype(BF)
        load(3).wait()
        rq_ref[...] = (dot(flip_ref[...], wq_ref[...]) + bias_of(bq_ref)).astype(BF)
        q_ref[...] = (dot(ext_ref[own], wq_ref[...]) + bias_of(bq_ref)).astype(BF)
        for copy in keep(0, 3):
            copy.start()
        load(4).wait()
        keys(own)
        head = (lax.broadcasted_iota(jnp.int32, rq_ref.shape, 1) // 64) % 2
        for hh in range(2):
            rqm_ref[hh] = jnp.where(head == hh, rq_ref[...].astype(F32), 0.0).astype(BF)
        mask_ref[0] = jnp.where(lane > row, 1.0, 0.0).astype(BF)
        mask_ref[1] = jnp.where(lane > row, 0.0, 1.0).astype(BF)
        turn(ext_ref, n, block, n)
        turn(flip_ref, 0, 2 * n, ext)
        halo.wait(True)
        halo.start(False)
        keys(slice(0, n))
        turn(ext_ref, 0, n, 0)
        if block == n:
            get_after()

    if block > n:
        pl.when((qt == 1) & (pair == 0))(get_after)

    @pl.when(pair == 0)
    def _():
        at = lambda m: pl.ds(pl.multiple_of((qt + m) * n, n), n)
        qid = qid_ref[at(0), :]
        first, middle, third = [kid_ref[:, at(m)] for m in range(3)]
        side = ((lane > row) & (qid == first)) | ((lane < row) & (qid == third))
        bias_ref[:, 0:n] = jnp.where(side, 0.0, -1e30)
        bias_ref[:, n:] = jnp.where(qid == middle, 0.0, -1e30)

    ctx_ref[...] = fwd_tile(n, scale, pair, qt, q_ref, k_ref, v_ref, rk_ref, rqm_ref, bias_ref, mask_ref, p_ref)

    @pl.when(last)
    def _():
        halo.finish()
        for copy in keep(0, 6):
            copy.wait()


def attn_fwd(span, x, rel_table, w_query, w_key, w_value, b_query, b_key, b_value, qid, kid):
    block, width = x.shape
    ext, table = block + 2 * span, 2 * span
    scale = (3.0 * 64) ** -0.5
    heads = width // 64
    whole = lambda shape: pl.BlockSpec(shape, lambda t, h: (0,) * len(shape), pipeline_mode=pl.Buffered(1))
    far = pl.BlockSpec(memory_space=pltpu.HBM)
    small = [b_query, b_key, b_value, qid, kid]
    kept = [(rows, width) for rows in (block, ext, ext, table, table)] + [(width, ext + table)]
    more = [(ext, width), (table, width), (table, width)] + [(width, width)] * 3
    return pl.pallas_call(
        functools.partial(fwd_kernel, span, scale),
        grid=(block // span, width // 128),
        out_shape=[pltpu.HBM((block, width), BF), pltpu.HBM((heads, block, table), BF)]
        + [pltpu.HBM(shape, BF) for shape in kept],
        in_specs=[far] * 5 + [whole(arg.shape) for arg in small],
        out_specs=[pl.BlockSpec((span, 128), lambda t, h: (t, h)), pl.BlockSpec((2, span, table), lambda t, h: (h, t, 0))]
        + [far] * 6,
        scratch_shapes=[pltpu.VMEM(shape, BF) for shape in kept + more]
        + [
            pltpu.VMEM((2, table, width), BF),
            pltpu.VMEM((span, table), F32),
            pltpu.VMEM((2, span, span), BF),
            pltpu.SemaphoreType.DMA((2, 2)),
            pltpu.SemaphoreType.DMA((5,)),
            pltpu.SemaphoreType.DMA((6,)),
        ],
        compiler_params=pltpu.CompilerParams(collective_id=1, has_side_effects=True, vmem_limit_bytes=44 << 20),
        cost_estimate=pl.CostEstimate(flops=20_000_000_000, bytes_accessed=20 << 20, transcendentals=heads * block * table),
        name="attn_fwd",
    )(*[pltpu.with_memory_space_constraint(arg, pltpu.HBM) for arg in (x, rel_table, w_key, w_query, w_value)], *small)


def bwd_tile(n, scale, qt, q_ref, k_ref, v_ref, g_ref, rk_ref, rq_ref, p_ref, mask_ref, kjt_ref, dk_acc, dvt_acc, drkt_acc, drqt_acc):
    at = lambda m: pl.ds(pl.multiple_of((qt + m) * n, n), n)
    row, lane = grid_of(n)
    flip = anti(n)
    ahead, behind, above, below = [mask_ref[m] for m in range(4)]
    qb, gb = q_ref[at(0), :], g_ref[at(0), :]
    qjt = dot(qb, flip, TN).astype(BF)
    gt = gb.astype(F32).T.astype(BF)
    dqs, dks = [], []
    for hh in range(2):
        lo, hi = 64 * hh, 64 * hh + 64
        gm = head_lanes(gb, hh)
        side, middle = p_ref[hh, at(0), 0:n], p_ref[hh, at(0), n:]
        ps, pm = side.astype(F32) * scale, middle.astype(F32) * scale
        gs = jnp.where(lane > row, dot(gm, v_ref[at(0), :], NT), dot(gm, v_ref[at(2), :], NT))
        gd = dot(gm, v_ref[at(1), :], NT)
        ts, td = ps * gs, pm * gd
        total = jnp.sum(ts + td, axis=-1, keepdims=True) * (1.0 / scale)
        ds, dm = (ts - ps * total).astype(BF), (td - pm * total).astype(BF)
        for m, part in enumerate((side * ahead, middle, side * behind)):
            dvt_acc[lo:hi, at(m)] += dot(gt[lo:hi], part)

        sj, mj = dot(flip, ds), dot(flip, dm)
        right = row + lane >= n
        to_low = sheared(jnp.where(right, sj, mj), 0).astype(BF)
        to_high = sheared(jnp.where(right, mj, sj), 0).astype(BF)
        sj, mj = sj.astype(BF), mj.astype(BF)
        dq = dot(sj * above, k_ref[at(0), :]) + dot(mj, k_ref[at(1), :]) + dot(sj * below, k_ref[at(2), :])
        dqs.append(dq + dot(to_low, rk_ref[0:n]) + dot(to_high, rk_ref[n:]))
        drkt_acc[lo:hi, 0:n] += dot(qjt[lo:hi], to_low)
        drkt_acc[lo:hi, n:] += dot(qjt[lo:hi], to_high)

        st, mt = dot(flip, ds, NT), dot(flip, dm, NT)
        us, um = sheared(st, 0).astype(BF), sheared(mt, 0).astype(BF)
        st, mt = st.astype(BF), mt.astype(BF)
        high_first, low_third = us * ahead, us * behind
        low_middle, high_middle = um * ahead, um * behind
        low, high = rq_ref[0:n], rq_ref[n:]
        dks.append((
            dot(st * below, qb) + dot(high_first, high),
            dot(mt, qb) + dot(low_middle, low) + dot(high_middle, high),
            dot(st * above, qb) + dot(low_third, low),
        ))
        kjt = [kjt_ref[qt + m, lo:hi, :] for m in range(3)]
        drqt_acc[lo:hi, 0:n] += dot(kjt[1], low_middle) + dot(kjt[2], low_third)
        drqt_acc[lo:hi, n:] += dot(kjt[0], high_first) + dot(kjt[1], high_middle)
    for m in range(3):
        dk_acc[qt + m] += both_heads(dks[0][m], dks[1][m])
    return dot(flip, both_heads(*dqs).astype(BF)).astype(BF)


def bwd_masks(n, mask_ref):
    row, lane = grid_of(n)
    for m, keep in enumerate((lane >= row, lane < row, row + lane >= n, row + lane < n)):
        mask_ref[m] = jnp.where(keep, 1.0, 0.0).astype(BF)


class Mesh:
    def __init__(self, ns, nb):
        self.ns, self.nb, self.nz = ns, nb, nb // 2
        self.bits = ns.bit_length() - 1
        self.ways = 2 if ns <= 4 else 1

    def locate(self):
        self.s = lax.axis_index("seq")
        self.b = lax.axis_index("batch")
        self.z, self.c = self.b // 2, self.b % 2

    def at(self, s, b):
        return {"seq": s, "batch": b}

    def greet(self):
        barrier = pltpu.get_barrier_semaphore()
        peers = [self.at(self.s, toggled(self.b, 1))]
        peers += [self.at(self.s, toggled(self.z, step) * 2 + self.c) for step in range(1, self.nz)]
        peers += [self.at(toggled(self.s, step), self.b) for step in range(1, self.ns)]
        for peer in peers:
            pl.semaphore_signal(barrier, inc=1, device_id=peer, device_id_type=MESH)
        pl.semaphore_wait(barrier, len(peers))


class Chunk:
    def __init__(self, mesh, rows, lanes, moves, box=None, early_z=False):
        self.mesh, self.rows, self.moves, self.box, self.early_z = mesh, rows, moves, box, early_z
        unit = 128 * mesh.ways * mesh.ns
        self.lanes = -(-lanes // unit) * unit
        self.piece = self.lanes // (mesh.ways * mesh.ns)
        self.depth = 1 if early_z else mesh.nz

    def scratch(self):
        mesh, rows, lanes = self.mesh, self.rows, self.lanes
        full = pltpu.VMEM((mesh.nz, rows, lanes), BF)
        shapes = [full] if self.box else [full, full]
        for level in range(mesh.bits):
            shapes.append(pltpu.VMEM((mesh.ways, self.depth, rows, lanes // mesh.ways // 2 >> level), BF))
        wide = lanes // mesh.ways if self.early_z else self.piece
        shapes += [pltpu.VMEM((mesh.ways, mesh.nz - 1, rows, wide), BF), pltpu.VMEM((rows, lanes), BF)]
        dma = pltpu.SemaphoreType.DMA
        moves = len(self.moves)
        shapes += [] if self.box else [dma((moves,))]
        shapes += [dma((2, moves)), dma((2, 2, mesh.bits)), dma((2, 2, mesh.nz - 1)), dma((2, 2, mesh.bits))]
        return shapes

    def bind(self, refs):
        bits = self.mesh.bits
        if self.box:
            self.mine = self.box(self.mesh.c)
        else:
            self.mine, refs = refs[0], refs[1:]
        self.first = refs[0]
        self.halves = refs[1 : 1 + bits]
        self.across, self.final = refs[1 + bits : 3 + bits]
        refs = refs[3 + bits :]
        if not self.box:
            self.own_sem, refs = refs[0], refs[1:]
        self.core_sem, self.seq_sem, self.z_sem, self.out_sem = refs[:4]
        return refs[4:]

    def copy(self, src, dst, sems, index, s, b):
        return pltpu.make_async_remote_copy(
            src_ref=src,
            dst_ref=dst,
            send_sem=sems.at[(0,) + index],
            recv_sem=sems.at[(1,) + index],
            device_id=self.mesh.at(s, b),
            device_id_type=MESH,
        )

    def own_copies(self):
        for n, (source, at, size) in enumerate([] if self.box else self.moves):
            yield pltpu.make_async_copy(source(self.mesh.c), self.mine.at[:, :, pl.ds(at, size)], self.own_sem.at[n])

    def core_copies(self):
        mesh = self.mesh
        for n, (source, at, size) in enumerate(self.moves):
            yield self.copy(
                source(1 - mesh.c), self.first.at[:, :, pl.ds(at, size)], self.core_sem, (n,), mesh.s, toggled(mesh.b, 1)
            )

    def order(self, half, level):
        return (level + half) % self.mesh.bits

    def region(self, level, half):
        size = self.lanes // self.mesh.ways
        base = half * size
        sent = base
        for at in range(level):
            mine = (self.mesh.s // (1 << self.order(half, at))) % 2
            size = size // 2
            sent = base + (1 - mine) * size
            base = base + mine * size
        return base, sent, size

    def span(self, start, size):
        return pl.ds(pl.multiple_of(start, 128), size)

    def planes(self):
        return pl.ds(self.mesh.z, 1) if self.early_z else slice(None)

    def seq_copy(self, level, half):
        unused, sent, size = self.region(level + 1, half)
        return self.copy(
            self.mine.at[self.planes(), :, self.span(sent, size)],
            self.halves[level].at[half],
            self.seq_sem,
            (half, level),
            toggled(self.mesh.s, 1 << self.order(half, level)),
            self.mesh.b,
        )

    def z_region(self, half):
        kept, unused, size = self.region(0 if self.early_z else self.mesh.bits, half)
        return self.span(kept, size)

    def z_copies(self, half):
        mesh = self.mesh
        for step in range(1, mesh.nz):
            other = toggled(mesh.z, step)
            yield self.copy(
                self.mine.at[other, :, self.z_region(half)],
                self.across.at[half, step - 1],
                self.z_sem,
                (half, step - 1),
                mesh.s,
                other * 2 + mesh.c,
            )

    def out_copy(self, level, half):
        kept, unused, size = self.region(level + 1, half)
        lanes = self.span(kept, size)
        return self.copy(
            self.final.at[:, lanes],
            self.final.at[:, lanes],
            self.out_sem,
            (half, level),
            toggled(self.mesh.s, 1 << self.order(half, level)),
            self.mesh.b,
        )

    def start_core(self):
        for copy in self.core_copies():
            copy.start()
        for copy in self.own_copies():
            copy.start()

    def add_core(self):
        for copy in self.own_copies():
            copy.wait()
        for copy in self.core_copies():
            copy.wait_recv()
        parts = 4
        size = self.lanes // parts

        def add(n, carry):
            z, lanes = n // parts, self.span((n % parts) * size, size)
            self.mine[z, :, lanes] = (self.mine[z, :, lanes].astype(F32) + self.first[z, :, lanes].astype(F32)).astype(BF)
            return carry

        lax.fori_loop(0, self.mesh.nz * parts, add, 0)

    def start_seq(self, level):
        for half in range(self.mesh.ways):
            self.seq_copy(level, half).start()

    def add_seq(self, level):
        for half in range(self.mesh.ways):
            self.seq_copy(level, half).wait_recv()
            kept, unused, size = self.region(level + 1, half)
            lanes = self.span(kept, size)

            def add(n, carry):
                z = self.mesh.z if self.early_z else n
                got = self.halves[level][half, n].astype(F32)
                self.mine[z, :, lanes] = (self.mine[z, :, lanes].astype(F32) + got).astype(BF)
                return carry

            lax.fori_loop(0, self.depth, add, 0)
            if self.early_z and level == self.mesh.bits - 1:
                self.final[:, lanes] = self.mine[self.mesh.z, :, lanes]

    def end_seq(self):
        self.add_seq(1)
        for level in range(2, self.mesh.bits):
            self.start_seq(level)
            self.add_seq(level)

    def start_z(self):
        for half in range(self.mesh.ways):
            for copy in self.z_copies(half):
                copy.start()

    def add_z(self):
        z = self.mesh.z
        for half in range(self.mesh.ways):
            for copy in self.z_copies(half):
                copy.wait_recv()
            lanes = self.z_region(half)
            total = self.mine[z, :, lanes].astype(F32)
            for step in range(1, self.mesh.nz):
                total = total + self.across[half, step - 1].astype(F32)
            if self.early_z:
                self.mine[z, :, lanes] = total.astype(BF)
            else:
                self.final[:, lanes] = total.astype(BF)

    def start_out(self, level):
        for half in range(self.mesh.ways):
            self.out_copy(level, half).start()

    def core(self):
        self.start_core()

    def s0(self):
        if self.early_z:
            self.add_z()
        else:
            self.add_core()
        self.start_seq(0)

    def s1(self):
        self.add_seq(0)
        self.start_seq(1)

    def z(self):
        if self.early_z:
            self.add_core()
        else:
            self.end_seq()
        self.start_z()

    def out(self):
        if self.early_z:
            self.end_seq()
        else:
            self.add_z()
        self.start_out(self.mesh.bits - 1)

    def out2(self):
        for level in reversed(range(self.mesh.bits - 1)):
            for half in range(self.mesh.ways):
                self.out_copy(level + 1, half).wait_recv()
            self.start_out(level)

    def finish(self):
        for half in range(self.mesh.ways):
            self.out_copy(0, half).wait()
            for level in range(1, self.mesh.bits):
                self.out_copy(level, half).wait_send()
            for copy in self.z_copies(half):
                copy.wait_send()
            for level in range(self.mesh.bits):
                self.seq_copy(level, half).wait_send()
        for copy in self.core_copies():
            copy.wait_send()


class Layout:
    def __init__(self, ns, nb, width, hidden, table):
        self.mesh = mesh = Mesh(ns, nb)
        self.width, self.hidden = width, hidden
        self.rows = rows = width // nb
        self.fold = hidden // nb // rows
        self.rel_rows = table // nb
        self.pairs = width // 128
        self.third = width // 3
        self.rel_at = 384
        self.small_at = 384 + 512
        self.stack = rows // 16
        small_lanes = -(-self.pairs // self.stack) * 128
        self.split = split = hidden // 3
        whole = lambda name, lanes, early=False: self.boxed(lambda c: getattr(self, name).at[:, c], lanes, early)
        self.down = whole("down_ref", self.fold * width)
        self.into = whole("into_ref", hidden - split)
        self.rest = whole("rest_ref", split, False)
        lanes = Chunk(mesh, rows, 768 + self.third, []).lanes
        self.near = [self.boxed(lambda c, n=n: self.near_ref.at[n, :, c], lanes, n in (2,)) for n in range(3)]
        self.far = whole("far_ref", self.small_at + small_lanes)
        self.chunks = [self.down, self.into, self.rest, *self.near, self.far]

    def boxed(self, box, lanes, early=False):
        chunk = Chunk(self.mesh, self.rows, lanes, [], early_z=early)
        chunk.box, chunk.moves = box, [(box, 0, chunk.lanes)]
        return chunk

    def starts(self):
        at = 0
        for chunk in self.chunks:
            yield at
            at += chunk.lanes

    def scratch(self):
        mesh = self.mesh
        box = lambda lanes: pltpu.VMEM((mesh.nz, 2, self.rows, lanes), BF)
        shapes = [box(chunk.lanes) for chunk in (self.down, self.into, self.rest, self.far)]
        shapes.append(pltpu.VMEM((3, mesh.nz, 2, self.rows, self.near[0].lanes), BF))
        for chunk in self.chunks:
            shapes += chunk.scratch()
        return shapes

    def bind(self, refs):
        self.mesh.locate()
        self.down_ref, self.into_ref, self.rest_ref, self.far_ref, self.near_ref = refs[:5]
        refs = refs[5:]
        for chunk in self.chunks:
            refs = chunk.bind(refs)
        return refs

    def store_down(self, m, grads):
        rows, share = self.rows, self.rows * self.fold
        for n in range(self.width // rows):
            b, part = divmod(m * self.width + n * rows, share)
            lanes = slice(part // rows * self.width, (part // rows + 1) * self.width)
            self.down_ref[b // 2, b % 2, :, lanes] = grads[n * rows : (n + 1) * rows]

    def store_into(self, m, grads):
        rows, split = self.rows, self.split
        ref, lanes = (self.rest_ref, slice(0, split)) if m == 0 else (self.into_ref, slice((m - 1) * split, m * split))
        for b in range(self.mesh.nb):
            ref[b // 2, b % 2, :, lanes] = grads[b * rows : (b + 1) * rows]

    def store_out(self, grads):
        rows, third = self.rows, self.third
        for b in range(self.mesh.nb):
            for n in range(3):
                part = grads[b * rows : (b + 1) * rows, n * third : (n + 1) * third]
                self.near_ref[n, b // 2, b % 2, :, 768 : 768 + third] = part

    def store_pair(self, pair, grads):
        rows = self.rows
        box = pair // 2
        lanes = pl.ds(pl.multiple_of((pair % 2) * 384, 128), 384)

        @pl.when(pair < self.pairs - 1)
        def _():
            for b in range(self.mesh.nb):
                self.near_ref[box, b // 2, b % 2, :, lanes] = grads[b * rows : (b + 1) * rows]

        @pl.when(pair == self.pairs - 1)
        def _():
            for b in range(self.mesh.nb):
                self.far_ref[b // 2, b % 2, :, 0:384] = grads[b * rows : (b + 1) * rows]

    def store_rest(self, rel, vectors):
        take, at, half = self.rel_rows, self.rel_at, self.rel_rows // 2
        for b in range(self.mesh.nb):
            part = rel[b * take : (b + 1) * take]
            put = self.far_ref.at[b // 2, b % 2]
            put[0:take, at : at + 512] = part[:, 0:512]
            put[take : take + half, at : at + 256] = part[0:half, 512:768]
            put[take : take + half, at + 256 : at + 512] = part[half:, 512:768]
            for n in range(self.pairs):
                row, lane = (n % self.stack) * 16, self.small_at + (n // self.stack) * 128
                put[row : row + 16, lane : lane + 128] = vectors[:, n * 128 : (n + 1) * 128]

    def schedule(self):
        down, into, rest, one, two, three, far = self.chunks

        steps = {
            1: [rest.s0],
            2: [into.s0],
            3: [down.s0],
            7: [one.core],
            8: [into.s1],
            9: [down.s1, rest.s1],
            11: [into.z],
            12: [one.s0, two.core],
            13: [rest.z, two.s0],
            14: [down.z, into.out, one.s1],
            15: [two.s1],
            16: [into.out2, rest.out, three.core, one.z],
            17: [two.z],
        }
        last = [
            far.core,
            three.z,
            far.s0,
            down.out,
            two.out,
            far.s1,
            one.out,
            three.s0,
            down.out2,
            far.z,
            three.s1,
            two.out2,
            one.out2,
            three.out,
            far.out,
            rest.out2,
            three.out2,
            far.out2,
        ]
        last += [chunk.finish for chunk in self.chunks]
        return steps, last


class Edges:
    def __init__(self, mesh, refs):
        self.mesh = mesh
        self.sent, self.got, self.sems = refs

    def copy(self, side):
        other = self.mesh.s + (2 * side - 1)
        return pltpu.make_async_remote_copy(
            src_ref=self.sent.at[side],
            dst_ref=self.got.at[1 - side],
            send_sem=self.sems.at[0, side],
            recv_sem=self.sems.at[1, 1 - side],
            device_id=self.mesh.at(other, self.mesh.b),
            device_id_type=MESH,
        )

    def has(self, side):
        return self.mesh.s > 0 if side == 0 else self.mesh.s < self.mesh.ns - 1

    def start(self):
        for side in range(2):
            pl.when(self.has(side))(lambda side=side: self.copy(side).start())

    def finish(self, add):
        for side in range(2):

            @pl.when(self.has(side))
            def _(side=side):
                self.copy(side).wait_send()
                self.copy(1 - side).wait_recv()
                add(side, self.got[side])


def bwd_kernel(tq, scale, layout, q_ref, k_ref, v_ref, g_ref, rk_ref, rq_ref, p_ref, wk_ref, wq_ref, wv_ref,
               act_hbm, branch_ref, hidden_ref, pre_hbm, ctx_hbm, attn_hbm, g_one_hbm, xt_hbm, picks_ref, small_ref, *rest):
    (dx_ref, packed_hbm,
               mask_ref, kjt_ref, dk_acc, dvt_acc, drkt_acc, drqt_acc,
               xt_ref, d_ref, rel_acc, vec_ref, dx_acc, sent_ref, got_ref, edge_sem,
     load_ref, load_sem, side_sem, packed_sem, *refs) = rest
    block = q_ref.shape[0]
    nq = block // tq
    ext = k_ref.shape[0]
    nk = ext // tq
    span = tq
    table = 2 * span
    pair = pl.program_id(0)
    pairs = layout.pairs
    flip = anti(tq)
    layout.bind(refs)
    edges = Edges(layout.mesh, (sent_ref, got_ref, edge_sem))
    steps, last = layout.schedule()

    def run(actions):
        def all_of():
            for action in actions:
                action()
        return all_of

    loads = [act_hbm.at[:, pl.ds(m * layout.width, layout.width)] for m in range(layout.fold)]
    loads += [pre_hbm.at[:, pl.ds(m * layout.split, layout.split)] for m in range(3)]
    loads += [ctx_hbm, attn_hbm]

    def load(m):
        size = loads[m].shape
        return pltpu.make_async_copy(loads[m], load_ref.at[m % 3, pl.ds(0, size[0]), pl.ds(0, size[1])], load_sem.at[m % 3])

    def loaded(m):
        size = loads[m].shape
        load(m).wait()
        return load_ref[m % 3, 0 : size[0], 0 : size[1]]

    def dx_copy():
        return pltpu.make_async_copy(g_one_hbm, dx_ref, side_sem.at[0])

    def xt_copy():
        return pltpu.make_async_copy(xt_hbm, xt_ref, side_sem.at[1])

    @pl.when(pair == 0)
    def _():
        for m in range(2):
            load(m).start()
        layout.mesh.greet()
        m = 0
        for n in range(layout.fold):
            load(m + 2).start()
            layout.store_down(n, dot(loaded(m), branch_ref[...], TN).astype(BF))
            m += 1
        layout.down.core()
        for n in range(3):
            if m + 2 < len(loads):
                load(m + 2).start()
            layout.store_into(n, dot(hidden_ref[...], loaded(m), TN).astype(BF))
            if n == 0:
                layout.rest.core()
            m += 1
        xt_copy().start()
        dx_copy().start()
        layout.into.core()
        run(steps.get(0, []))()
        layout.store_out(dot(loaded(m), loaded(m + 1), TN).astype(BF))
        bwd_masks(tq, mask_ref)
        d_ref[...] = jnp.zeros_like(d_ref)
        rel_acc[...] = jnp.zeros_like(rel_acc)
        dx_acc[...] = jnp.zeros_like(dx_acc)
        vec_ref[...] = small_ref[...]

    for kt in range(nk):
        kjt_ref[kt] = dot(k_ref[kt * tq : (kt + 1) * tq, :], flip, TN).astype(BF)
    dk_acc[...] = jnp.zeros_like(dk_acc)
    dvt_acc[...] = jnp.zeros_like(dvt_acc)
    drkt_acc[...] = jnp.zeros_like(drkt_acc)
    drqt_acc[...] = jnp.zeros_like(drqt_acc)

    def tile(qt, carry):
        for step, actions in steps.items():
            if step and step % 3 < min(nq, 2):
                pl.when((pair == step // 3) & (qt == step % 3))(run(actions))
        row = pl.multiple_of(qt * tq, tq)
        dq = bwd_tile(
            tq, scale, qt, q_ref, k_ref, v_ref, g_ref, rk_ref, rq_ref, p_ref, mask_ref, kjt_ref, dk_acc, dvt_acc, drkt_acc, drqt_acc
        )
        d_ref[pl.ds(span + row, tq), 0:128] = dq
        return carry

    lax.fori_loop(0, nq, tile, 0)
    for step, actions in steps.items():
        if step % 3 >= min(nq, 2):
            pl.when(pair == step // 3)(run(actions))
    for kt in range(nk):
        here = slice(kt * tq, (kt + 1) * tq)
        dk = dot(flip, dk_acc[kt].astype(BF)).astype(BF)
        dv = dvt_acc[:, here].T.astype(BF)
        d_ref[here, 128:256] = dk
        d_ref[here, 256:384] = dv
    for st in range(table // 128):
        here = slice(ext + st * 128, ext + (st + 1) * 128)
        d_ref[here, 0:128] = drqt_acc[:, st * 128 : (st + 1) * 128].T.astype(BF)
        d_ref[here, 128:256] = drkt_acc[:, st * 128 : (st + 1) * 128].T.astype(BF)

    weights = jnp.concatenate([wq_ref[...], wk_ref[...], wv_ref[...]], axis=1)
    dx_acc[...] += dot(d_ref[0:ext], weights, NT)

    @pl.when(pair == pairs - 1)
    def _():
        sent_ref[0] = dx_acc[0:span].astype(BF)
        sent_ref[1] = dx_acc[ext - span :].astype(BF)
        edges.start()

    pl.when(pair == 0)(lambda: xt_copy().wait())
    grads = dot(xt_ref[...], d_ref[...]).astype(BF)
    layout.store_pair(pair, grads)
    rel_acc[...] += dot(d_ref[ext:, 0:128], wq_ref[...], NT) + dot(d_ref[ext:, 128:256], wk_ref[...], NT)
    sums = dot(jnp.ones((8, ext + table), BF), d_ref[...])[0:1]
    for n in range(3):
        vec_ref[10 + n : 11 + n, pl.ds(pl.multiple_of(pair * 128, 128), 128)] = sums[:, n * 128 : (n + 1) * 128]

    @pl.when(pair == pairs - 1)
    def _():
        rel = dot(picks_ref[...], rel_acc[...].astype(BF)).astype(BF)
        layout.store_rest(rel, vec_ref[...].astype(BF))
        run(last[:1])()
        dx_copy().wait()
        dx_ref[...] += dx_acc[span : span + block]
        run(last[1:])()

        packed_copies = []
        for n, (at, chunk) in enumerate(zip(layout.starts(), layout.chunks)):
            packed_copies.append(pltpu.make_async_copy(chunk.final, packed_hbm.at[:, pl.ds(at, chunk.lanes)], packed_sem.at[n]))
            packed_copies[-1].start()

        def take(side, rows):
            here = slice(0, span) if side == 0 else slice(block - span, block)
            dx_ref[here] += rows.astype(F32)

        edges.finish(take)
        for copy in packed_copies:
            copy.wait()


def attn_bwd(span, q, k, v, g, rk, rq, probs, w_key, w_query, w_value, act, branch, hidden, pre, context, g_attn, g_one, xt, picks, small):
    block, width = q.shape
    ext = k.shape[0]
    table = 2 * span
    scale = (3.0 * 64) ** -0.5
    ns, nb = lax.axis_size("seq"), lax.axis_size("batch")
    layout = Layout(ns, nb, width, act.shape[1], table)
    col = lambda rows: pl.BlockSpec((rows, 128), lambda h: (0, h))
    whole = lambda shape: pl.BlockSpec(shape, lambda h: (0, 0), pipeline_mode=pl.Buffered(1))
    any_spec = pl.BlockSpec(memory_space=pltpu.HBM)
    packed = jax.ShapeDtypeStruct((layout.rows, sum(chunk.lanes for chunk in layout.chunks)), BF)
    outs = pl.pallas_call(
        functools.partial(bwd_kernel, span, scale, layout),
        grid=(width // 128,),
        out_shape=(
            jax.ShapeDtypeStruct((block, width), F32),
            packed,
        ),
        in_specs=[col(block), col(ext), col(ext), col(block), col(rk.shape[0]), col(rq.shape[0]),
                  pl.BlockSpec((2, block, table), lambda h: (h, 0, 0)), col(width), col(width), col(width),
                  any_spec, whole(branch.shape), whole(hidden.shape), any_spec, any_spec, any_spec, any_spec, any_spec,
                  whole(picks.shape), whole(small.shape)],
        out_specs=(whole((block, width)), any_spec),
        scratch_shapes=[
            pltpu.VMEM((4, span, span), BF),
            pltpu.VMEM((ext // span, 128, span), BF),
            pltpu.VMEM((ext // span, span, 128), F32),
            pltpu.VMEM((128, ext), F32),
            pltpu.VMEM((128, table), F32),
            pltpu.VMEM((128, table), F32),
            pltpu.VMEM((width, ext + table), BF),
            pltpu.VMEM((ext + table, 384), BF),
            pltpu.VMEM((table, width), F32),
            pltpu.VMEM((16, width), F32),
            pltpu.VMEM((ext, width), F32),
            pltpu.VMEM((2, span, width), BF),
            pltpu.VMEM((2, span, width), BF),
            pltpu.SemaphoreType.DMA((2, 2)),
            pltpu.VMEM((3, block, layout.split), BF),
            pltpu.SemaphoreType.DMA((3,)),
            pltpu.SemaphoreType.DMA((2,)),
            pltpu.SemaphoreType.DMA((len(layout.chunks),)),
        ] + layout.scratch(),
        compiler_params=pltpu.CompilerParams(collective_id=0, has_side_effects=True, vmem_limit_bytes=60 << 20),
        cost_estimate=pl.CostEstimate(flops=50_000_000_000, bytes_accessed=20 << 20, transcendentals=0),
        name="attn_bwd_reduce",
    )(*[pltpu.with_memory_space_constraint(arg, pltpu.HBM) for arg in (q, k, v)], g, *[pltpu.with_memory_space_constraint(arg, pltpu.HBM) for arg in (rk, rq, probs)], w_key, w_query, w_value, act, branch, hidden, pre, context, g_attn, g_one, pltpu.with_memory_space_constraint(xt, pltpu.HBM), picks, small)
    return layout, outs


def unpack_kernel(layout, packed_hbm, dx_hbm,
                  dx_out, down_out, into_out, out_out, query_out, key_out, value_out, rel_out, *refs):
    vec_outs, wide_out, (packed_ref, rel_ref, vec_ref, sems) = refs[:-5], refs[-5], refs[-4:]
    packed_copy = pltpu.make_async_copy(packed_hbm, packed_ref, sems.at[0])
    dx_copy = pltpu.make_async_copy(dx_hbm, dx_out, sems.at[1])
    packed_copy.start()
    dx_copy.start()
    packed_copy.wait()
    rows, width, pairs = layout.rows, layout.width, layout.pairs
    parts = [packed_ref.at[:, at : at + chunk.lanes] for at, chunk in zip(layout.starts(), layout.chunks)]
    down_ref, into_ref, rest_ref, *near, far_ref = parts
    split = layout.hidden // 3
    into_out[:, :split] = rest_ref[:, :split].astype(F32)
    into_out[:, split:] = into_ref[:, : layout.hidden - split].astype(F32)
    for n in range(layout.fold):
        down_out[n * rows : (n + 1) * rows, :] = down_ref[:, n * width : (n + 1) * width].astype(F32)
    for n, side in enumerate(near):
        out_out[:, n * layout.third : (n + 1) * layout.third] = side[:, 768 : 768 + layout.third].astype(F32)
    for m in range(pairs):
        side, at = (far_ref, 0) if m == pairs - 1 else (near[m // 2], m % 2 * 384)
        for n, out in enumerate((query_out, key_out, value_out)):
            out[:, m * 128 : (m + 1) * 128] = side[:, at + n * 128 : at + (n + 1) * 128].astype(F32)
    take, at, half = layout.rel_rows, layout.rel_at, layout.rel_rows // 2
    rel_ref[:, 0:512] = far_ref[0:take, at : at + 512].astype(F32)
    for n in range(2):
        rel_ref[n * half : (n + 1) * half, 512:768] = far_ref[take : take + half, at + n * 256 : at + (n + 1) * 256].astype(F32)
    own = take // layout.mesh.ns
    rel_out[...] = pltpu.roll(rel_ref[...], take - lax.axis_index("seq") * own, 0)[:own]
    for n in range(pairs):
        row, lane = (n % layout.stack) * 16, layout.small_at + (n // layout.stack) * 128
        vec_ref[:, n * 128 : (n + 1) * 128] = far_ref[row : row + 16, lane : lane + 128].astype(F32)
    b = lax.axis_index("batch")
    mine = pltpu.roll(vec_ref[...], width - b * rows, 1)
    for out, n in zip(vec_outs, (0, 1, 2, 3, 4, 5, 10, 11, 12)):
        out[...] = mine[n, :rows]
    wide = wide_out.shape[0]
    fit = width // wide
    line = pltpu.roll(pltpu.roll(vec_ref[...], width - (b % fit) * wide, 1), 10 - b // fit, 0)
    wide_out[...] = line[0, :wide]
    dx_copy.wait()


def unpack(layout, packed, dx):
    rows, width = layout.rows, layout.width
    shape = lambda *dims: jax.ShapeDtypeStruct(dims, F32)
    shapes = [shape(*dx.shape), shape(layout.fold * rows, width), shape(rows, layout.hidden)] + [shape(rows, width)] * 4
    shapes += [shape(layout.rel_rows // layout.mesh.ns, width)] + [shape(rows)] * 9 + [shape(layout.fold * rows)]
    vmem, far = pl.BlockSpec(memory_space=pltpu.VMEM), pl.BlockSpec(memory_space=pltpu.HBM)
    return pl.pallas_call(
        functools.partial(unpack_kernel, layout),
        out_shape=shapes,
        in_specs=[far, far],
        out_specs=[vmem] * len(shapes),
        scratch_shapes=[
            pltpu.VMEM(packed.shape, BF),
            pltpu.VMEM((layout.rel_rows, width), F32),
            pltpu.VMEM((16, width), F32),
            pltpu.SemaphoreType.DMA((2,)),
        ],
        compiler_params=pltpu.CompilerParams(vmem_limit_bytes=32 << 20),
        name="unpack",
    )(*[pltpu.with_memory_space_constraint(arg, pltpu.HBM) for arg in (packed, dx)])


NORM_EPS = 1e-07
STEP = 1536


def mid_kernel(ctx_ref, x_ref, cot_ref, b_out, gain_attn, shift_attn, b_in, b_down, gain_ffn, shift_ffn, w_out_hbm, w_in_hbm, w_down_hbm,
               out_ref, branch_ref, hidden_ref, gone_ref, gattn_ref, gctx_ref, vec_ref, act_hbm, pre_hbm,
               w_out_ref, w_in_ref, w_down_ref, act_ref, pre_ref, slope_ref, full_ref, normed_ref, inv_ref, acc_ref, line_ref, in_sem, out_sem):
    block, width = x_ref.shape
    wide = w_in_ref.shape[1]
    parts = wide // width
    loads = [(w_out_hbm, w_out_ref)]
    for n in range(parts):
        loads.append((w_in_hbm.at[:, pl.ds(n * width, width)], w_in_ref.at[:, pl.ds(n * width, width)]))
    loads.append((w_down_hbm, w_down_ref))
    row_of = lambda ref: ref[...].astype(F32)[None]
    total = lambda values: jnp.sum(values, axis=0, keepdims=True)
    mean = lambda values: jnp.mean(values, axis=-1, keepdims=True)

    def load(n):
        return pltpu.make_async_copy(*loads[n], in_sem.at[n])

    def norm(values):
        centred = values - mean(values)
        inv = lax.rsqrt(mean(centred * centred) + NORM_EPS)
        return centred * inv, inv

    def norm_back(grads, normed, inv):
        return inv * (grads - mean(grads) - normed * mean(grads * normed))

    for n in range(len(loads)):
        load(n).start()
    blocks = [slice(n, n + 128) for n in range(0, block, 128)]
    load(0).wait()
    for rows in blocks:
        normed, inv = norm(x_ref[rows].astype(F32) + dot(ctx_ref[rows], w_out_ref[...]) + row_of(b_out))
        normed_ref[rows], inv_ref[rows] = normed, inv
        hidden = normed * row_of(gain_attn) + row_of(shift_attn)
        full_ref[rows] = hidden
        hidden_ref[rows] = hidden.astype(BF)
    for n in range(1, len(loads)):
        load(n).wait()
    acc_ref[...] = full_ref[...] + row_of(b_down)

    def up(n, carry):
        cols = pl.ds(pl.multiple_of(n * STEP, STEP), STEP)
        pre = dot(hidden_ref[...], w_in_ref[:, cols]) + b_in[cols].astype(F32)[None]
        phi = 0.5 + 0.5 * lax.erf(pre * (0.5**0.5))
        act = (pre * phi).astype(BF)
        act_ref[:, cols] = act
        slope_ref[:, cols] = phi + pre * (jnp.exp(-0.5 * pre * pre) * ((2.0 * math.pi) ** -0.5))
        acc_ref[...] += dot(act, w_down_ref[cols, :])
        return carry

    lax.fori_loop(0, wide // STEP, up, 0, unroll=1)
    act_copy = pltpu.make_async_copy(act_ref, act_hbm, out_sem.at[0])
    act_copy.start()
    gain, shift, bias = 0.0, 0.0, 0.0
    for rows in blocks:
        normed, inv = norm(acc_ref[rows])
        out_ref[rows] = (normed * row_of(gain_ffn) + row_of(shift_ffn)).astype(BF)
        grads = cot_ref[rows].astype(F32)
        gain, shift = gain + total(grads * normed), shift + total(grads)
        grad_two = norm_back(grads * row_of(gain_ffn), normed, inv)
        acc_ref[rows] = grad_two
        branch = grad_two.astype(BF)
        branch_ref[rows] = branch
        bias = bias + total(branch.astype(F32))
    vec_ref[...] = jnp.zeros_like(vec_ref)
    vec_ref[3:4], vec_ref[4:5], vec_ref[5:6] = bias, gain, shift

    def down(n, carry):
        cols = pl.ds(pl.multiple_of(n * STEP, STEP), STEP)
        pre = (dot(branch_ref[...], w_down_ref[cols, :], NT) * slope_ref[:, cols]).astype(BF)
        pre_ref[:, cols] = pre
        line_ref[0:1, cols] = total(pre.astype(F32))
        acc_ref[...] += dot(pre, w_in_ref[:, cols], NT)
        return carry

    lax.fori_loop(0, wide // STEP, down, 0, unroll=1)
    pre_copy = pltpu.make_async_copy(pre_ref, pre_hbm, out_sem.at[1])
    pre_copy.start()
    for n in range(parts):
        vec_ref[6 + n : 7 + n] = line_ref[0:1, n * width : (n + 1) * width]
    gain, shift, bias = 0.0, 0.0, 0.0
    for rows in blocks:
        grads, normed = acc_ref[rows], normed_ref[rows]
        gain, shift = gain + total(grads * normed), shift + total(grads)
        grad_one = norm_back(grads * row_of(gain_attn), normed, inv_ref[rows])
        gone_ref[rows] = grad_one
        grad_attn = grad_one.astype(BF)
        gattn_ref[rows] = grad_attn
        bias = bias + total(grad_attn.astype(F32))
        gctx_ref[rows] = dot(grad_attn, w_out_ref[...], NT).astype(BF)
    vec_ref[0:1], vec_ref[1:2], vec_ref[2:3] = bias, gain, shift
    act_copy.wait()
    pre_copy.wait()


def middle(context, x, cotangent, small, w_out, w_in, w_down):
    block, width = x.shape
    wide = w_in.shape[1]
    far = pl.BlockSpec(memory_space=pltpu.HBM)
    whole = lambda arg: pl.BlockSpec(arg.shape, lambda t: (0,) * len(arg.shape), pipeline_mode=pl.Buffered(1))
    tall = (block, width)
    args = [context, x, cotangent, *small]
    outs = [jax.ShapeDtypeStruct(tall, BF)]
    outs += [pltpu.HBM(dims, kind) for dims, kind in ((tall, BF), (tall, BF), (tall, F32), (tall, BF), (tall, BF), ((16, width), F32))]
    return pl.pallas_call(
        mid_kernel,
        grid=(1,),
        out_shape=outs + [pltpu.HBM((block, wide), BF)] * 2,
        in_specs=[whole(arg) for arg in args] + [far] * 3,
        out_specs=[whole(out) for out in outs] + [far] * 2,
        scratch_shapes=[
            pltpu.VMEM((width, width), BF),
            pltpu.VMEM((width, wide), BF),
            pltpu.VMEM((wide, width), BF),
            pltpu.VMEM((block, wide), BF),
            pltpu.VMEM((block, wide), BF),
            pltpu.VMEM((block, wide), F32),
            pltpu.VMEM(tall, F32),
            pltpu.VMEM(tall, F32),
            pltpu.VMEM((block, 1), F32),
            pltpu.VMEM(tall, F32),
            pltpu.VMEM((8, wide), F32),
            pltpu.SemaphoreType.DMA((2 + wide // width,)),
            pltpu.SemaphoreType.DMA((2,)),
        ],
        compiler_params=pltpu.CompilerParams(vmem_limit_bytes=56 << 20),
        name="middle",
    )(*args, *[pltpu.with_memory_space_constraint(arg, pltpu.HBM) for arg in (w_out, w_in, w_down)])


def local(
    layer_input,
    w_query,
    b_query,
    w_key,
    b_key,
    w_value,
    b_value,
    w_out,
    b_out,
    gain_attn,
    shift_attn,
    w_in,
    b_in,
    w_down,
    b_down,
    gain_ffn,
    shift_ffn,
    rel_table,
    segment_ids,
    cotangent,
):
    rows, block, width = layer_input.shape
    span = rel_table.shape[0] // 2
    x = layer_input[0]
    start = lax.axis_index("seq") * block
    padded = jnp.pad(segment_ids[0], (span, span), constant_values=-1)
    kid = lax.dynamic_slice_in_dim(padded, start, block + 2 * span, 0)
    qid = kid[span : span + block]
    context, probs, q, k, v, rk, rq, xt = attn_fwd(
        span, x, rel_table, w_query, w_key, w_value, b_query, b_key, b_value, qid[:, None], kid[None]
    )

    output, grad_branch, hidden_low, grad_one, grad_attn, grad_context, small, act_low, grad_pre = middle(
        context, x, cotangent[0], [b_out, gain_attn, shift_attn, b_in, b_down, gain_ffn, shift_ffn], w_out, w_in, w_down
    )
    share, lanes = lax.axis_size("batch"), lax.axis_size("seq")
    rel_rows = 2 * span // (share * lanes)
    order = np.arange(2 * span).reshape(lanes, share, rel_rows).transpose(1, 0, 2).reshape(-1)
    picks = jnp.asarray((2 * span - 1 - order)[:, None] == np.arange(2 * span)[None], BF)
    layout, outs = attn_bwd(
        span, q, k, v, grad_context, rk, rq, probs, w_key, w_query, w_value, act_low, grad_branch, hidden_low, grad_pre,
        context, grad_attn, grad_one, xt, picks, small,
    )
    input_grad, packed = outs
    input_grad, down_sum, in_sum, out_sum, query_sum, key_sum, value_sum, rel_sum, *vectors = unpack(layout, packed, input_grad)
    ob, ga, sa, db, gf, sf, qb, kb, vb, ib = vectors
    return (
        output[None], input_grad[None], query_sum, qb, key_sum, kb, value_sum, vb, out_sum, ob,
        ga, sa, in_sum, ib, down_sum, db, gf, sf, rel_sum,
    )


def solution(mesh):
    tokens = P("batch", "seq", None)
    in_specs = (tokens,) + (P(),) * 17 + (P("batch", None), tokens)
    matrix, vector = P("batch", None), P("batch")
    out_specs = (
        (tokens, tokens)
        + (matrix, vector) * 4
        + (vector, vector)
        + (matrix, vector) * 2
        + (vector, vector, P(("seq", "batch"), None))
    )
    return jax.shard_map(local, mesh=mesh, in_specs=in_specs, out_specs=out_specs, check_vma=False)
```

```python
import functools
import math

import jax
import jax.numpy as jnp
import numpy as np
from jax import lax
from jax.experimental import pallas as pl
from jax.experimental.pallas import tpu as pltpu
from jax.sharding import PartitionSpec as P

F32 = jnp.float32
BF = jnp.bfloat16
NN = (((1,), (0,)), ((), ()))
NT = (((1,), (1,)), ((), ()))
TN = (((0,), (0,)), ((), ()))
MESH = pl.DeviceIdType.MESH


def toggled(value, mask):
    out = value
    for bit in range(mask.bit_length()):
        if mask >> bit & 1:
            out = out + (1 - 2 * ((value // (1 << bit)) % 2)) * (1 << bit)
    return out


def dot(a, b, dims=NN):
    return lax.dot_general(a, b, dims, preferred_element_type=F32)


def head_lanes(x, hh):
    lane = lax.broadcasted_iota(jnp.int32, x.shape, len(x.shape) - 1)
    keep = (lane < 64) if hh == 0 else (lane >= 64)
    return jnp.where(keep, x.astype(F32), 0.0).astype(x.dtype)


def both_heads(first, second):
    lane = lax.broadcasted_iota(jnp.int32, first.shape, 1)
    return jnp.where(lane < 64, first, second)


def grid_of(n):
    return lax.broadcasted_iota(jnp.int32, (n, n), 0), lax.broadcasted_iota(jnp.int32, (n, n), 1)


def anti(n):
    row, lane = grid_of(n)
    return jnp.where(row + lane == n - 1, 1.0, 0.0).astype(BF)


def sheared(x, shift):
    return pltpu.roll(x, shift, 1, stride=1, stride_axis=0)


def fwd_tile(n, scale, pair, qt, q_ref, k_ref, v_ref, rk_ref, rqm_ref, bias_ref, mask_ref, p_ref):
    factor = scale * math.log2(math.e)
    row, lane = grid_of(n)
    right, upper = lane > row, row + lane >= n - 1
    lanes = pl.ds(pl.multiple_of(pair * 128, 128), 128)
    at = lambda m: (pl.ds(pl.multiple_of((qt + m) * n, n), n), lanes)
    qb = q_ref[at(0)]
    rk_low, rk_high = rk_ref[0:n, lanes], rk_ref[n:, lanes]
    outs = []
    for hh in range(2):
        qm = head_lanes(qb, hh)
        low, high = rqm_ref[hh, 0:n, lanes], rqm_ref[hh, n:, lanes]
        to_low = sheared(dot(qm, rk_low, NT), 1)
        to_high = sheared(dot(qm, rk_high, NT), 1)
        side = jnp.where(right, dot(qm, k_ref[at(0)], NT) + to_low, dot(qm, k_ref[at(2)], NT) + to_high)
        middle = dot(qm, k_ref[at(1)], NT) + jnp.where(right, to_high, to_low)
        key_side = jnp.where(upper, dot(k_ref[at(0)], high, NT), dot(k_ref[at(2)], low, NT))
        key_middle = jnp.where(upper, dot(k_ref[at(1)], low, NT), dot(k_ref[at(1)], high, NT))
        side = (side + sheared(key_side, 1).T) * factor + bias_ref[:, 0:n]
        middle = (middle + sheared(key_middle, 1).T) * factor + bias_ref[:, n:]
        top = jnp.max(jnp.maximum(side, middle), axis=-1, keepdims=True)
        side, middle = jnp.exp2(side - top), jnp.exp2(middle - top)
        inverse = 1.0 / jnp.sum(side + middle, axis=-1, keepdims=True)
        side, middle = (side * inverse).astype(BF), (middle * inverse).astype(BF)
        p_ref[hh, :, 0:n] = side
        p_ref[hh, :, n:] = middle
        out = dot(side * mask_ref[0], v_ref[at(0)]) + dot(middle, v_ref[at(1)])
        outs.append(out + dot(side * mask_ref[1], v_ref[at(2)]))
    return both_heads(*outs).astype(BF)


class Halo:
    def __init__(self, span, block, ext_ref, sems):
        self.span, self.block, self.ext_ref, self.sems = span, block, ext_ref, sems
        self.s, self.b, self.ns = lax.axis_index("seq"), lax.axis_index("batch"), lax.axis_size("seq")

    def greet(self):
        barrier = pltpu.get_barrier_semaphore()
        for step in range(1, self.ns):
            peer = {"seq": toggled(self.s, step), "batch": self.b}
            pl.semaphore_signal(barrier, inc=1, device_id=peer, device_id_type=MESH)
        pl.semaphore_wait(barrier, self.ns - 1)

    def copy(self, up):
        span, block = self.span, self.block
        src, dst = (block, 0) if up else (span, span + block)
        return pltpu.make_async_remote_copy(
            src_ref=self.ext_ref.at[pl.ds(src, span)],
            dst_ref=self.ext_ref.at[pl.ds(dst, span)],
            send_sem=self.sems.at[0, int(up)],
            recv_sem=self.sems.at[1, int(up)],
            device_id={"seq": self.s + (1 if up else -1), "batch": self.b},
            device_id_type=MESH,
        )

    def sends(self, up):
        return self.s < self.ns - 1 if up else self.s > 0

    def gets(self, up):
        return self.s > 0 if up else self.s < self.ns - 1

    def start(self, up):
        pl.when(self.sends(up))(lambda: self.copy(up).start())

    def wait(self, up):
        at = pl.ds(0 if up else self.span + self.block, self.span)
        pl.when(self.gets(up))(lambda: self.copy(up).wait_recv())

        @pl.when(jnp.logical_not(self.gets(up)))
        def _():
            self.ext_ref[at] = jnp.zeros((self.span, self.ext_ref.shape[1]), BF)

    def finish(self):
        for up in (True, False):
            pl.when(self.sends(up))(lambda up=up: self.copy(up).wait_send())


def fwd_kernel(n, scale, x_hbm, rel_hbm, wk_hbm, wq_hbm, wv_hbm, bq_ref, bk_ref, bv_ref, qid_ref, kid_ref,
               ctx_ref, p_ref, q_out, k_out, v_out, rk_out, rq_out, xt_out,
               q_ref, k_ref, v_ref, rk_ref, rq_ref, xt_ref, ext_ref, rel_ref, flip_ref, wk_ref, wq_ref, wv_ref,
               rqm_ref, bias_ref, mask_ref, halo_sem, in_sem, out_sem):
    block = x_hbm.shape[0]
    ext = block + 2 * n
    qt, pair = pl.program_id(0), pl.program_id(1)
    last = (qt == pl.num_programs(0) - 1) & (pair == pl.num_programs(1) - 1)
    halo = Halo(n, block, ext_ref, halo_sem)
    row, lane = grid_of(n)
    bias_of = lambda ref: ref[...].astype(F32)[None]
    own = slice(n, n + block)
    kept = ((q_ref, q_out), (rk_ref, rk_out), (rq_ref, rq_out), (k_ref, k_out), (v_ref, v_out), (xt_ref, xt_out))
    loads = ((x_hbm, ext_ref.at[pl.ds(n, block)]), (rel_hbm, rel_ref), (wk_hbm, wk_ref), (wq_hbm, wq_ref), (wv_hbm, wv_ref))

    def load(m):
        return pltpu.make_async_copy(*loads[m], in_sem.at[m])

    def keep(first, end):
        for m in range(first, end):
            yield pltpu.make_async_copy(*kept[m], out_sem.at[m])

    def keys(rows):
        k_ref[rows] = (dot(ext_ref[rows], wk_ref[...]) + bias_of(bk_ref)).astype(BF)
        v_ref[rows] = (dot(ext_ref[rows], wv_ref[...]) + bias_of(bv_ref)).astype(BF)

    def turn(ref, first, size, at):
        for m in range(0, size, 128):
            xt_ref[:, at + m : at + m + 128] = ref[first + m : first + m + 128, :].astype(F32).T.astype(BF)

    def get_after():
        halo.wait(False)
        keys(slice(n + block, ext))
        turn(ext_ref, n + block, n, n + block)
        for copy in keep(3, 6):
            copy.start()

    @pl.when((qt == 0) & (pair == 0))
    def _():
        for m in range(5):
            load(m).start()
        halo.greet()
        load(0).wait()
        halo.start(True)
        load(1).wait()
        flip_ref[...] = dot(anti(2 * n), rel_ref[...]).astype(BF)
        load(2).wait()
        rk_ref[...] = (dot(flip_ref[...], wk_ref[...]) + bias_of(bk_ref)).astype(BF)
        load(3).wait()
        rq_ref[...] = (dot(flip_ref[...], wq_ref[...]) + bias_of(bq_ref)).astype(BF)
        q_ref[...] = (dot(ext_ref[own], wq_ref[...]) + bias_of(bq_ref)).astype(BF)
        for copy in keep(0, 3):
            copy.start()
        load(4).wait()
        keys(own)
        head = (lax.broadcasted_iota(jnp.int32, rq_ref.shape, 1) // 64) % 2
        for hh in range(2):
            rqm_ref[hh] = jnp.where(head == hh, rq_ref[...].astype(F32), 0.0).astype(BF)
        mask_ref[0] = jnp.where(lane > row, 1.0, 0.0).astype(BF)
        mask_ref[1] = jnp.where(lane > row, 0.0, 1.0).astype(BF)
        turn(ext_ref, n, block, n)
        turn(flip_ref, 0, 2 * n, ext)
        halo.wait(True)
        halo.start(False)
        keys(slice(0, n))
        turn(ext_ref, 0, n, 0)
        if block == n:
            get_after()

    if block > n:
        pl.when((qt == 1) & (pair == 0))(get_after)

    @pl.when(pair == 0)
    def _():
        at = lambda m: pl.ds(pl.multiple_of((qt + m) * n, n), n)
        qid = qid_ref[at(0), :]
        first, middle, third = [kid_ref[:, at(m)] for m in range(3)]
        side = ((lane > row) & (qid == first)) | ((lane < row) & (qid == third))
        bias_ref[:, 0:n] = jnp.where(side, 0.0, -1e30)
        bias_ref[:, n:] = jnp.where(qid == middle, 0.0, -1e30)

    ctx_ref[...] = fwd_tile(n, scale, pair, qt, q_ref, k_ref, v_ref, rk_ref, rqm_ref, bias_ref, mask_ref, p_ref)

    @pl.when(last)
    def _():
        halo.finish()
        for copy in keep(0, 6):
            copy.wait()


def attn_fwd(span, x, rel_table, w_query, w_key, w_value, b_query, b_key, b_value, qid, kid):
    block, width = x.shape
    ext, table = block + 2 * span, 2 * span
    scale = (3.0 * 64) ** -0.5
    heads = width // 64
    whole = lambda shape: pl.BlockSpec(shape, lambda t, h: (0,) * len(shape), pipeline_mode=pl.Buffered(1))
    far = pl.BlockSpec(memory_space=pltpu.HBM)
    small = [b_query, b_key, b_value, qid, kid]
    kept = [(rows, width) for rows in (block, ext, ext, table, table)] + [(width, ext + table)]
    more = [(ext, width), (table, width), (table, width)] + [(width, width)] * 3
    return pl.pallas_call(
        functools.partial(fwd_kernel, span, scale),
        grid=(block // span, width // 128),
        out_shape=[pltpu.HBM((block, width), BF), pltpu.HBM((heads, block, table), BF)]
        + [pltpu.HBM(shape, BF) for shape in kept],
        in_specs=[far] * 5 + [whole(arg.shape) for arg in small],
        out_specs=[pl.BlockSpec((span, 128), lambda t, h: (t, h)), pl.BlockSpec((2, span, table), lambda t, h: (h, t, 0))]
        + [far] * 6,
        scratch_shapes=[pltpu.VMEM(shape, BF) for shape in kept + more]
        + [
            pltpu.VMEM((2, table, width), BF),
            pltpu.VMEM((span, table), F32),
            pltpu.VMEM((2, span, span), BF),
            pltpu.SemaphoreType.DMA((2, 2)),
            pltpu.SemaphoreType.DMA((5,)),
            pltpu.SemaphoreType.DMA((6,)),
        ],
        compiler_params=pltpu.CompilerParams(collective_id=1, has_side_effects=True, vmem_limit_bytes=44 << 20),
        cost_estimate=pl.CostEstimate(flops=20_000_000_000, bytes_accessed=20 << 20, transcendentals=heads * block * table),
        name="attn_fwd",
    )(*[pltpu.with_memory_space_constraint(arg, pltpu.HBM) for arg in (x, rel_table, w_key, w_query, w_value, b_query, b_key, b_value)], qid, kid)


def bwd_tile(n, scale, qt, q_ref, k_ref, v_ref, g_ref, rk_ref, rq_ref, p_ref, mask_ref, kjt_ref, dk_acc, dvt_acc, drkt_acc, drqt_acc):
    at = lambda m: pl.ds(pl.multiple_of((qt + m) * n, n), n)
    row, lane = grid_of(n)
    flip = anti(n)
    ahead, behind, above, below = [mask_ref[m] for m in range(4)]
    qb, gb = q_ref[at(0), :], g_ref[at(0), :]
    qjt = dot(qb, flip, TN).astype(BF)
    gt = gb.astype(F32).T.astype(BF)
    dqs, dks = [], []
    for hh in range(2):
        lo, hi = 64 * hh, 64 * hh + 64
        gm = head_lanes(gb, hh)
        side, middle = p_ref[hh, at(0), 0:n], p_ref[hh, at(0), n:]
        ps, pm = side.astype(F32) * scale, middle.astype(F32) * scale
        gs = jnp.where(lane > row, dot(gm, v_ref[at(0), :], NT), dot(gm, v_ref[at(2), :], NT))
        gd = dot(gm, v_ref[at(1), :], NT)
        ts, td = ps * gs, pm * gd
        total = jnp.sum(ts + td, axis=-1, keepdims=True) * (1.0 / scale)
        ds, dm = (ts - ps * total).astype(BF), (td - pm * total).astype(BF)
        for m, part in enumerate((side * ahead, middle, side * behind)):
            dvt_acc[lo:hi, at(m)] += dot(gt[lo:hi], part)

        sj, mj = dot(flip, ds), dot(flip, dm)
        right = row + lane >= n
        to_low = sheared(jnp.where(right, sj, mj), 0).astype(BF)
        to_high = sheared(jnp.where(right, mj, sj), 0).astype(BF)
        sj, mj = sj.astype(BF), mj.astype(BF)
        dq = dot(sj * above, k_ref[at(0), :]) + dot(mj, k_ref[at(1), :]) + dot(sj * below, k_ref[at(2), :])
        dqs.append(dq + dot(to_low, rk_ref[0:n]) + dot(to_high, rk_ref[n:]))
        drkt_acc[lo:hi, 0:n] += dot(qjt[lo:hi], to_low)
        drkt_acc[lo:hi, n:] += dot(qjt[lo:hi], to_high)

        st, mt = dot(flip, ds, NT), dot(flip, dm, NT)
        us, um = sheared(st, 0).astype(BF), sheared(mt, 0).astype(BF)
        st, mt = st.astype(BF), mt.astype(BF)
        high_first, low_third = us * ahead, us * behind
        low_middle, high_middle = um * ahead, um * behind
        low, high = rq_ref[0:n], rq_ref[n:]
        dks.append((
            dot(st * below, qb) + dot(high_first, high),
            dot(mt, qb) + dot(low_middle, low) + dot(high_middle, high),
            dot(st * above, qb) + dot(low_third, low),
        ))
        kjt = [kjt_ref[qt + m, lo:hi, :] for m in range(3)]
        drqt_acc[lo:hi, 0:n] += dot(kjt[1], low_middle) + dot(kjt[2], low_third)
        drqt_acc[lo:hi, n:] += dot(kjt[0], high_first) + dot(kjt[1], high_middle)
    for m in range(3):
        dk_acc[qt + m] += both_heads(dks[0][m], dks[1][m])
    return dot(flip, both_heads(*dqs).astype(BF)).astype(BF)


def bwd_masks(n, mask_ref):
    row, lane = grid_of(n)
    for m, keep in enumerate((lane >= row, lane < row, row + lane >= n, row + lane < n)):
        mask_ref[m] = jnp.where(keep, 1.0, 0.0).astype(BF)


class Mesh:
    def __init__(self, ns, nb):
        self.ns, self.nb, self.nz = ns, nb, nb // 2
        self.bits = ns.bit_length() - 1
        self.ways = 2 if ns <= 4 else 1

    def locate(self):
        self.s = lax.axis_index("seq")
        self.b = lax.axis_index("batch")
        self.z, self.c = self.b // 2, self.b % 2

    def at(self, s, b):
        return {"seq": s, "batch": b}

    def greet(self):
        barrier = pltpu.get_barrier_semaphore()
        peers = [self.at(self.s, toggled(self.b, 1))]
        peers += [self.at(self.s, toggled(self.z, step) * 2 + self.c) for step in range(1, self.nz)]
        peers += [self.at(toggled(self.s, step), self.b) for step in range(1, self.ns)]
        for peer in peers:
            pl.semaphore_signal(barrier, inc=1, device_id=peer, device_id_type=MESH)
        pl.semaphore_wait(barrier, len(peers))


class Chunk:
    def __init__(self, mesh, rows, lanes, moves, box=None, early_z=False):
        self.mesh, self.rows, self.moves, self.box, self.early_z = mesh, rows, moves, box, early_z
        unit = 128 * mesh.ways * mesh.ns
        self.lanes = -(-lanes // unit) * unit
        self.piece = self.lanes // (mesh.ways * mesh.ns)
        self.depth = 1 if early_z else mesh.nz

    def scratch(self):
        mesh, rows, lanes = self.mesh, self.rows, self.lanes
        full = pltpu.VMEM((mesh.nz, rows, lanes), BF)
        shapes = [full] if self.box else [full, full]
        for level in range(mesh.bits):
            shapes.append(pltpu.VMEM((mesh.ways, self.depth, rows, lanes // mesh.ways // 2 >> level), BF))
        wide = lanes // mesh.ways if self.early_z else self.piece
        shapes += [pltpu.VMEM((mesh.ways, mesh.nz - 1, rows, wide), BF), pltpu.VMEM((rows, lanes), BF)]
        dma = pltpu.SemaphoreType.DMA
        moves = len(self.moves)
        shapes += [] if self.box else [dma((moves,))]
        shapes += [dma((2, moves)), dma((2, 2, mesh.bits)), dma((2, 2, mesh.nz - 1)), dma((2, 2, mesh.bits))]
        return shapes

    def bind(self, refs):
        bits = self.mesh.bits
        if self.box:
            self.mine = self.box(self.mesh.c)
        else:
            self.mine, refs = refs[0], refs[1:]
        self.first = refs[0]
        self.halves = refs[1 : 1 + bits]
        self.across, self.final = refs[1 + bits : 3 + bits]
        refs = refs[3 + bits :]
        if not self.box:
            self.own_sem, refs = refs[0], refs[1:]
        self.core_sem, self.seq_sem, self.z_sem, self.out_sem = refs[:4]
        return refs[4:]

    def copy(self, src, dst, sems, index, s, b):
        return pltpu.make_async_remote_copy(
            src_ref=src,
            dst_ref=dst,
            send_sem=sems.at[(0,) + index],
            recv_sem=sems.at[(1,) + index],
            device_id=self.mesh.at(s, b),
            device_id_type=MESH,
        )

    def own_copies(self):
        for n, (source, at, size) in enumerate([] if self.box else self.moves):
            yield pltpu.make_async_copy(source(self.mesh.c), self.mine.at[:, :, pl.ds(at, size)], self.own_sem.at[n])

    def core_copies(self):
        mesh = self.mesh
        for n, (source, at, size) in enumerate(self.moves):
            yield self.copy(
                source(1 - mesh.c), self.first.at[:, :, pl.ds(at, size)], self.core_sem, (n,), mesh.s, toggled(mesh.b, 1)
            )

    def order(self, half, level):
        return (level + half) % self.mesh.bits

    def region(self, level, half):
        size = self.lanes // self.mesh.ways
        base = half * size
        sent = base
        for at in range(level):
            mine = (self.mesh.s // (1 << self.order(half, at))) % 2
            size = size // 2
            sent = base + (1 - mine) * size
            base = base + mine * size
        return base, sent, size

    def span(self, start, size):
        return pl.ds(pl.multiple_of(start, 128), size)

    def planes(self):
        return pl.ds(self.mesh.z, 1) if self.early_z else slice(None)

    def seq_copy(self, level, half):
        unused, sent, size = self.region(level + 1, half)
        return self.copy(
            self.mine.at[self.planes(), :, self.span(sent, size)],
            self.halves[level].at[half],
            self.seq_sem,
            (half, level),
            toggled(self.mesh.s, 1 << self.order(half, level)),
            self.mesh.b,
        )

    def z_region(self, half):
        kept, unused, size = self.region(0 if self.early_z else self.mesh.bits, half)
        return self.span(kept, size)

    def z_copies(self, half):
        mesh = self.mesh
        for step in range(1, mesh.nz):
            other = toggled(mesh.z, step)
            yield self.copy(
                self.mine.at[other, :, self.z_region(half)],
                self.across.at[half, step - 1],
                self.z_sem,
                (half, step - 1),
                mesh.s,
                other * 2 + mesh.c,
            )

    def out_copy(self, level, half):
        kept, unused, size = self.region(level + 1, half)
        lanes = self.span(kept, size)
        return self.copy(
            self.final.at[:, lanes],
            self.final.at[:, lanes],
            self.out_sem,
            (half, level),
            toggled(self.mesh.s, 1 << self.order(half, level)),
            self.mesh.b,
        )

    def start_core(self):
        for copy in self.core_copies():
            copy.start()
        for copy in self.own_copies():
            copy.start()

    def add_core(self):
        for copy in self.own_copies():
            copy.wait()
        for copy in self.core_copies():
            copy.wait_recv()
        parts = 4
        size = self.lanes // parts

        def add(n, carry):
            z, lanes = n // parts, self.span((n % parts) * size, size)
            self.mine[z, :, lanes] = (self.mine[z, :, lanes].astype(F32) + self.first[z, :, lanes].astype(F32)).astype(BF)
            return carry

        lax.fori_loop(0, self.mesh.nz * parts, add, 0)

    def start_seq(self, level):
        for half in range(self.mesh.ways):
            self.seq_copy(level, half).start()

    def add_seq(self, level):
        for half in range(self.mesh.ways):
            self.seq_copy(level, half).wait_recv()
            kept, unused, size = self.region(level + 1, half)
            lanes = self.span(kept, size)

            def add(n, carry):
                z = self.mesh.z if self.early_z else n
                got = self.halves[level][half, n].astype(F32)
                self.mine[z, :, lanes] = (self.mine[z, :, lanes].astype(F32) + got).astype(BF)
                return carry

            lax.fori_loop(0, self.depth, add, 0)
            if self.early_z and level == self.mesh.bits - 1:
                self.final[:, lanes] = self.mine[self.mesh.z, :, lanes]

    def end_seq(self):
        self.add_seq(1)
        for level in range(2, self.mesh.bits):
            self.start_seq(level)
            self.add_seq(level)

    def start_z(self):
        for half in range(self.mesh.ways):
            for copy in self.z_copies(half):
                copy.start()

    def add_z(self):
        z = self.mesh.z
        for half in range(self.mesh.ways):
            for copy in self.z_copies(half):
                copy.wait_recv()
            lanes = self.z_region(half)
            total = self.mine[z, :, lanes].astype(F32)
            for step in range(1, self.mesh.nz):
                total = total + self.across[half, step - 1].astype(F32)
            if self.early_z:
                self.mine[z, :, lanes] = total.astype(BF)
            else:
                self.final[:, lanes] = total.astype(BF)

    def start_out(self, level):
        for half in range(self.mesh.ways):
            self.out_copy(level, half).start()

    def core(self):
        self.start_core()

    def s0(self):
        if self.early_z:
            self.add_z()
        else:
            self.add_core()
        self.start_seq(0)

    def s1(self):
        self.add_seq(0)
        self.start_seq(1)

    def z(self):
        if self.early_z:
            self.add_core()
        else:
            self.end_seq()
        self.start_z()

    def out(self):
        if self.early_z:
            self.end_seq()
        else:
            self.add_z()
        self.start_out(self.mesh.bits - 1)

    def out2(self):
        for level in reversed(range(self.mesh.bits - 1)):
            for half in range(self.mesh.ways):
                self.out_copy(level + 1, half).wait_recv()
            self.start_out(level)

    def finish(self):
        for half in range(self.mesh.ways):
            self.out_copy(0, half).wait()
            for level in range(1, self.mesh.bits):
                self.out_copy(level, half).wait_send()
            for copy in self.z_copies(half):
                copy.wait_send()
            for level in range(self.mesh.bits):
                self.seq_copy(level, half).wait_send()
        for copy in self.core_copies():
            copy.wait_send()


class Layout:
    def __init__(self, ns, nb, width, hidden, table):
        self.mesh = mesh = Mesh(ns, nb)
        self.width, self.hidden = width, hidden
        self.rows = rows = width // nb
        self.fold = hidden // nb // rows
        self.rel_rows = table // nb
        self.pairs = width // 128
        self.third = width // 3
        self.rel_at = 384
        self.small_at = 384 + 512
        self.stack = rows // 16
        small_lanes = -(-self.pairs // self.stack) * 128
        self.split = split = hidden // 3
        whole = lambda name, lanes, early=False: self.boxed(lambda c: getattr(self, name).at[:, c], lanes, early)
        self.down = whole("down_ref", self.fold * width)
        self.into = whole("into_ref", hidden - split)
        self.rest = whole("rest_ref", split, False)
        lanes = Chunk(mesh, rows, 768 + self.third, []).lanes
        self.near = [self.boxed(lambda c, n=n: self.near_ref.at[n, :, c], lanes, n in (2,)) for n in range(3)]
        self.far = whole("far_ref", self.small_at + small_lanes)
        self.chunks = [self.down, self.into, self.rest, *self.near, self.far]

    def boxed(self, box, lanes, early=False):
        chunk = Chunk(self.mesh, self.rows, lanes, [], early_z=early)
        chunk.box, chunk.moves = box, [(box, 0, chunk.lanes)]
        return chunk

    def starts(self):
        at = 0
        for chunk in self.chunks:
            yield at
            at += chunk.lanes

    def scratch(self):
        mesh = self.mesh
        box = lambda lanes: pltpu.VMEM((mesh.nz, 2, self.rows, lanes), BF)
        shapes = [box(chunk.lanes) for chunk in (self.down, self.into, self.rest, self.far)]
        shapes.append(pltpu.VMEM((3, mesh.nz, 2, self.rows, self.near[0].lanes), BF))
        for chunk in self.chunks:
            shapes += chunk.scratch()
        return shapes

    def bind(self, refs):
        self.mesh.locate()
        self.down_ref, self.into_ref, self.rest_ref, self.far_ref, self.near_ref = refs[:5]
        refs = refs[5:]
        for chunk in self.chunks:
            refs = chunk.bind(refs)
        return refs

    def store_down(self, m, grads):
        rows, share = self.rows, self.rows * self.fold
        for n in range(self.width // rows):
            b, part = divmod(m * self.width + n * rows, share)
            lanes = slice(part // rows * self.width, (part // rows + 1) * self.width)
            self.down_ref[b // 2, b % 2, :, lanes] = grads[n * rows : (n + 1) * rows]

    def store_into(self, m, grads):
        rows, split = self.rows, self.split
        ref, lanes = (self.rest_ref, slice(0, split)) if m == 0 else (self.into_ref, slice((m - 1) * split, m * split))
        for b in range(self.mesh.nb):
            ref[b // 2, b % 2, :, lanes] = grads[b * rows : (b + 1) * rows]

    def store_out(self, grads):
        rows, third = self.rows, self.third
        for b in range(self.mesh.nb):
            for n in range(3):
                part = grads[b * rows : (b + 1) * rows, n * third : (n + 1) * third]
                self.near_ref[n, b // 2, b % 2, :, 768 : 768 + third] = part

    def store_pair(self, pair, grads):
        rows = self.rows
        box = pair // 2
        lanes = pl.ds(pl.multiple_of((pair % 2) * 384, 128), 384)

        @pl.when(pair < self.pairs - 1)
        def _():
            for b in range(self.mesh.nb):
                self.near_ref[box, b // 2, b % 2, :, lanes] = grads[b * rows : (b + 1) * rows]

        @pl.when(pair == self.pairs - 1)
        def _():
            for b in range(self.mesh.nb):
                self.far_ref[b // 2, b % 2, :, 0:384] = grads[b * rows : (b + 1) * rows]

    def store_rest(self, rel, vectors):
        take, at, half = self.rel_rows, self.rel_at, self.rel_rows // 2
        for b in range(self.mesh.nb):
            part = rel[b * take : (b + 1) * take]
            put = self.far_ref.at[b // 2, b % 2]
            put[0:take, at : at + 512] = part[:, 0:512]
            put[take : take + half, at : at + 256] = part[0:half, 512:768]
            put[take : take + half, at + 256 : at + 512] = part[half:, 512:768]
            for n in range(self.pairs):
                row, lane = (n % self.stack) * 16, self.small_at + (n // self.stack) * 128
                put[row : row + 16, lane : lane + 128] = vectors[:, n * 128 : (n + 1) * 128]

    def schedule(self):
        down, into, rest, one, two, three, far = self.chunks

        steps = {
            1: [rest.s0],
            2: [into.s0],
            4: [down.s0],
            8: [into.s1],
            9: [rest.s1],
            10: [down.s1, one.core],
            11: [into.z],
            12: [rest.z, one.s0, two.core],
            13: [two.s0, down.z],
            14: [one.s1],
            15: [three.core, into.out],
            16: [three.z, into.out2, two.s1],
            17: [rest.out],
        }
        last = [
            far.core,
            far.s0,
            three.s0,
            one.z,
            down.out,
            far.s1,
            two.z,
            one.out,
            three.s1,
            down.out2,
            far.z,
            rest.out2,
            three.out,
            two.out,
            one.out2,
            far.out,
            two.out2,
            three.out2,
            far.out2,
        ]
        last += [chunk.finish for chunk in self.chunks]
        return steps, last


class Edges:
    def __init__(self, mesh, refs):
        self.mesh = mesh
        self.sent, self.got, self.sems = refs

    def copy(self, side):
        other = self.mesh.s + (2 * side - 1)
        return pltpu.make_async_remote_copy(
            src_ref=self.sent.at[side],
            dst_ref=self.got.at[1 - side],
            send_sem=self.sems.at[0, side],
            recv_sem=self.sems.at[1, 1 - side],
            device_id=self.mesh.at(other, self.mesh.b),
            device_id_type=MESH,
        )

    def has(self, side):
        return self.mesh.s > 0 if side == 0 else self.mesh.s < self.mesh.ns - 1

    def start(self):
        for side in range(2):
            pl.when(self.has(side))(lambda side=side: self.copy(side).start())

    def finish(self, add):
        for side in range(2):

            @pl.when(self.has(side))
            def _(side=side):
                self.copy(side).wait_send()
                self.copy(1 - side).wait_recv()
                add(side, self.got[side])


def bwd_kernel(tq, scale, layout, q_ref, k_ref, v_ref, g_ref, rk_ref, rq_ref, p_ref, wk_ref, wq_ref, wv_ref,
               act_hbm, branch_ref, hidden_ref, pre_hbm, ctx_hbm, attn_hbm, g_one_hbm, xt_hbm, picks_ref, small_ref, *rest):
    (dx_ref, packed_hbm,
               mask_ref, kjt_ref, dk_acc, dvt_acc, drkt_acc, drqt_acc,
               xt_ref, d_ref, rel_acc, vec_ref, dx_acc, sent_ref, got_ref, edge_sem,
     load_ref, load_sem, side_sem, packed_sem, *refs) = rest
    block = q_ref.shape[0]
    nq = block // tq
    ext = k_ref.shape[0]
    nk = ext // tq
    span = tq
    table = 2 * span
    pair = pl.program_id(0)
    pairs = layout.pairs
    flip = anti(tq)
    layout.bind(refs)
    edges = Edges(layout.mesh, (sent_ref, got_ref, edge_sem))
    steps, last = layout.schedule()

    def run(actions):
        def all_of():
            for action in actions:
                action()
        return all_of

    loads = [act_hbm.at[:, pl.ds(m * layout.width, layout.width)] for m in range(layout.fold)]
    loads += [pre_hbm.at[:, pl.ds(m * layout.split, layout.split)] for m in range(3)]
    loads += [ctx_hbm, attn_hbm]

    def load(m):
        size = loads[m].shape
        return pltpu.make_async_copy(loads[m], load_ref.at[m % 3, pl.ds(0, size[0]), pl.ds(0, size[1])], load_sem.at[m % 3])

    def loaded(m):
        size = loads[m].shape
        load(m).wait()
        return load_ref[m % 3, 0 : size[0], 0 : size[1]]

    def dx_copy():
        return pltpu.make_async_copy(g_one_hbm, dx_ref, side_sem.at[0])

    def xt_copy():
        return pltpu.make_async_copy(xt_hbm, xt_ref, side_sem.at[1])

    @pl.when(pair == 0)
    def _():
        for m in range(2):
            load(m).start()
        layout.mesh.greet()
        m = 0
        for n in range(layout.fold):
            load(m + 2).start()
            layout.store_down(n, dot(loaded(m), branch_ref[...], TN).astype(BF))
            m += 1
        layout.down.core()
        for n in range(3):
            if m + 2 < len(loads):
                load(m + 2).start()
            layout.store_into(n, dot(hidden_ref[...], loaded(m), TN).astype(BF))
            if n == 0:
                layout.rest.core()
            m += 1
        xt_copy().start()
        dx_copy().start()
        layout.into.core()
        run(steps.get(0, []))()
        layout.store_out(dot(loaded(m), loaded(m + 1), TN).astype(BF))
        bwd_masks(tq, mask_ref)
        d_ref[...] = jnp.zeros_like(d_ref)
        rel_acc[...] = jnp.zeros_like(rel_acc)
        dx_acc[...] = jnp.zeros_like(dx_acc)
        vec_ref[...] = small_ref[...]

    for kt in range(nk):
        kjt_ref[kt] = dot(k_ref[kt * tq : (kt + 1) * tq, :], flip, TN).astype(BF)
    dk_acc[...] = jnp.zeros_like(dk_acc)
    dvt_acc[...] = jnp.zeros_like(dvt_acc)
    drkt_acc[...] = jnp.zeros_like(drkt_acc)
    drqt_acc[...] = jnp.zeros_like(drqt_acc)

    def tile(qt, carry):
        for step, actions in steps.items():
            if step and step % 3 < min(nq, 2):
                pl.when((pair == step // 3) & (qt == step % 3))(run(actions))
        row = pl.multiple_of(qt * tq, tq)
        dq = bwd_tile(
            tq, scale, qt, q_ref, k_ref, v_ref, g_ref, rk_ref, rq_ref, p_ref, mask_ref, kjt_ref, dk_acc, dvt_acc, drkt_acc, drqt_acc
        )
        d_ref[pl.ds(span + row, tq), 0:128] = dq
        return carry

    lax.fori_loop(0, nq, tile, 0)
    for step, actions in steps.items():
        if step % 3 >= min(nq, 2):
            pl.when(pair == step // 3)(run(actions))
    for kt in range(nk):
        here = slice(kt * tq, (kt + 1) * tq)
        dk = dot(flip, dk_acc[kt].astype(BF)).astype(BF)
        dv = dvt_acc[:, here].T.astype(BF)
        d_ref[here, 128:256] = dk
        d_ref[here, 256:384] = dv
    for st in range(table // 128):
        here = slice(ext + st * 128, ext + (st + 1) * 128)
        d_ref[here, 0:128] = drqt_acc[:, st * 128 : (st + 1) * 128].T.astype(BF)
        d_ref[here, 128:256] = drkt_acc[:, st * 128 : (st + 1) * 128].T.astype(BF)

    weights = jnp.concatenate([wq_ref[...], wk_ref[...], wv_ref[...]], axis=1)
    dx_acc[...] += dot(d_ref[0:ext], weights, NT)

    @pl.when(pair == pairs - 1)
    def _():
        sent_ref[0] = dx_acc[0:span].astype(BF)
        sent_ref[1] = dx_acc[ext - span :].astype(BF)
        edges.start()

    pl.when(pair == 0)(lambda: xt_copy().wait())
    grads = dot(xt_ref[...], d_ref[...]).astype(BF)
    layout.store_pair(pair, grads)
    rel_acc[...] += dot(d_ref[ext:, 0:128], wq_ref[...], NT) + dot(d_ref[ext:, 128:256], wk_ref[...], NT)
    sums = dot(jnp.ones((8, ext + table), BF), d_ref[...])[0:1]
    for n in range(3):
        vec_ref[10 + n : 11 + n, pl.ds(pl.multiple_of(pair * 128, 128), 128)] = sums[:, n * 128 : (n + 1) * 128]

    @pl.when(pair == pairs - 1)
    def _():
        rel = dot(picks_ref[...], rel_acc[...].astype(BF)).astype(BF)
        layout.store_rest(rel, vec_ref[...].astype(BF))
        run(last[:1])()
        dx_copy().wait()
        dx_ref[...] += dx_acc[span : span + block]
        run(last[1:])()

        packed_copies = []
        for n, (at, chunk) in enumerate(zip(layout.starts(), layout.chunks)):
            packed_copies.append(pltpu.make_async_copy(chunk.final, packed_hbm.at[:, pl.ds(at, chunk.lanes)], packed_sem.at[n]))
            packed_copies[-1].start()

        def take(side, rows):
            here = slice(0, span) if side == 0 else slice(block - span, block)
            dx_ref[here] += rows.astype(F32)

        edges.finish(take)
        for copy in packed_copies:
            copy.wait()


def attn_bwd(span, q, k, v, g, rk, rq, probs, w_key, w_query, w_value, act, branch, hidden, pre, context, g_attn, g_one, xt, picks, small):
    block, width = q.shape
    ext = k.shape[0]
    table = 2 * span
    scale = (3.0 * 64) ** -0.5
    ns, nb = lax.axis_size("seq"), lax.axis_size("batch")
    layout = Layout(ns, nb, width, act.shape[1], table)
    col = lambda rows: pl.BlockSpec((rows, 128), lambda h: (0, h))
    whole = lambda shape: pl.BlockSpec(shape, lambda h: (0, 0), pipeline_mode=pl.Buffered(1))
    any_spec = pl.BlockSpec(memory_space=pltpu.HBM)
    packed = jax.ShapeDtypeStruct((layout.rows, sum(chunk.lanes for chunk in layout.chunks)), BF)
    outs = pl.pallas_call(
        functools.partial(bwd_kernel, span, scale, layout),
        grid=(width // 128,),
        out_shape=(
            jax.ShapeDtypeStruct((block, width), F32),
            packed,
        ),
        in_specs=[col(block), col(ext), col(ext), col(block), col(rk.shape[0]), col(rq.shape[0]),
                  pl.BlockSpec((2, block, table), lambda h: (h, 0, 0)), col(width), col(width), col(width),
                  any_spec, whole(branch.shape), whole(hidden.shape), any_spec, any_spec, any_spec, any_spec, any_spec,
                  whole(picks.shape), whole(small.shape)],
        out_specs=(whole((block, width)), any_spec),
        scratch_shapes=[
            pltpu.VMEM((4, span, span), BF),
            pltpu.VMEM((ext // span, 128, span), BF),
            pltpu.VMEM((ext // span, span, 128), F32),
            pltpu.VMEM((128, ext), F32),
            pltpu.VMEM((128, table), F32),
            pltpu.VMEM((128, table), F32),
            pltpu.VMEM((width, ext + table), BF),
            pltpu.VMEM((ext + table, 384), BF),
            pltpu.VMEM((table, width), F32),
            pltpu.VMEM((16, width), F32),
            pltpu.VMEM((ext, width), F32),
            pltpu.VMEM((2, span, width), BF),
            pltpu.VMEM((2, span, width), BF),
            pltpu.SemaphoreType.DMA((2, 2)),
            pltpu.VMEM((3, block, layout.split), BF),
            pltpu.SemaphoreType.DMA((3,)),
            pltpu.SemaphoreType.DMA((2,)),
            pltpu.SemaphoreType.DMA((len(layout.chunks),)),
        ] + layout.scratch(),
        compiler_params=pltpu.CompilerParams(collective_id=0, has_side_effects=True, vmem_limit_bytes=60 << 20),
        cost_estimate=pl.CostEstimate(flops=50_000_000_000, bytes_accessed=20 << 20, transcendentals=0),
        name="attn_bwd_reduce",
    )(*[pltpu.with_memory_space_constraint(arg, pltpu.HBM) for arg in (q, k, v)], g, *[pltpu.with_memory_space_constraint(arg, pltpu.HBM) for arg in (rk, rq, probs)], w_key, w_query, w_value, act, branch, hidden, pre, context, g_attn, g_one, pltpu.with_memory_space_constraint(xt, pltpu.HBM), picks, small)
    return layout, outs


def unpack_kernel(layout, packed_hbm, dx_hbm,
                  dx_out, down_out, into_out, out_out, query_out, key_out, value_out, rel_out, *refs):
    vec_outs, wide_out, (packed_ref, rel_ref, vec_ref, sems) = refs[:-5], refs[-5], refs[-4:]
    packed_copy = pltpu.make_async_copy(packed_hbm, packed_ref, sems.at[0])
    dx_copy = pltpu.make_async_copy(dx_hbm, dx_out, sems.at[1])
    packed_copy.start()
    dx_copy.start()
    packed_copy.wait()
    rows, width, pairs = layout.rows, layout.width, layout.pairs
    parts = [packed_ref.at[:, at : at + chunk.lanes] for at, chunk in zip(layout.starts(), layout.chunks)]
    down_ref, into_ref, rest_ref, *near, far_ref = parts
    split = layout.hidden // 3
    into_out[:, :split] = rest_ref[:, :split].astype(F32)
    into_out[:, split:] = into_ref[:, : layout.hidden - split].astype(F32)
    for n in range(layout.fold):
        down_out[n * rows : (n + 1) * rows, :] = down_ref[:, n * width : (n + 1) * width].astype(F32)
    for n, side in enumerate(near):
        out_out[:, n * layout.third : (n + 1) * layout.third] = side[:, 768 : 768 + layout.third].astype(F32)
    for m in range(pairs):
        side, at = (far_ref, 0) if m == pairs - 1 else (near[m // 2], m % 2 * 384)
        for n, out in enumerate((query_out, key_out, value_out)):
            out[:, m * 128 : (m + 1) * 128] = side[:, at + n * 128 : at + (n + 1) * 128].astype(F32)
    take, at, half = layout.rel_rows, layout.rel_at, layout.rel_rows // 2
    rel_ref[:, 0:512] = far_ref[0:take, at : at + 512].astype(F32)
    for n in range(2):
        rel_ref[n * half : (n + 1) * half, 512:768] = far_ref[take : take + half, at + n * 256 : at + (n + 1) * 256].astype(F32)
    own = take // layout.mesh.ns
    rel_out[...] = pltpu.roll(rel_ref[...], take - lax.axis_index("seq") * own, 0)[:own]
    for n in range(pairs):
        row, lane = (n % layout.stack) * 16, layout.small_at + (n // layout.stack) * 128
        vec_ref[:, n * 128 : (n + 1) * 128] = far_ref[row : row + 16, lane : lane + 128].astype(F32)
    b = lax.axis_index("batch")
    mine = pltpu.roll(vec_ref[...], width - b * rows, 1)
    for out, n in zip(vec_outs, (0, 1, 2, 3, 4, 5, 10, 11, 12)):
        out[...] = mine[n, :rows]
    wide = wide_out.shape[0]
    fit = width // wide
    line = pltpu.roll(pltpu.roll(vec_ref[...], width - (b % fit) * wide, 1), 10 - b // fit, 0)
    wide_out[...] = line[0, :wide]
    dx_copy.wait()


def unpack(layout, packed, dx):
    rows, width = layout.rows, layout.width
    shape = lambda *dims: jax.ShapeDtypeStruct(dims, F32)
    shapes = [shape(*dx.shape), shape(layout.fold * rows, width), shape(rows, layout.hidden)] + [shape(rows, width)] * 4
    shapes += [shape(layout.rel_rows // layout.mesh.ns, width)] + [shape(rows)] * 9 + [shape(layout.fold * rows)]
    vmem, far = pl.BlockSpec(memory_space=pltpu.VMEM), pl.BlockSpec(memory_space=pltpu.HBM)
    return pl.pallas_call(
        functools.partial(unpack_kernel, layout),
        out_shape=shapes,
        in_specs=[far, far],
        out_specs=[vmem] * len(shapes),
        scratch_shapes=[
            pltpu.VMEM(packed.shape, BF),
            pltpu.VMEM((layout.rel_rows, width), F32),
            pltpu.VMEM((16, width), F32),
            pltpu.SemaphoreType.DMA((2,)),
        ],
        compiler_params=pltpu.CompilerParams(vmem_limit_bytes=32 << 20),
        name="unpack",
    )(*[pltpu.with_memory_space_constraint(arg, pltpu.HBM) for arg in (packed, dx)])


NORM_EPS = 1e-07
STEP = 1536


def mid_kernel(ctx_ref, x_ref, cot_ref, b_out, gain_attn, shift_attn, b_in, b_down, gain_ffn, shift_ffn, w_out_hbm, w_in_hbm, w_down_hbm,
               out_ref, branch_ref, hidden_ref, gone_ref, gattn_ref, gctx_ref, vec_ref, act_hbm, pre_hbm,
               w_out_ref, w_in_ref, w_down_ref, act_ref, pre_ref, slope_ref, full_ref, normed_ref, inv_ref, acc_ref, line_ref, in_sem, out_sem):
    block, width = x_ref.shape
    wide = w_in_ref.shape[1]
    parts = wide // width
    loads = [(w_out_hbm, w_out_ref)]
    for n in range(parts):
        loads.append((w_in_hbm.at[:, pl.ds(n * width, width)], w_in_ref.at[:, pl.ds(n * width, width)]))
    loads.append((w_down_hbm, w_down_ref))
    row_of = lambda ref: ref[...].astype(F32)[None]
    total = lambda values: jnp.sum(values, axis=0, keepdims=True)
    mean = lambda values: jnp.mean(values, axis=-1, keepdims=True)

    def load(n):
        return pltpu.make_async_copy(*loads[n], in_sem.at[n])

    def norm(values):
        centred = values - mean(values)
        inv = lax.rsqrt(mean(centred * centred) + NORM_EPS)
        return centred * inv, inv

    def norm_back(grads, normed, inv):
        return inv * (grads - mean(grads) - normed * mean(grads * normed))

    for n in range(len(loads)):
        load(n).start()
    blocks = [slice(n, n + 128) for n in range(0, block, 128)]
    load(0).wait()
    for rows in blocks:
        normed, inv = norm(x_ref[rows].astype(F32) + dot(ctx_ref[rows], w_out_ref[...]) + row_of(b_out))
        normed_ref[rows], inv_ref[rows] = normed, inv
        hidden = normed * row_of(gain_attn) + row_of(shift_attn)
        full_ref[rows] = hidden
        hidden_ref[rows] = hidden.astype(BF)
    for n in range(1, len(loads)):
        load(n).wait()
    acc_ref[...] = full_ref[...] + row_of(b_down)

    def up(n, carry):
        cols = pl.ds(pl.multiple_of(n * STEP, STEP), STEP)
        pre = dot(hidden_ref[...], w_in_ref[:, cols]) + b_in[cols].astype(F32)[None]
        phi = 0.5 + 0.5 * lax.erf(pre * (0.5**0.5))
        act = (pre * phi).astype(BF)
        act_ref[:, cols] = act
        slope_ref[:, cols] = phi + pre * (jnp.exp(-0.5 * pre * pre) * ((2.0 * math.pi) ** -0.5))
        acc_ref[...] += dot(act, w_down_ref[cols, :])
        return carry

    lax.fori_loop(0, wide // STEP, up, 0, unroll=1)
    act_copy = pltpu.make_async_copy(act_ref, act_hbm, out_sem.at[0])
    act_copy.start()
    gain, shift, bias = 0.0, 0.0, 0.0
    for rows in blocks:
        normed, inv = norm(acc_ref[rows])
        out_ref[rows] = (normed * row_of(gain_ffn) + row_of(shift_ffn)).astype(BF)
        grads = cot_ref[rows].astype(F32)
        gain, shift = gain + total(grads * normed), shift + total(grads)
        grad_two = norm_back(grads * row_of(gain_ffn), normed, inv)
        acc_ref[rows] = grad_two
        branch = grad_two.astype(BF)
        branch_ref[rows] = branch
        bias = bias + total(branch.astype(F32))
    vec_ref[...] = jnp.zeros_like(vec_ref)
    vec_ref[3:4], vec_ref[4:5], vec_ref[5:6] = bias, gain, shift

    def down(n, carry):
        cols = pl.ds(pl.multiple_of(n * STEP, STEP), STEP)
        pre = (dot(branch_ref[...], w_down_ref[cols, :], NT) * slope_ref[:, cols]).astype(BF)
        pre_ref[:, cols] = pre
        line_ref[0:1, cols] = total(pre.astype(F32))
        acc_ref[...] += dot(pre, w_in_ref[:, cols], NT)
        return carry

    lax.fori_loop(0, wide // STEP, down, 0, unroll=1)
    pre_copy = pltpu.make_async_copy(pre_ref, pre_hbm, out_sem.at[1])
    pre_copy.start()
    for n in range(parts):
        vec_ref[6 + n : 7 + n] = line_ref[0:1, n * width : (n + 1) * width]
    gain, shift, bias = 0.0, 0.0, 0.0
    for rows in blocks:
        grads, normed = acc_ref[rows], normed_ref[rows]
        gain, shift = gain + total(grads * normed), shift + total(grads)
        grad_one = norm_back(grads * row_of(gain_attn), normed, inv_ref[rows])
        gone_ref[rows] = grad_one
        grad_attn = grad_one.astype(BF)
        gattn_ref[rows] = grad_attn
        bias = bias + total(grad_attn.astype(F32))
        gctx_ref[rows] = dot(grad_attn, w_out_ref[...], NT).astype(BF)
    vec_ref[0:1], vec_ref[1:2], vec_ref[2:3] = bias, gain, shift
    act_copy.wait()
    pre_copy.wait()


def middle(context, x, cotangent, small, w_out, w_in, w_down):
    block, width = x.shape
    wide = w_in.shape[1]
    far = pl.BlockSpec(memory_space=pltpu.HBM)
    whole = lambda arg: pl.BlockSpec(arg.shape, lambda t: (0,) * len(arg.shape), pipeline_mode=pl.Buffered(1))
    tall = (block, width)
    args = [context, x, cotangent, *small]
    outs = [jax.ShapeDtypeStruct(tall, BF)]
    outs += [pltpu.HBM(dims, kind) for dims, kind in ((tall, BF), (tall, BF), (tall, F32), (tall, BF), (tall, BF), ((16, width), F32))]
    return pl.pallas_call(
        mid_kernel,
        grid=(1,),
        out_shape=outs + [pltpu.HBM((block, wide), BF)] * 2,
        in_specs=[whole(arg) for arg in args] + [far] * 3,
        out_specs=[whole(out) for out in outs] + [far] * 2,
        scratch_shapes=[
            pltpu.VMEM((width, width), BF),
            pltpu.VMEM((width, wide), BF),
            pltpu.VMEM((wide, width), BF),
            pltpu.VMEM((block, wide), BF),
            pltpu.VMEM((block, wide), BF),
            pltpu.VMEM((block, wide), F32),
            pltpu.VMEM(tall, F32),
            pltpu.VMEM(tall, F32),
            pltpu.VMEM((block, 1), F32),
            pltpu.VMEM(tall, F32),
            pltpu.VMEM((8, wide), F32),
            pltpu.SemaphoreType.DMA((2 + wide // width,)),
            pltpu.SemaphoreType.DMA((2,)),
        ],
        compiler_params=pltpu.CompilerParams(vmem_limit_bytes=56 << 20),
        name="middle",
    )(*args, *[pltpu.with_memory_space_constraint(arg, pltpu.HBM) for arg in (w_out, w_in, w_down)])


def local(
    layer_input,
    w_query,
    b_query,
    w_key,
    b_key,
    w_value,
    b_value,
    w_out,
    b_out,
    gain_attn,
    shift_attn,
    w_in,
    b_in,
    w_down,
    b_down,
    gain_ffn,
    shift_ffn,
    rel_table,
    segment_ids,
    cotangent,
):
    rows, block, width = layer_input.shape
    span = rel_table.shape[0] // 2
    x = layer_input[0]
    start = lax.axis_index("seq") * block
    padded = jnp.pad(segment_ids[0], (span, span), constant_values=-1)
    kid = lax.dynamic_slice_in_dim(padded, start, block + 2 * span, 0)
    qid = kid[span : span + block]
    context, probs, q, k, v, rk, rq, xt = attn_fwd(
        span, x, rel_table, w_query, w_key, w_value, b_query, b_key, b_value, qid[:, None], kid[None]
    )

    output, grad_branch, hidden_low, grad_one, grad_attn, grad_context, small, act_low, grad_pre = middle(
        context, x, cotangent[0], [b_out, gain_attn, shift_attn, b_in, b_down, gain_ffn, shift_ffn], w_out, w_in, w_down
    )
    share, lanes = lax.axis_size("batch"), lax.axis_size("seq")
    rel_rows = 2 * span // (share * lanes)
    order = np.arange(2 * span).reshape(lanes, share, rel_rows).transpose(1, 0, 2).reshape(-1)
    picks = jnp.asarray((2 * span - 1 - order)[:, None] == np.arange(2 * span)[None], BF)
    layout, outs = attn_bwd(
        span, q, k, v, grad_context, rk, rq, probs, w_key, w_query, w_value, act_low, grad_branch, hidden_low, grad_pre,
        context, grad_attn, grad_one, xt, picks, small,
    )
    input_grad, packed = outs
    input_grad, down_sum, in_sum, out_sum, query_sum, key_sum, value_sum, rel_sum, *vectors = unpack(layout, packed, input_grad)
    ob, ga, sa, db, gf, sf, qb, kb, vb, ib = vectors
    return (
        output[None], input_grad[None], query_sum, qb, key_sum, kb, value_sum, vb, out_sum, ob,
        ga, sa, in_sum, ib, down_sum, db, gf, sf, rel_sum,
    )


def solution(mesh):
    tokens = P("batch", "seq", None)
    in_specs = (tokens,) + (P(),) * 17 + (P("batch", None), tokens)
    matrix, vector = P("batch", None), P("batch")
    out_specs = (
        (tokens, tokens)
        + (matrix, vector) * 4
        + (vector, vector)
        + (matrix, vector) * 2
        + (vector, vector, P(("seq", "batch"), None))
    )
    return jax.shard_map(local, mesh=mesh, in_specs=in_specs, out_specs=out_specs, check_vma=False)
```

```python
import functools
import math

import jax
import jax.numpy as jnp
import numpy as np
from jax import lax
from jax.experimental import pallas as pl
from jax.experimental.pallas import tpu as pltpu
from jax.sharding import PartitionSpec as P

F32 = jnp.float32
BF = jnp.bfloat16
NN = (((1,), (0,)), ((), ()))
NT = (((1,), (1,)), ((), ()))
TN = (((0,), (0,)), ((), ()))
MESH = pl.DeviceIdType.MESH


def toggled(value, mask):
    out = value
    for bit in range(mask.bit_length()):
        if mask >> bit & 1:
            out = out + (1 - 2 * ((value // (1 << bit)) % 2)) * (1 << bit)
    return out


def dot(a, b, dims=NN):
    return lax.dot_general(a, b, dims, preferred_element_type=F32)


def head_lanes(x, hh):
    lane = lax.broadcasted_iota(jnp.int32, x.shape, len(x.shape) - 1)
    keep = (lane < 64) if hh == 0 else (lane >= 64)
    return jnp.where(keep, x.astype(F32), 0.0).astype(x.dtype)


def both_heads(first, second):
    lane = lax.broadcasted_iota(jnp.int32, first.shape, 1)
    return jnp.where(lane < 64, first, second)


def grid_of(n):
    return lax.broadcasted_iota(jnp.int32, (n, n), 0), lax.broadcasted_iota(jnp.int32, (n, n), 1)


def anti(n):
    row, lane = grid_of(n)
    return jnp.where(row + lane == n - 1, 1.0, 0.0).astype(BF)


def sheared(x, shift):
    return pltpu.roll(x, shift, 1, stride=1, stride_axis=0)


def fwd_tile(n, scale, pair, qt, q_ref, k_ref, v_ref, rk_ref, rqm_ref, bias_ref, mask_ref, p_ref):
    factor = scale * math.log2(math.e)
    row, lane = grid_of(n)
    right, upper = lane > row, row + lane >= n - 1
    lanes = pl.ds(pl.multiple_of(pair * 128, 128), 128)
    at = lambda m: (pl.ds(pl.multiple_of((qt + m) * n, n), n), lanes)
    qb = q_ref[at(0)]
    rk_low, rk_high = rk_ref[0:n, lanes], rk_ref[n:, lanes]
    outs = []
    for hh in range(2):
        qm = head_lanes(qb, hh)
        low, high = rqm_ref[hh, 0:n, lanes], rqm_ref[hh, n:, lanes]
        to_low = sheared(dot(qm, rk_low, NT), 1)
        to_high = sheared(dot(qm, rk_high, NT), 1)
        side = jnp.where(right, dot(qm, k_ref[at(0)], NT) + to_low, dot(qm, k_ref[at(2)], NT) + to_high)
        middle = dot(qm, k_ref[at(1)], NT) + jnp.where(right, to_high, to_low)
        key_side = jnp.where(upper, dot(k_ref[at(0)], high, NT), dot(k_ref[at(2)], low, NT))
        key_middle = jnp.where(upper, dot(k_ref[at(1)], low, NT), dot(k_ref[at(1)], high, NT))
        side = (side + sheared(key_side, 1).T) * factor + bias_ref[:, 0:n]
        middle = (middle + sheared(key_middle, 1).T) * factor + bias_ref[:, n:]
        top = jnp.max(jnp.maximum(side, middle), axis=-1, keepdims=True)
        side, middle = jnp.exp2(side - top), jnp.exp2(middle - top)
        inverse = 1.0 / jnp.sum(side + middle, axis=-1, keepdims=True)
        side, middle = (side * inverse).astype(BF), (middle * inverse).astype(BF)
        p_ref[hh, :, 0:n] = side
        p_ref[hh, :, n:] = middle
        out = dot(side * mask_ref[0], v_ref[at(0)]) + dot(middle, v_ref[at(1)])
        outs.append(out + dot(side * mask_ref[1], v_ref[at(2)]))
    return both_heads(*outs).astype(BF)


class Halo:
    def __init__(self, span, block, ext_ref, sems):
        self.span, self.block, self.ext_ref, self.sems = span, block, ext_ref, sems
        self.s, self.b, self.ns = lax.axis_index("seq"), lax.axis_index("batch"), lax.axis_size("seq")

    def greet(self):
        barrier = pltpu.get_barrier_semaphore()
        for step in range(1, self.ns):
            peer = {"seq": toggled(self.s, step), "batch": self.b}
            pl.semaphore_signal(barrier, inc=1, device_id=peer, device_id_type=MESH)
        pl.semaphore_wait(barrier, self.ns - 1)

    def copy(self, up):
        span, block = self.span, self.block
        src, dst = (block, 0) if up else (span, span + block)
        return pltpu.make_async_remote_copy(
            src_ref=self.ext_ref.at[pl.ds(src, span)],
            dst_ref=self.ext_ref.at[pl.ds(dst, span)],
            send_sem=self.sems.at[0, int(up)],
            recv_sem=self.sems.at[1, int(up)],
            device_id={"seq": self.s + (1 if up else -1), "batch": self.b},
            device_id_type=MESH,
        )

    def sends(self, up):
        return self.s < self.ns - 1 if up else self.s > 0

    def gets(self, up):
        return self.s > 0 if up else self.s < self.ns - 1

    def start(self, up):
        pl.when(self.sends(up))(lambda: self.copy(up).start())

    def wait(self, up):
        at = pl.ds(0 if up else self.span + self.block, self.span)
        pl.when(self.gets(up))(lambda: self.copy(up).wait_recv())

        @pl.when(jnp.logical_not(self.gets(up)))
        def _():
            self.ext_ref[at] = jnp.zeros((self.span, self.ext_ref.shape[1]), BF)

    def finish(self):
        for up in (True, False):
            pl.when(self.sends(up))(lambda up=up: self.copy(up).wait_send())


def fwd_kernel(n, scale, x_hbm, rel_hbm, wk_hbm, wq_hbm, wv_hbm, bq_ref, bk_ref, bv_ref, qid_ref, kid_ref,
               ctx_ref, p_ref, q_out, k_out, v_out, rk_out, rq_out, xt_out,
               q_ref, k_ref, v_ref, rk_ref, rq_ref, xt_ref, ext_ref, rel_ref, flip_ref, wk_ref, wq_ref, wv_ref,
               rqm_ref, bias_ref, mask_ref, halo_sem, in_sem, out_sem):
    block = x_hbm.shape[0]
    ext = block + 2 * n
    qt, pair = pl.program_id(0), pl.program_id(1)
    last = (qt == pl.num_programs(0) - 1) & (pair == pl.num_programs(1) - 1)
    halo = Halo(n, block, ext_ref, halo_sem)
    row, lane = grid_of(n)
    bias_of = lambda ref: ref[...].astype(F32)[None]
    own = slice(n, n + block)
    kept = ((q_ref, q_out), (rk_ref, rk_out), (rq_ref, rq_out), (k_ref, k_out), (v_ref, v_out), (xt_ref, xt_out))
    loads = ((x_hbm, ext_ref.at[pl.ds(n, block)]), (rel_hbm, rel_ref), (wk_hbm, wk_ref), (wq_hbm, wq_ref), (wv_hbm, wv_ref))

    def load(m):
        return pltpu.make_async_copy(*loads[m], in_sem.at[m])

    def keep(first, end):
        for m in range(first, end):
            yield pltpu.make_async_copy(*kept[m], out_sem.at[m])

    def keys(rows):
        k_ref[rows] = (dot(ext_ref[rows], wk_ref[...]) + bias_of(bk_ref)).astype(BF)
        v_ref[rows] = (dot(ext_ref[rows], wv_ref[...]) + bias_of(bv_ref)).astype(BF)

    def turn(ref, first, size, at):
        for m in range(0, size, 128):
            xt_ref[:, at + m : at + m + 128] = ref[first + m : first + m + 128, :].astype(F32).T.astype(BF)

    def get_after():
        halo.wait(False)
        keys(slice(n + block, ext))
        turn(ext_ref, n + block, n, n + block)
        for copy in keep(3, 6):
            copy.start()

    @pl.when((qt == 0) & (pair == 0))
    def _():
        for m in range(5):
            load(m).start()
        halo.greet()
        load(0).wait()
        halo.start(True)
        load(1).wait()
        flip_ref[...] = dot(anti(2 * n), rel_ref[...]).astype(BF)
        load(2).wait()
        rk_ref[...] = (dot(flip_ref[...], wk_ref[...]) + bias_of(bk_ref)).astype(BF)
        load(3).wait()
        rq_ref[...] = (dot(flip_ref[...], wq_ref[...]) + bias_of(bq_ref)).astype(BF)
        q_ref[...] = (dot(ext_ref[own], wq_ref[...]) + bias_of(bq_ref)).astype(BF)
        for copy in keep(0, 3):
            copy.start()
        load(4).wait()
        keys(own)
        head = (lax.broadcasted_iota(jnp.int32, rq_ref.shape, 1) // 64) % 2
        for hh in range(2):
            rqm_ref[hh] = jnp.where(head == hh, rq_ref[...].astype(F32), 0.0).astype(BF)
        mask_ref[0] = jnp.where(lane > row, 1.0, 0.0).astype(BF)
        mask_ref[1] = jnp.where(lane > row, 0.0, 1.0).astype(BF)
        turn(ext_ref, n, block, n)
        turn(flip_ref, 0, 2 * n, ext)
        halo.wait(True)
        halo.start(False)
        keys(slice(0, n))
        turn(ext_ref, 0, n, 0)
        if block == n:
            get_after()

    if block > n:
        pl.when((qt == 1) & (pair == 0))(get_after)

    @pl.when(pair == 0)
    def _():
        at = lambda m: pl.ds(pl.multiple_of((qt + m) * n, n), n)
        qid = qid_ref[at(0), :]
        first, middle, third = [kid_ref[:, at(m)] for m in range(3)]
        side = ((lane > row) & (qid == first)) | ((lane < row) & (qid == third))
        bias_ref[:, 0:n] = jnp.where(side, 0.0, -1e30)
        bias_ref[:, n:] = jnp.where(qid == middle, 0.0, -1e30)

    ctx_ref[...] = fwd_tile(n, scale, pair, qt, q_ref, k_ref, v_ref, rk_ref, rqm_ref, bias_ref, mask_ref, p_ref)

    @pl.when(last)
    def _():
        halo.finish()
        for copy in keep(0, 6):
            copy.wait()


def attn_fwd(span, x, rel_table, w_query, w_key, w_value, b_query, b_key, b_value, qid, kid):
    block, width = x.shape
    ext, table = block + 2 * span, 2 * span
    scale = (3.0 * 64) ** -0.5
    heads = width // 64
    whole = lambda shape: pl.BlockSpec(shape, lambda t, h: (0,) * len(shape), pipeline_mode=pl.Buffered(1))
    far = pl.BlockSpec(memory_space=pltpu.HBM)
    small = [b_query, b_key, b_value, qid, kid]
    kept = [(rows, width) for rows in (block, ext, ext, table, table)] + [(width, ext + table)]
    more = [(ext, width), (table, width), (table, width)] + [(width, width)] * 3
    return pl.pallas_call(
        functools.partial(fwd_kernel, span, scale),
        grid=(block // span, width // 128),
        out_shape=[pltpu.HBM((block, width), BF), pltpu.HBM((heads, block, table), BF)]
        + [pltpu.HBM(shape, BF) for shape in kept],
        in_specs=[far] * 5 + [whole(arg.shape) for arg in small],
        out_specs=[pl.BlockSpec((span, 128), lambda t, h: (t, h)), pl.BlockSpec((2, span, table), lambda t, h: (h, t, 0))]
        + [far] * 6,
        scratch_shapes=[pltpu.VMEM(shape, BF) for shape in kept + more]
        + [
            pltpu.VMEM((2, table, width), BF),
            pltpu.VMEM((span, table), F32),
            pltpu.VMEM((2, span, span), BF),
            pltpu.SemaphoreType.DMA((2, 2)),
            pltpu.SemaphoreType.DMA((5,)),
            pltpu.SemaphoreType.DMA((6,)),
        ],
        compiler_params=pltpu.CompilerParams(collective_id=1, has_side_effects=True, vmem_limit_bytes=44 << 20),
        cost_estimate=pl.CostEstimate(flops=20_000_000_000, bytes_accessed=20 << 20, transcendentals=heads * block * table),
        name="attn_fwd",
    )(*[pltpu.with_memory_space_constraint(arg, pltpu.HBM) for arg in (x, rel_table, w_key, w_query, w_value, b_query, b_key, b_value)], qid, kid)


def bwd_tile(n, scale, qt, q_ref, k_ref, v_ref, g_ref, rk_ref, rq_ref, p_ref, mask_ref, kjt_ref, dk_acc, dvt_acc, drkt_acc, drqt_acc):
    at = lambda m: pl.ds(pl.multiple_of((qt + m) * n, n), n)
    row, lane = grid_of(n)
    flip = anti(n)
    ahead, behind, above, below = [mask_ref[m] for m in range(4)]
    qb, gb = q_ref[at(0), :], g_ref[at(0), :]
    qjt = dot(qb, flip, TN).astype(BF)
    gt = gb.astype(F32).T.astype(BF)
    dqs, dks = [], []
    for hh in range(2):
        lo, hi = 64 * hh, 64 * hh + 64
        gm = head_lanes(gb, hh)
        side, middle = p_ref[hh, at(0), 0:n], p_ref[hh, at(0), n:]
        ps, pm = side.astype(F32) * scale, middle.astype(F32) * scale
        gs = jnp.where(lane > row, dot(gm, v_ref[at(0), :], NT), dot(gm, v_ref[at(2), :], NT))
        gd = dot(gm, v_ref[at(1), :], NT)
        ts, td = ps * gs, pm * gd
        total = jnp.sum(ts + td, axis=-1, keepdims=True) * (1.0 / scale)
        ds, dm = (ts - ps * total).astype(BF), (td - pm * total).astype(BF)
        for m, part in enumerate((side * ahead, middle, side * behind)):
            dvt_acc[lo:hi, at(m)] += dot(gt[lo:hi], part)

        sj, mj = dot(flip, ds), dot(flip, dm)
        right = row + lane >= n
        to_low = sheared(jnp.where(right, sj, mj), 0).astype(BF)
        to_high = sheared(jnp.where(right, mj, sj), 0).astype(BF)
        sj, mj = sj.astype(BF), mj.astype(BF)
        dq = dot(sj * above, k_ref[at(0), :]) + dot(mj, k_ref[at(1), :]) + dot(sj * below, k_ref[at(2), :])
        dqs.append(dq + dot(to_low, rk_ref[0:n]) + dot(to_high, rk_ref[n:]))
        drkt_acc[lo:hi, 0:n] += dot(qjt[lo:hi], to_low)
        drkt_acc[lo:hi, n:] += dot(qjt[lo:hi], to_high)

        st, mt = dot(flip, ds, NT), dot(flip, dm, NT)
        us, um = sheared(st, 0).astype(BF), sheared(mt, 0).astype(BF)
        st, mt = st.astype(BF), mt.astype(BF)
        high_first, low_third = us * ahead, us * behind
        low_middle, high_middle = um * ahead, um * behind
        low, high = rq_ref[0:n], rq_ref[n:]
        dks.append((
            dot(st * below, qb) + dot(high_first, high),
            dot(mt, qb) + dot(low_middle, low) + dot(high_middle, high),
            dot(st * above, qb) + dot(low_third, low),
        ))
        kjt = [kjt_ref[qt + m, lo:hi, :] for m in range(3)]
        drqt_acc[lo:hi, 0:n] += dot(kjt[1], low_middle) + dot(kjt[2], low_third)
        drqt_acc[lo:hi, n:] += dot(kjt[0], high_first) + dot(kjt[1], high_middle)
    for m in range(3):
        dk_acc[qt + m] += both_heads(dks[0][m], dks[1][m])
    return dot(flip, both_heads(*dqs).astype(BF)).astype(BF)


def bwd_masks(n, mask_ref):
    row, lane = grid_of(n)
    for m, keep in enumerate((lane >= row, lane < row, row + lane >= n, row + lane < n)):
        mask_ref[m] = jnp.where(keep, 1.0, 0.0).astype(BF)


class Mesh:
    def __init__(self, ns, nb):
        self.ns, self.nb, self.nz = ns, nb, nb // 2
        self.bits = ns.bit_length() - 1
        self.ways = 2 if ns <= 4 else 1

    def locate(self):
        self.s = lax.axis_index("seq")
        self.b = lax.axis_index("batch")
        self.z, self.c = self.b // 2, self.b % 2

    def at(self, s, b):
        return {"seq": s, "batch": b}

    def greet(self):
        barrier = pltpu.get_barrier_semaphore()
        peers = [self.at(self.s, toggled(self.b, 1))]
        peers += [self.at(self.s, toggled(self.z, step) * 2 + self.c) for step in range(1, self.nz)]
        peers += [self.at(toggled(self.s, step), self.b) for step in range(1, self.ns)]
        for peer in peers:
            pl.semaphore_signal(barrier, inc=1, device_id=peer, device_id_type=MESH)
        self.greeted = len(peers)

    def meet(self):
        pl.semaphore_wait(pltpu.get_barrier_semaphore(), self.greeted)


class Chunk:
    def __init__(self, mesh, rows, lanes, moves, box=None, early_z=False):
        self.mesh, self.rows, self.moves, self.box, self.early_z = mesh, rows, moves, box, early_z
        unit = 128 * mesh.ways * mesh.ns
        self.lanes = -(-lanes // unit) * unit
        self.piece = self.lanes // (mesh.ways * mesh.ns)
        self.depth = 1 if early_z else mesh.nz

    def scratch(self):
        mesh, rows, lanes = self.mesh, self.rows, self.lanes
        full = pltpu.VMEM((mesh.nz, rows, lanes), BF)
        shapes = [full] if self.box else [full, full]
        for level in range(mesh.bits):
            shapes.append(pltpu.VMEM((mesh.ways, self.depth, rows, lanes // mesh.ways // 2 >> level), BF))
        wide = lanes // mesh.ways if self.early_z else self.piece
        shapes += [pltpu.VMEM((mesh.ways, mesh.nz - 1, rows, wide), BF), pltpu.VMEM((rows, lanes), BF)]
        dma = pltpu.SemaphoreType.DMA
        moves = len(self.moves)
        shapes += [] if self.box else [dma((moves,))]
        shapes += [dma((2, moves)), dma((2, 2, mesh.bits)), dma((2, 2, mesh.nz - 1)), dma((2, 2, mesh.bits))]
        return shapes

    def bind(self, refs):
        bits = self.mesh.bits
        if self.box:
            self.mine = self.box(self.mesh.c)
        else:
            self.mine, refs = refs[0], refs[1:]
        self.first = refs[0]
        self.halves = refs[1 : 1 + bits]
        self.across, self.final = refs[1 + bits : 3 + bits]
        refs = refs[3 + bits :]
        if not self.box:
            self.own_sem, refs = refs[0], refs[1:]
        self.core_sem, self.seq_sem, self.z_sem, self.out_sem = refs[:4]
        return refs[4:]

    def copy(self, src, dst, sems, index, s, b):
        return pltpu.make_async_remote_copy(
            src_ref=src,
            dst_ref=dst,
            send_sem=sems.at[(0,) + index],
            recv_sem=sems.at[(1,) + index],
            device_id=self.mesh.at(s, b),
            device_id_type=MESH,
        )

    def own_copies(self):
        for n, (source, at, size) in enumerate([] if self.box else self.moves):
            yield pltpu.make_async_copy(source(self.mesh.c), self.mine.at[:, :, pl.ds(at, size)], self.own_sem.at[n])

    def core_copies(self):
        mesh = self.mesh
        for n, (source, at, size) in enumerate(self.moves):
            yield self.copy(
                source(1 - mesh.c), self.first.at[:, :, pl.ds(at, size)], self.core_sem, (n,), mesh.s, toggled(mesh.b, 1)
            )

    def order(self, half, level):
        return (level + half) % self.mesh.bits

    def region(self, level, half):
        size = self.lanes // self.mesh.ways
        base = half * size
        sent = base
        for at in range(level):
            mine = (self.mesh.s // (1 << self.order(half, at))) % 2
            size = size // 2
            sent = base + (1 - mine) * size
            base = base + mine * size
        return base, sent, size

    def span(self, start, size):
        return pl.ds(pl.multiple_of(start, 128), size)

    def planes(self):
        return pl.ds(self.mesh.z, 1) if self.early_z else slice(None)

    def seq_copy(self, level, half):
        unused, sent, size = self.region(level + 1, half)
        return self.copy(
            self.mine.at[self.planes(), :, self.span(sent, size)],
            self.halves[level].at[half],
            self.seq_sem,
            (half, level),
            toggled(self.mesh.s, 1 << self.order(half, level)),
            self.mesh.b,
        )

    def z_region(self, half):
        kept, unused, size = self.region(0 if self.early_z else self.mesh.bits, half)
        return self.span(kept, size)

    def z_copies(self, half):
        mesh = self.mesh
        for step in range(1, mesh.nz):
            other = toggled(mesh.z, step)
            yield self.copy(
                self.mine.at[other, :, self.z_region(half)],
                self.across.at[half, step - 1],
                self.z_sem,
                (half, step - 1),
                mesh.s,
                other * 2 + mesh.c,
            )

    def out_copy(self, level, half):
        kept, unused, size = self.region(level + 1, half)
        lanes = self.span(kept, size)
        return self.copy(
            self.final.at[:, lanes],
            self.final.at[:, lanes],
            self.out_sem,
            (half, level),
            toggled(self.mesh.s, 1 << self.order(half, level)),
            self.mesh.b,
        )

    def start_core(self):
        for copy in self.core_copies():
            copy.start()
        for copy in self.own_copies():
            copy.start()

    def add_core(self):
        for copy in self.own_copies():
            copy.wait()
        for copy in self.core_copies():
            copy.wait_recv()
        parts = 4
        size = self.lanes // parts

        def add(n, carry):
            z, lanes = n // parts, self.span((n % parts) * size, size)
            self.mine[z, :, lanes] = (self.mine[z, :, lanes].astype(F32) + self.first[z, :, lanes].astype(F32)).astype(BF)
            return carry

        lax.fori_loop(0, self.mesh.nz * parts, add, 0)

    def start_seq(self, level):
        for half in range(self.mesh.ways):
            self.seq_copy(level, half).start()

    def add_seq(self, level):
        for half in range(self.mesh.ways):
            self.seq_copy(level, half).wait_recv()
            kept, unused, size = self.region(level + 1, half)
            lanes = self.span(kept, size)

            def add(n, carry):
                z = self.mesh.z if self.early_z else n
                got = self.halves[level][half, n].astype(F32)
                self.mine[z, :, lanes] = (self.mine[z, :, lanes].astype(F32) + got).astype(BF)
                return carry

            lax.fori_loop(0, self.depth, add, 0)
            if self.early_z and level == self.mesh.bits - 1:
                self.final[:, lanes] = self.mine[self.mesh.z, :, lanes]

    def end_seq(self):
        self.add_seq(1)
        for level in range(2, self.mesh.bits):
            self.start_seq(level)
            self.add_seq(level)

    def start_z(self):
        for half in range(self.mesh.ways):
            for copy in self.z_copies(half):
                copy.start()

    def add_z(self):
        z = self.mesh.z
        for half in range(self.mesh.ways):
            for copy in self.z_copies(half):
                copy.wait_recv()
            lanes = self.z_region(half)
            total = self.mine[z, :, lanes].astype(F32)
            for step in range(1, self.mesh.nz):
                total = total + self.across[half, step - 1].astype(F32)
            if self.early_z:
                self.mine[z, :, lanes] = total.astype(BF)
            else:
                self.final[:, lanes] = total.astype(BF)

    def start_out(self, level):
        for half in range(self.mesh.ways):
            self.out_copy(level, half).start()

    def core(self):
        self.start_core()

    def s0(self):
        if self.early_z:
            self.add_z()
        else:
            self.add_core()
        self.start_seq(0)

    def s1(self):
        self.add_seq(0)
        self.start_seq(1)

    def z(self):
        if self.early_z:
            self.add_core()
        else:
            self.end_seq()
        self.start_z()

    def out(self):
        if self.early_z:
            self.end_seq()
        else:
            self.add_z()
        self.start_out(self.mesh.bits - 1)

    def out2(self):
        for level in reversed(range(self.mesh.bits - 1)):
            for half in range(self.mesh.ways):
                self.out_copy(level + 1, half).wait_recv()
            self.start_out(level)

    def finish(self):
        for half in range(self.mesh.ways):
            self.out_copy(0, half).wait()
            for level in range(1, self.mesh.bits):
                self.out_copy(level, half).wait_send()
            for copy in self.z_copies(half):
                copy.wait_send()
            for level in range(self.mesh.bits):
                self.seq_copy(level, half).wait_send()
        for copy in self.core_copies():
            copy.wait_send()


class Layout:
    def __init__(self, ns, nb, width, hidden, table):
        self.mesh = mesh = Mesh(ns, nb)
        self.width, self.hidden = width, hidden
        self.rows = rows = width // nb
        self.fold = hidden // nb // rows
        self.rel_rows = table // nb
        self.pairs = width // 128
        self.third = width // 3
        self.rel_at = 384
        self.small_at = 384 + 512
        self.stack = rows // 16
        small_lanes = -(-self.pairs // self.stack) * 128
        self.split = split = hidden // 3
        whole = lambda name, lanes, early=False: self.boxed(lambda c: getattr(self, name).at[:, c], lanes, early)
        self.down = whole("down_ref", self.fold * width)
        self.into = whole("into_ref", hidden - split)
        self.rest = whole("rest_ref", split, False)
        lanes = Chunk(mesh, rows, 768 + self.third, []).lanes
        self.near = [self.boxed(lambda c, n=n: self.near_ref.at[n, :, c], lanes, n in (2,)) for n in range(3)]
        self.far = whole("far_ref", self.small_at + small_lanes)
        self.chunks = [self.down, self.into, self.rest, *self.near, self.far]

    def boxed(self, box, lanes, early=False):
        chunk = Chunk(self.mesh, self.rows, lanes, [], early_z=early)
        chunk.box, chunk.moves = box, [(box, 0, chunk.lanes)]
        return chunk

    def starts(self):
        at = 0
        for chunk in self.chunks:
            yield at
            at += chunk.lanes

    def scratch(self):
        mesh = self.mesh
        box = lambda lanes: pltpu.VMEM((mesh.nz, 2, self.rows, lanes), BF)
        shapes = [box(chunk.lanes) for chunk in (self.down, self.into, self.rest, self.far)]
        shapes.append(pltpu.VMEM((3, mesh.nz, 2, self.rows, self.near[0].lanes), BF))
        for chunk in self.chunks:
            shapes += chunk.scratch()
        return shapes

    def bind(self, refs):
        self.mesh.locate()
        self.down_ref, self.into_ref, self.rest_ref, self.far_ref, self.near_ref = refs[:5]
        refs = refs[5:]
        for chunk in self.chunks:
            refs = chunk.bind(refs)
        return refs

    def store_down(self, m, grads):
        rows, share = self.rows, self.rows * self.fold
        for n in range(self.width // rows):
            b, part = divmod(m * self.width + n * rows, share)
            lanes = slice(part // rows * self.width, (part // rows + 1) * self.width)
            self.down_ref[b // 2, b % 2, :, lanes] = grads[n * rows : (n + 1) * rows]

    def store_into(self, m, grads):
        rows, split = self.rows, self.split
        ref, lanes = (self.rest_ref, slice(0, split)) if m == 0 else (self.into_ref, slice((m - 1) * split, m * split))
        for b in range(self.mesh.nb):
            ref[b // 2, b % 2, :, lanes] = grads[b * rows : (b + 1) * rows]

    def store_out(self, grads):
        rows, third = self.rows, self.third
        for b in range(self.mesh.nb):
            for n in range(3):
                part = grads[b * rows : (b + 1) * rows, n * third : (n + 1) * third]
                self.near_ref[n, b // 2, b % 2, :, 768 : 768 + third] = part

    def store_pair(self, pair, grads):
        rows = self.rows
        box = pair // 2
        lanes = pl.ds(pl.multiple_of((pair % 2) * 384, 128), 384)

        @pl.when(pair < self.pairs - 1)
        def _():
            for b in range(self.mesh.nb):
                self.near_ref[box, b // 2, b % 2, :, lanes] = grads[b * rows : (b + 1) * rows]

        @pl.when(pair == self.pairs - 1)
        def _():
            for b in range(self.mesh.nb):
                self.far_ref[b // 2, b % 2, :, 0:384] = grads[b * rows : (b + 1) * rows]

    def store_rest(self, rel, vectors):
        take, at, half = self.rel_rows, self.rel_at, self.rel_rows // 2
        for b in range(self.mesh.nb):
            part = rel[b * take : (b + 1) * take]
            put = self.far_ref.at[b // 2, b % 2]
            put[0:take, at : at + 512] = part[:, 0:512]
            put[take : take + half, at : at + 256] = part[0:half, 512:768]
            put[take : take + half, at + 256 : at + 512] = part[half:, 512:768]
            for n in range(self.pairs):
                row, lane = (n % self.stack) * 16, self.small_at + (n // self.stack) * 128
                put[row : row + 16, lane : lane + 128] = vectors[:, n * 128 : (n + 1) * 128]

    def schedule(self):
        down, into, rest, one, two, three, far = self.chunks

        steps = {
            1: [rest.s0],
            2: [into.s0],
            4: [down.s0],
            8: [into.s1],
            9: [rest.s1],
            10: [down.s1, one.core],
            11: [into.z],
            12: [rest.z, one.s0, two.core],
            13: [two.s0, down.z],
            14: [one.s1],
            15: [three.core, into.out],
            16: [three.z, into.out2, two.s1],
            17: [rest.out],
        }
        last = [
            far.core,
            far.s0,
            three.s0,
            one.z,
            down.out,
            far.s1,
            two.z,
            one.out,
            three.s1,
            down.out2,
            far.z,
            rest.out2,
            three.out,
            two.out,
            one.out2,
            far.out,
            two.out2,
            three.out2,
            far.out2,
        ]
        last += [chunk.finish for chunk in self.chunks]
        return steps, last


class Edges:
    def __init__(self, mesh, refs):
        self.mesh = mesh
        self.sent, self.got, self.sems = refs

    def copy(self, side):
        other = self.mesh.s + (2 * side - 1)
        return pltpu.make_async_remote_copy(
            src_ref=self.sent.at[side],
            dst_ref=self.got.at[1 - side],
            send_sem=self.sems.at[0, side],
            recv_sem=self.sems.at[1, 1 - side],
            device_id=self.mesh.at(other, self.mesh.b),
            device_id_type=MESH,
        )

    def has(self, side):
        return self.mesh.s > 0 if side == 0 else self.mesh.s < self.mesh.ns - 1

    def start(self):
        for side in range(2):
            pl.when(self.has(side))(lambda side=side: self.copy(side).start())

    def finish(self, add):
        for side in range(2):

            @pl.when(self.has(side))
            def _(side=side):
                self.copy(side).wait_send()
                self.copy(1 - side).wait_recv()
                add(side, self.got[side])


def bwd_kernel(tq, scale, layout, q_ref, k_ref, v_ref, g_ref, rk_ref, rq_ref, p_ref, wk_ref, wq_ref, wv_ref,
               act_hbm, branch_ref, hidden_ref, pre_hbm, ctx_hbm, attn_hbm, g_one_hbm, xt_hbm, picks_ref, small_ref, *rest):
    (dx_ref, packed_hbm,
               mask_ref, kjt_ref, dk_acc, dvt_acc, drkt_acc, drqt_acc,
               xt_ref, d_ref, rel_acc, vec_ref, dx_acc, sent_ref, got_ref, edge_sem,
     load_ref, load_sem, side_sem, packed_sem, *refs) = rest
    block = q_ref.shape[0]
    nq = block // tq
    ext = k_ref.shape[0]
    nk = ext // tq
    span = tq
    table = 2 * span
    pair = pl.program_id(0)
    pairs = layout.pairs
    flip = anti(tq)
    layout.bind(refs)
    edges = Edges(layout.mesh, (sent_ref, got_ref, edge_sem))
    steps, last = layout.schedule()

    def run(actions):
        def all_of():
            for action in actions:
                action()
        return all_of

    loads = [act_hbm.at[:, pl.ds(m * layout.width, layout.width)] for m in range(layout.fold)]
    loads += [pre_hbm.at[:, pl.ds(m * layout.split, layout.split)] for m in range(3)]
    loads += [ctx_hbm, attn_hbm]

    def load(m):
        size = loads[m].shape
        return pltpu.make_async_copy(loads[m], load_ref.at[m % 3, pl.ds(0, size[0]), pl.ds(0, size[1])], load_sem.at[m % 3])

    def loaded(m):
        size = loads[m].shape
        load(m).wait()
        return load_ref[m % 3, 0 : size[0], 0 : size[1]]

    def dx_copy():
        return pltpu.make_async_copy(g_one_hbm, dx_ref, side_sem.at[0])

    def xt_copy():
        return pltpu.make_async_copy(xt_hbm, xt_ref, side_sem.at[1])

    @pl.when(pair == 0)
    def _():
        layout.mesh.greet()
        for m in range(2):
            load(m).start()
        m = 0
        for n in range(layout.fold):
            load(m + 2).start()
            layout.store_down(n, dot(loaded(m), branch_ref[...], TN).astype(BF))
            m += 1
        layout.mesh.meet()
        layout.down.core()
        for n in range(3):
            if m + 2 < len(loads):
                load(m + 2).start()
            layout.store_into(n, dot(hidden_ref[...], loaded(m), TN).astype(BF))
            if n == 0:
                layout.rest.core()
            m += 1
        xt_copy().start()
        dx_copy().start()
        layout.into.core()
        run(steps.get(0, []))()
        layout.store_out(dot(loaded(m), loaded(m + 1), TN).astype(BF))
        bwd_masks(tq, mask_ref)
        d_ref[...] = jnp.zeros_like(d_ref)
        rel_acc[...] = jnp.zeros_like(rel_acc)
        dx_acc[...] = jnp.zeros_like(dx_acc)
        vec_ref[...] = small_ref[...]

    for kt in range(nk):
        kjt_ref[kt] = dot(k_ref[kt * tq : (kt + 1) * tq, :], flip, TN).astype(BF)
    dk_acc[...] = jnp.zeros_like(dk_acc)
    dvt_acc[...] = jnp.zeros_like(dvt_acc)
    drkt_acc[...] = jnp.zeros_like(drkt_acc)
    drqt_acc[...] = jnp.zeros_like(drqt_acc)

    def tile(qt, carry):
        for step, actions in steps.items():
            if step and step % 3 < min(nq, 2):
                pl.when((pair == step // 3) & (qt == step % 3))(run(actions))
        row = pl.multiple_of(qt * tq, tq)
        dq = bwd_tile(
            tq, scale, qt, q_ref, k_ref, v_ref, g_ref, rk_ref, rq_ref, p_ref, mask_ref, kjt_ref, dk_acc, dvt_acc, drkt_acc, drqt_acc
        )
        d_ref[pl.ds(span + row, tq), 0:128] = dq
        return carry

    lax.fori_loop(0, nq, tile, 0)
    for step, actions in steps.items():
        if step % 3 >= min(nq, 2):
            pl.when(pair == step // 3)(run(actions))
    for kt in range(nk):
        here = slice(kt * tq, (kt + 1) * tq)
        dk = dot(flip, dk_acc[kt].astype(BF)).astype(BF)
        dv = dvt_acc[:, here].T.astype(BF)
        d_ref[here, 128:256] = dk
        d_ref[here, 256:384] = dv
    for st in range(table // 128):
        here = slice(ext + st * 128, ext + (st + 1) * 128)
        d_ref[here, 0:128] = drqt_acc[:, st * 128 : (st + 1) * 128].T.astype(BF)
        d_ref[here, 128:256] = drkt_acc[:, st * 128 : (st + 1) * 128].T.astype(BF)

    weights = jnp.concatenate([wq_ref[...], wk_ref[...], wv_ref[...]], axis=1)
    dx_acc[...] += dot(d_ref[0:ext], weights, NT)

    @pl.when(pair == pairs - 1)
    def _():
        sent_ref[0] = dx_acc[0:span].astype(BF)
        sent_ref[1] = dx_acc[ext - span :].astype(BF)
        edges.start()

    pl.when(pair == 0)(lambda: xt_copy().wait())
    grads = dot(xt_ref[...], d_ref[...]).astype(BF)
    layout.store_pair(pair, grads)
    rel_acc[...] += dot(d_ref[ext:, 0:128], wq_ref[...], NT) + dot(d_ref[ext:, 128:256], wk_ref[...], NT)
    sums = dot(jnp.ones((8, ext + table), BF), d_ref[...])[0:1]
    for n in range(3):
        vec_ref[10 + n : 11 + n, pl.ds(pl.multiple_of(pair * 128, 128), 128)] = sums[:, n * 128 : (n + 1) * 128]

    @pl.when(pair == pairs - 1)
    def _():
        rel = dot(picks_ref[...], rel_acc[...].astype(BF)).astype(BF)
        layout.store_rest(rel, vec_ref[...].astype(BF))
        run(last[:1])()
        dx_copy().wait()
        dx_ref[...] += dx_acc[span : span + block]
        run(last[1:])()

        packed_copies = []
        for n, (at, chunk) in enumerate(zip(layout.starts(), layout.chunks)):
            packed_copies.append(pltpu.make_async_copy(chunk.final, packed_hbm.at[:, pl.ds(at, chunk.lanes)], packed_sem.at[n]))
            packed_copies[-1].start()

        def take(side, rows):
            here = slice(0, span) if side == 0 else slice(block - span, block)
            dx_ref[here] += rows.astype(F32)

        edges.finish(take)
        for copy in packed_copies:
            copy.wait()


def attn_bwd(span, q, k, v, g, rk, rq, probs, w_key, w_query, w_value, act, branch, hidden, pre, context, g_attn, g_one, xt, picks, small):
    block, width = q.shape
    ext = k.shape[0]
    table = 2 * span
    scale = (3.0 * 64) ** -0.5
    ns, nb = lax.axis_size("seq"), lax.axis_size("batch")
    layout = Layout(ns, nb, width, act.shape[1], table)
    col = lambda rows: pl.BlockSpec((rows, 128), lambda h: (0, h))
    whole = lambda shape: pl.BlockSpec(shape, lambda h: (0, 0), pipeline_mode=pl.Buffered(1))
    any_spec = pl.BlockSpec(memory_space=pltpu.HBM)
    packed = jax.ShapeDtypeStruct((layout.rows, sum(chunk.lanes for chunk in layout.chunks)), BF)
    outs = pl.pallas_call(
        functools.partial(bwd_kernel, span, scale, layout),
        grid=(width // 128,),
        out_shape=(
            jax.ShapeDtypeStruct((block, width), F32),
            packed,
        ),
        in_specs=[col(block), col(ext), col(ext), col(block), col(rk.shape[0]), col(rq.shape[0]),
                  pl.BlockSpec((2, block, table), lambda h: (h, 0, 0)), col(width), col(width), col(width),
                  any_spec, whole(branch.shape), whole(hidden.shape), any_spec, any_spec, any_spec, any_spec, any_spec,
                  whole(picks.shape), whole(small.shape)],
        out_specs=(whole((block, width)), any_spec),
        scratch_shapes=[
            pltpu.VMEM((4, span, span), BF),
            pltpu.VMEM((ext // span, 128, span), BF),
            pltpu.VMEM((ext // span, span, 128), F32),
            pltpu.VMEM((128, ext), F32),
            pltpu.VMEM((128, table), F32),
            pltpu.VMEM((128, table), F32),
            pltpu.VMEM((width, ext + table), BF),
            pltpu.VMEM((ext + table, 384), BF),
            pltpu.VMEM((table, width), F32),
            pltpu.VMEM((16, width), F32),
            pltpu.VMEM((ext, width), F32),
            pltpu.VMEM((2, span, width), BF),
            pltpu.VMEM((2, span, width), BF),
            pltpu.SemaphoreType.DMA((2, 2)),
            pltpu.VMEM((3, block, layout.split), BF),
            pltpu.SemaphoreType.DMA((3,)),
            pltpu.SemaphoreType.DMA((2,)),
            pltpu.SemaphoreType.DMA((len(layout.chunks),)),
        ] + layout.scratch(),
        compiler_params=pltpu.CompilerParams(collective_id=0, has_side_effects=True, vmem_limit_bytes=60 << 20),
        cost_estimate=pl.CostEstimate(flops=50_000_000_000, bytes_accessed=20 << 20, transcendentals=0),
        name="attn_bwd_reduce",
    )(*[pltpu.with_memory_space_constraint(arg, pltpu.HBM) for arg in (q, k, v)], g, *[pltpu.with_memory_space_constraint(arg, pltpu.HBM) for arg in (rk, rq, probs)], w_key, w_query, w_value, act, branch, hidden, pre, context, g_attn, g_one, pltpu.with_memory_space_constraint(xt, pltpu.HBM), picks, small)
    return layout, outs


def unpack_kernel(layout, packed_hbm, dx_hbm,
                  dx_out, down_out, into_out, out_out, query_out, key_out, value_out, rel_out, *refs):
    vec_outs, wide_out, (packed_ref, rel_ref, vec_ref, sems) = refs[:-5], refs[-5], refs[-4:]
    packed_copy = pltpu.make_async_copy(packed_hbm, packed_ref, sems.at[0])
    dx_copy = pltpu.make_async_copy(dx_hbm, dx_out, sems.at[1])
    packed_copy.start()
    dx_copy.start()
    packed_copy.wait()
    rows, width, pairs = layout.rows, layout.width, layout.pairs
    parts = [packed_ref.at[:, at : at + chunk.lanes] for at, chunk in zip(layout.starts(), layout.chunks)]
    down_ref, into_ref, rest_ref, *near, far_ref = parts
    split = layout.hidden // 3
    into_out[:, :split] = rest_ref[:, :split].astype(F32)
    into_out[:, split:] = into_ref[:, : layout.hidden - split].astype(F32)
    for n in range(layout.fold):
        down_out[n * rows : (n + 1) * rows, :] = down_ref[:, n * width : (n + 1) * width].astype(F32)
    for n, side in enumerate(near):
        out_out[:, n * layout.third : (n + 1) * layout.third] = side[:, 768 : 768 + layout.third].astype(F32)
    for m in range(pairs):
        side, at = (far_ref, 0) if m == pairs - 1 else (near[m // 2], m % 2 * 384)
        for n, out in enumerate((query_out, key_out, value_out)):
            out[:, m * 128 : (m + 1) * 128] = side[:, at + n * 128 : at + (n + 1) * 128].astype(F32)
    take, at, half = layout.rel_rows, layout.rel_at, layout.rel_rows // 2
    rel_ref[:, 0:512] = far_ref[0:take, at : at + 512].astype(F32)
    for n in range(2):
        rel_ref[n * half : (n + 1) * half, 512:768] = far_ref[take : take + half, at + n * 256 : at + (n + 1) * 256].astype(F32)
    own = take // layout.mesh.ns
    rel_out[...] = pltpu.roll(rel_ref[...], take - lax.axis_index("seq") * own, 0)[:own]
    for n in range(pairs):
        row, lane = (n % layout.stack) * 16, layout.small_at + (n // layout.stack) * 128
        vec_ref[:, n * 128 : (n + 1) * 128] = far_ref[row : row + 16, lane : lane + 128].astype(F32)
    b = lax.axis_index("batch")
    mine = pltpu.roll(vec_ref[...], width - b * rows, 1)
    for out, n in zip(vec_outs, (0, 1, 2, 3, 4, 5, 10, 11, 12)):
        out[...] = mine[n, :rows]
    wide = wide_out.shape[0]
    fit = width // wide
    line = pltpu.roll(pltpu.roll(vec_ref[...], width - (b % fit) * wide, 1), 10 - b // fit, 0)
    wide_out[...] = line[0, :wide]
    dx_copy.wait()


def unpack(layout, packed, dx):
    rows, width = layout.rows, layout.width
    shape = lambda *dims: jax.ShapeDtypeStruct(dims, F32)
    shapes = [shape(*dx.shape), shape(layout.fold * rows, width), shape(rows, layout.hidden)] + [shape(rows, width)] * 4
    shapes += [shape(layout.rel_rows // layout.mesh.ns, width)] + [shape(rows)] * 9 + [shape(layout.fold * rows)]
    vmem, far = pl.BlockSpec(memory_space=pltpu.VMEM), pl.BlockSpec(memory_space=pltpu.HBM)
    return pl.pallas_call(
        functools.partial(unpack_kernel, layout),
        out_shape=shapes,
        in_specs=[far, far],
        out_specs=[vmem] * len(shapes),
        scratch_shapes=[
            pltpu.VMEM(packed.shape, BF),
            pltpu.VMEM((layout.rel_rows, width), F32),
            pltpu.VMEM((16, width), F32),
            pltpu.SemaphoreType.DMA((2,)),
        ],
        compiler_params=pltpu.CompilerParams(vmem_limit_bytes=32 << 20),
        name="unpack",
    )(*[pltpu.with_memory_space_constraint(arg, pltpu.HBM) for arg in (packed, dx)])


NORM_EPS = 1e-07
STEP = 1536


def mid_kernel(ctx_ref, x_ref, cot_ref, b_out, gain_attn, shift_attn, b_in, b_down, gain_ffn, shift_ffn, w_out_hbm, w_in_hbm, w_down_hbm,
               out_ref, branch_ref, hidden_ref, gone_ref, gattn_ref, gctx_ref, vec_ref, act_hbm, pre_hbm,
               w_out_ref, w_in_ref, w_down_ref, act_ref, pre_ref, slope_ref, full_ref, normed_ref, inv_ref, acc_ref, line_ref, in_sem, out_sem):
    block, width = x_ref.shape
    wide = w_in_ref.shape[1]
    parts = wide // width
    loads = [(w_out_hbm, w_out_ref)]
    for n in range(parts):
        loads.append((w_in_hbm.at[:, pl.ds(n * width, width)], w_in_ref.at[:, pl.ds(n * width, width)]))
    loads.append((w_down_hbm, w_down_ref))
    row_of = lambda ref: ref[...].astype(F32)[None]
    total = lambda values: jnp.sum(values, axis=0, keepdims=True)
    mean = lambda values: jnp.mean(values, axis=-1, keepdims=True)

    def load(n):
        return pltpu.make_async_copy(*loads[n], in_sem.at[n])

    def norm(values):
        centred = values - mean(values)
        inv = lax.rsqrt(mean(centred * centred) + NORM_EPS)
        return centred * inv, inv

    def norm_back(grads, normed, inv):
        return inv * (grads - mean(grads) - normed * mean(grads * normed))

    for n in range(len(loads)):
        load(n).start()
    blocks = [slice(n, n + 128) for n in range(0, block, 128)]
    load(0).wait()
    for rows in blocks:
        normed, inv = norm(x_ref[rows].astype(F32) + dot(ctx_ref[rows], w_out_ref[...]) + row_of(b_out))
        normed_ref[rows], inv_ref[rows] = normed, inv
        hidden = normed * row_of(gain_attn) + row_of(shift_attn)
        full_ref[rows] = hidden
        hidden_ref[rows] = hidden.astype(BF)
    for n in range(1, len(loads)):
        load(n).wait()
    acc_ref[...] = full_ref[...] + row_of(b_down)

    def up(n, carry):
        cols = pl.ds(pl.multiple_of(n * STEP, STEP), STEP)
        pre = dot(hidden_ref[...], w_in_ref[:, cols]) + b_in[cols].astype(F32)[None]
        phi = 0.5 + 0.5 * lax.erf(pre * (0.5**0.5))
        act = (pre * phi).astype(BF)
        act_ref[:, cols] = act
        slope_ref[:, cols] = phi + pre * (jnp.exp(-0.5 * pre * pre) * ((2.0 * math.pi) ** -0.5))
        acc_ref[...] += dot(act, w_down_ref[cols, :])
        return carry

    lax.fori_loop(0, wide // STEP, up, 0, unroll=1)
    act_copy = pltpu.make_async_copy(act_ref, act_hbm, out_sem.at[0])
    act_copy.start()
    gain, shift, bias = 0.0, 0.0, 0.0
    for rows in blocks:
        normed, inv = norm(acc_ref[rows])
        out_ref[rows] = (normed * row_of(gain_ffn) + row_of(shift_ffn)).astype(BF)
        grads = cot_ref[rows].astype(F32)
        gain, shift = gain + total(grads * normed), shift + total(grads)
        grad_two = norm_back(grads * row_of(gain_ffn), normed, inv)
        acc_ref[rows] = grad_two
        branch = grad_two.astype(BF)
        branch_ref[rows] = branch
        bias = bias + total(branch.astype(F32))
    vec_ref[...] = jnp.zeros_like(vec_ref)
    vec_ref[3:4], vec_ref[4:5], vec_ref[5:6] = bias, gain, shift

    def down(n, carry):
        cols = pl.ds(pl.multiple_of(n * STEP, STEP), STEP)
        pre = (dot(branch_ref[...], w_down_ref[cols, :], NT) * slope_ref[:, cols]).astype(BF)
        pre_ref[:, cols] = pre
        line_ref[0:1, cols] = total(pre.astype(F32))
        acc_ref[...] += dot(pre, w_in_ref[:, cols], NT)
        return carry

    lax.fori_loop(0, wide // STEP, down, 0, unroll=1)
    pre_copy = pltpu.make_async_copy(pre_ref, pre_hbm, out_sem.at[1])
    pre_copy.start()
    for n in range(parts):
        vec_ref[6 + n : 7 + n] = line_ref[0:1, n * width : (n + 1) * width]
    gain, shift, bias = 0.0, 0.0, 0.0
    for rows in blocks:
        grads, normed = acc_ref[rows], normed_ref[rows]
        gain, shift = gain + total(grads * normed), shift + total(grads)
        grad_one = norm_back(grads * row_of(gain_attn), normed, inv_ref[rows])
        gone_ref[rows] = grad_one
        grad_attn = grad_one.astype(BF)
        gattn_ref[rows] = grad_attn
        bias = bias + total(grad_attn.astype(F32))
        gctx_ref[rows] = dot(grad_attn, w_out_ref[...], NT).astype(BF)
    vec_ref[0:1], vec_ref[1:2], vec_ref[2:3] = bias, gain, shift
    act_copy.wait()
    pre_copy.wait()


def middle(context, x, cotangent, small, w_out, w_in, w_down):
    block, width = x.shape
    wide = w_in.shape[1]
    far = pl.BlockSpec(memory_space=pltpu.HBM)
    whole = lambda arg: pl.BlockSpec(arg.shape, lambda t: (0,) * len(arg.shape), pipeline_mode=pl.Buffered(1))
    tall = (block, width)
    args = [context, x, cotangent, *small]
    outs = [jax.ShapeDtypeStruct(tall, BF)]
    outs += [pltpu.HBM(dims, kind) for dims, kind in ((tall, BF), (tall, BF), (tall, F32), (tall, BF), (tall, BF), ((16, width), F32))]
    return pl.pallas_call(
        mid_kernel,
        grid=(1,),
        out_shape=outs + [pltpu.HBM((block, wide), BF)] * 2,
        in_specs=[whole(arg) for arg in args] + [far] * 3,
        out_specs=[whole(out) for out in outs] + [far] * 2,
        scratch_shapes=[
            pltpu.VMEM((width, width), BF),
            pltpu.VMEM((width, wide), BF),
            pltpu.VMEM((wide, width), BF),
            pltpu.VMEM((block, wide), BF),
            pltpu.VMEM((block, wide), BF),
            pltpu.VMEM((block, wide), F32),
            pltpu.VMEM(tall, F32),
            pltpu.VMEM(tall, F32),
            pltpu.VMEM((block, 1), F32),
            pltpu.VMEM(tall, F32),
            pltpu.VMEM((8, wide), F32),
            pltpu.SemaphoreType.DMA((2 + wide // width,)),
            pltpu.SemaphoreType.DMA((2,)),
        ],
        compiler_params=pltpu.CompilerParams(vmem_limit_bytes=56 << 20),
        name="middle",
    )(*args, *[pltpu.with_memory_space_constraint(arg, pltpu.HBM) for arg in (w_out, w_in, w_down)])


def local(
    layer_input,
    w_query,
    b_query,
    w_key,
    b_key,
    w_value,
    b_value,
    w_out,
    b_out,
    gain_attn,
    shift_attn,
    w_in,
    b_in,
    w_down,
    b_down,
    gain_ffn,
    shift_ffn,
    rel_table,
    segment_ids,
    cotangent,
):
    rows, block, width = layer_input.shape
    span = rel_table.shape[0] // 2
    x = layer_input[0]
    start = lax.axis_index("seq") * block
    padded = jnp.pad(segment_ids[0], (span, span), constant_values=-1)
    kid = lax.dynamic_slice_in_dim(padded, start, block + 2 * span, 0)
    qid = kid[span : span + block]
    context, probs, q, k, v, rk, rq, xt = attn_fwd(
        span, x, rel_table, w_query, w_key, w_value, b_query, b_key, b_value, qid[:, None], kid[None]
    )

    output, grad_branch, hidden_low, grad_one, grad_attn, grad_context, small, act_low, grad_pre = middle(
        context, x, cotangent[0], [b_out, gain_attn, shift_attn, b_in, b_down, gain_ffn, shift_ffn], w_out, w_in, w_down
    )
    share, lanes = lax.axis_size("batch"), lax.axis_size("seq")
    rel_rows = 2 * span // (share * lanes)
    order = np.arange(2 * span).reshape(lanes, share, rel_rows).transpose(1, 0, 2).reshape(-1)
    picks = jnp.asarray((2 * span - 1 - order)[:, None] == np.arange(2 * span)[None], BF)
    layout, outs = attn_bwd(
        span, q, k, v, grad_context, rk, rq, probs, w_key, w_query, w_value, act_low, grad_branch, hidden_low, grad_pre,
        context, grad_attn, grad_one, xt, picks, small,
    )
    input_grad, packed = outs
    input_grad, down_sum, in_sum, out_sum, query_sum, key_sum, value_sum, rel_sum, *vectors = unpack(layout, packed, input_grad)
    ob, ga, sa, db, gf, sf, qb, kb, vb, ib = vectors
    return (
        output[None], input_grad[None], query_sum, qb, key_sum, kb, value_sum, vb, out_sum, ob,
        ga, sa, in_sum, ib, down_sum, db, gf, sf, rel_sum,
    )


def solution(mesh):
    tokens = P("batch", "seq", None)
    in_specs = (tokens,) + (P(),) * 17 + (P("batch", None), tokens)
    matrix, vector = P("batch", None), P("batch")
    out_specs = (
        (tokens, tokens)
        + (matrix, vector) * 4
        + (vector, vector)
        + (matrix, vector) * 2
        + (vector, vector, P(("seq", "batch"), None))
    )
    return jax.shard_map(local, mesh=mesh, in_specs=in_specs, out_specs=out_specs, check_vma=False)
```
